256 devices in a mesh: section: 8 (over z_lo, core), dp: 32 (over y, x, z_hi).
Axes of the slice: x: 4, y: 4, z: 8 (z_hi: 2, z_lo: 4; z = z_hi * 4 + z_lo), core: 2. Of those that a mesh axis runs over, the one named last changes fastest.
Arguments:
- clips: bfloat16 [8, 32, 4, 8, 8, 128], P(None, 'dp'), may hold values from -6 to 6
- cotangent: bfloat16 [8, 32, 4, 8, 8, 128], P(None, 'dp'), may hold values from -6 to 6
- weights: bfloat16 [8, 3456, 128], P('section', 'dp'), may hold values from -0.078125 to 0.078125
Outputs:
- section_outs: bfloat16 [8, 8, 32, 4, 8, 8, 128], P('section', None, 'dp')
- weight_grads: float32 [8, 3456, 128], P('section', 'dp')
The draws below stay inside these ranges and needn't reach their ends.
All inputs are finite; a program needn't handle non-finite values.
Results may differ from the reference program's by a relative error of at most 0.027.
Values may be sent and summed in bfloat16 or wider, within the bound.
A program may use at most 64 MiB of HBM per device.

```python
import jax
import jax.numpy as jnp
from jax import lax

C = 128
TF = 4
HT = 8
WT = 8
MB = 8
CLIPS = 32
KROWS = 3456
N_SECTION = 8


def levels(key, shape, shards, low, top_value):
    def one(position, shards_of):
        draws = jax.random.uniform(jax.random.fold_in(jax.random.fold_in(key, 6), position), (shards_of,), jnp.float32, low / len(shards), top_value / len(shards))
        return jnp.repeat(jnp.exp(draws), shape[position] // shards_of).reshape((-1,) + (1,) * (len(shape) - position - 1))

    factor_of = one(*shards[0])
    for cut in shards[1:]:
        factor_of = factor_of * one(*cut)
    return factor_of


def noise(rng, extent, scale, reach, cuts=(), held_as=jnp.bfloat16):
    level = levels(rng, extent, cuts, -0.22, 0.18) if cuts else 1.0
    entries = jax.random.normal(rng, extent, jnp.float32) * scale * level
    return jnp.minimum(jnp.maximum(entries, -reach), reach).astype(held_as)


def setup_inputs(seed: int = 0) -> dict:
    arg_keys = jax.random.split(jax.random.key(seed), 4)
    clips = noise(arg_keys[0], (MB, CLIPS, TF, HT, WT, C), 1.0, 6.0, ((1, 32),))
    cotangent = noise(arg_keys[1], (MB, CLIPS, TF, HT, WT, C), 1.0, 6.0, ((1, 32),))
    weights = noise(arg_keys[2], (N_SECTION, KROWS, C), (2 * KROWS) ** -0.5, 0.078125, ((0, 8), (1, 32)))
    return {"clips": clips, "cotangent": cotangent, "weights": weights}


def gather_patches(field):
    frames, height, width, channels = field.shape
    first_frame = field[:1]
    padded = jnp.concatenate([first_frame, first_frame, field], axis=0)
    padded = jnp.pad(padded, ((0, 0), (1, 1), (1, 1), (0, 0)))
    pieces = [padded[offset_time:offset_time + frames, offset_row:offset_row + height, offset_col:offset_col + width] for offset_time in range(3) for offset_row in range(3) for offset_col in range(3)]
    return jnp.stack(pieces, axis=3).reshape(frames * height * width, 27 * channels)

def squash_columns(activation):
    squashed = jax.nn.silu(activation.astype(jnp.float32)).astype(jnp.bfloat16)
    return gather_patches(squashed)

def layer_forward(activation, weight):
    branch = jnp.dot(squash_columns(activation), weight, preferred_element_type=jnp.float32)
    return (activation.astype(jnp.float32) + branch.reshape(activation.shape)).astype(jnp.bfloat16)

def input_gradient(activation, upstream, weight):
    flat_grad = upstream.reshape(-1, weight.shape[1])
    column_grad = lax.dot_general(flat_grad, weight, (((1,), (1,)), ((), ())), preferred_element_type=jnp.float32)
    base = activation.astype(jnp.float32)
    _, unfold = jax.vjp(gather_patches, base)
    field_grad = unfold(column_grad)[0]
    sigmoid_value = jax.nn.sigmoid(base)
    slope = sigmoid_value * (1.0 + base * (1.0 - sigmoid_value))
    return (upstream.astype(jnp.float32) + field_grad * slope).astype(jnp.bfloat16)

def weight_term(activation, upstream):
    flat_grad = upstream.reshape(-1, upstream.shape[-1])
    return lax.dot_general(squash_columns(activation), flat_grad, (((0,), (0,)), ((), ())), preferred_element_type=jnp.float32)

def reference(clips, cotangent, weights):
    section_count = weights.shape[0]
    lead_shape = clips.shape[:2]
    acts = clips.reshape((-1,) + clips.shape[2:])
    inputs_kept = []
    outputs_kept = []
    for section in range(section_count):
        inputs_kept.append(acts)
        layer_weight = weights[section]

        def run_one(activation, layer_weight=layer_weight):
            return layer_forward(activation, layer_weight)
        acts = lax.map(run_one, acts)
        outputs_kept.append(acts)
    grad = cotangent.reshape(acts.shape)
    grads_kept = [None] * section_count
    for section in reversed(range(section_count)):
        layer_weight = weights[section]

        def accumulate(running, pair, layer_weight=layer_weight):
            activation, upstream = pair
            return (running + weight_term(activation, upstream), input_gradient(activation, upstream, layer_weight))
        start_total = jnp.zeros(layer_weight.shape, jnp.float32)
        running, grad = lax.scan(accumulate, start_total, (inputs_kept[section], grad))
        grads_kept[section] = running
    section_outs = jnp.stack(outputs_kept).reshape((section_count,) + lead_shape + clips.shape[2:])
    return (section_outs, jnp.stack(grads_kept))
```

```python
import jax
import jax.numpy as jnp
from jax import lax
from jax.sharding import PartitionSpec as P

from jax.experimental import pallas as pl
from jax.experimental.pallas import tpu as pltpu

MESH_ID = pl.DeviceIdType.MESH


def greet_peers(peers, here, row):
    barrier = pltpu.get_barrier_semaphore()

    def signal(i, carry):
        peer = lax.rem(here + i, peers)
        pl.semaphore_signal(barrier, inc=1, device_id=(row, peer), device_id_type=MESH_ID)
        return carry

    lax.fori_loop(1, peers, signal, 0)
    pl.semaphore_wait(barrier, peers - 1)


def gather_kernel(shard_ref, out_ref, send_sem, recv_sem):
    peers = lax.axis_size("dp")
    here = lax.axis_index("dp")
    row = lax.axis_index("section")
    greet_peers(peers, here, row)

    def outgoing(peer):
        return pltpu.make_async_remote_copy(
            src_ref=shard_ref,
            dst_ref=out_ref.at[here],
            send_sem=send_sem.at[peer],
            recv_sem=recv_sem.at[here],
            device_id=(row, peer),
            device_id_type=MESH_ID,
        )

    def incoming(peer):
        return pltpu.make_async_remote_copy(
            src_ref=shard_ref,
            dst_ref=out_ref.at[peer],
            send_sem=send_sem.at[peer],
            recv_sem=recv_sem.at[peer],
            device_id=(row, peer),
            device_id_type=MESH_ID,
        )

    def start(i, carry):
        outgoing(lax.rem(here + i, peers)).start()
        return carry

    lax.fori_loop(1, peers, start, 0)
    out_ref[here] = shard_ref[...]

    def finish(i, carry):
        peer = lax.rem(here + i, peers)
        outgoing(peer).wait_send()
        incoming(peer).wait_recv()
        return carry

    lax.fori_loop(1, peers, finish, 0)


def gather_rows(shard):
    peers = lax.axis_size("dp")
    rows, cols = shard.shape
    return pl.pallas_call(
        gather_kernel,
        out_shape=jax.ShapeDtypeStruct((peers, rows, cols), shard.dtype),
        in_specs=[pl.BlockSpec(memory_space=pltpu.VMEM)],
        out_specs=pl.BlockSpec(memory_space=pltpu.VMEM),
        scratch_shapes=[pltpu.SemaphoreType.DMA((peers,)), pltpu.SemaphoreType.DMA((peers,))],
        compiler_params=pltpu.CompilerParams(collective_id=0, has_side_effects=True),
    )(shard)


def scatter_kernel(parts_ref, out_ref, held, send_sem, recv_sem):
    peers = lax.axis_size("dp")
    here = lax.axis_index("dp")
    row = lax.axis_index("section")
    greet_peers(peers, here, row)

    def outgoing(peer):
        return pltpu.make_async_remote_copy(
            src_ref=parts_ref.at[peer],
            dst_ref=held.at[here],
            send_sem=send_sem.at[peer],
            recv_sem=recv_sem.at[here],
            device_id=(row, peer),
            device_id_type=MESH_ID,
        )

    def incoming(peer):
        return pltpu.make_async_remote_copy(
            src_ref=parts_ref.at[peer],
            dst_ref=held.at[peer],
            send_sem=send_sem.at[peer],
            recv_sem=recv_sem.at[peer],
            device_id=(row, peer),
            device_id_type=MESH_ID,
        )

    def start(i, carry):
        outgoing(lax.rem(here + i, peers)).start()
        return carry

    lax.fori_loop(1, peers, start, 0)

    def finish(i, total):
        peer = lax.rem(here + i, peers)
        outgoing(peer).wait_send()
        incoming(peer).wait_recv()
        return total + held[peer]

    out_ref[...] = lax.fori_loop(1, peers, finish, parts_ref[here])


def scatter_rows(parts):
    peers, rows, cols = parts.shape
    return pl.pallas_call(
        scatter_kernel,
        out_shape=jax.ShapeDtypeStruct((rows, cols), parts.dtype),
        in_specs=[pl.BlockSpec(memory_space=pltpu.VMEM)],
        out_specs=pl.BlockSpec(memory_space=pltpu.VMEM),
        scratch_shapes=[
            pltpu.VMEM((peers, rows, cols), parts.dtype),
            pltpu.SemaphoreType.DMA((peers,)),
            pltpu.SemaphoreType.DMA((peers,)),
        ],
        compiler_params=pltpu.CompilerParams(collective_id=1, has_side_effects=True),
    )(parts)


def passed_along(block, axis, distance):
    devices = range(lax.axis_size(axis))
    route = [(i - distance, i) for i in devices if i - distance in devices]
    return lax.ppermute(block, axis, route)


def gather_patches(field):
    frames, height, width, channels = field.shape
    first_frame = field[:1]
    padded = jnp.concatenate([first_frame, first_frame, field], axis=0)
    padded = jnp.pad(padded, ((0, 0), (1, 1), (1, 1), (0, 0)))
    pieces = [
        padded[
            offset_time : offset_time + frames,
            offset_row : offset_row + height,
            offset_col : offset_col + width,
        ]
        for offset_time in range(3)
        for offset_row in range(3)
        for offset_col in range(3)
    ]
    return jnp.stack(pieces, axis=3).reshape(frames * height * width, 27 * channels)


def squash_field(activation):
    return jax.nn.silu(activation.astype(jnp.float32)).astype(jnp.bfloat16)


def squash_columns(activation):
    return gather_patches(squash_field(activation))


def layer_forward(activation, weight):
    branch = jnp.dot(squash_columns(activation), weight, preferred_element_type=jnp.float32)
    return (activation.astype(jnp.float32) + branch.reshape(activation.shape)).astype(jnp.bfloat16)


def input_gradient(activation, upstream, weight):
    flat_grad = upstream.reshape(-1, weight.shape[1])
    column_grad = lax.dot_general(
        flat_grad, weight, (((1,), (1,)), ((), ())), preferred_element_type=jnp.float32
    )
    base = activation.astype(jnp.float32)
    _, unfold = jax.vjp(gather_patches, base)
    field_grad = unfold(column_grad)[0]
    sigmoid_value = jax.nn.sigmoid(base)
    slope = sigmoid_value * (1.0 + base * (1.0 - sigmoid_value))
    return (upstream.astype(jnp.float32) + field_grad * slope).astype(jnp.bfloat16)


def weight_term(activation, upstream):
    flat_grad = upstream.reshape(-1, upstream.shape[-1])
    return lax.dot_general(
        squash_columns(activation),
        flat_grad,
        (((0,), (0,)), ((), ())),
        preferred_element_type=jnp.float32,
    )


def per_device(clips, cotangent, weights):
    section_total = lax.axis_size("section")
    section_index = lax.axis_index("section")
    weight = gather_rows(weights[0]).reshape(-1, weights.shape[-1])
    local_clips = clips[:, 0]
    local_grads = cotangent[:, 0]
    micro_count = local_clips.shape[0]
    step_count = micro_count + section_total - 1
    empty_field = jnp.zeros(local_clips.shape[1:], jnp.bfloat16)

    def forward_step(step_index, carry):
        received, saved_inputs, produced = carry
        micro_index = step_index - section_index
        active = (micro_index >= 0) & (micro_index < micro_count)
        slot_index = jnp.clip(micro_index, 0, micro_count - 1)
        fresh = lax.dynamic_index_in_dim(local_clips, slot_index, 0, keepdims=False)
        layer_input = jnp.where(section_index == 0, fresh, received)
        layer_output = layer_forward(layer_input, weight)
        kept_input = jnp.where(
            active,
            layer_input,
            lax.dynamic_index_in_dim(saved_inputs, slot_index, 0, keepdims=False),
        )
        kept_output = jnp.where(
            active, layer_output, lax.dynamic_index_in_dim(produced, slot_index, 0, keepdims=False)
        )
        saved_inputs = lax.dynamic_update_index_in_dim(saved_inputs, kept_input, slot_index, 0)
        produced = lax.dynamic_update_index_in_dim(produced, kept_output, slot_index, 0)
        received = passed_along(layer_output, "section", 1)
        return (received, saved_inputs, produced)

    start_forward = (empty_field, jnp.zeros_like(local_clips), jnp.zeros_like(local_clips))
    _, saved_inputs, produced = lax.fori_loop(0, step_count, forward_step, start_forward)

    def backward_step(step_index, carry):
        received, grad_total, kept_grads = carry
        micro_index = step_index - (section_total - 1 - section_index)
        active = (micro_index >= 0) & (micro_index < micro_count)
        slot_index = jnp.clip(micro_index, 0, micro_count - 1)
        fresh = lax.dynamic_index_in_dim(local_grads, slot_index, 0, keepdims=False)
        upstream = jnp.where(section_index == section_total - 1, fresh, received)
        activation = lax.dynamic_index_in_dim(saved_inputs, slot_index, 0, keepdims=False)
        grad_total = grad_total + jnp.where(active, weight_term(activation, upstream), 0.0)
        layer_grad = input_gradient(activation, upstream, weight)
        received = passed_along(layer_grad, "section", -1)
        return (received, grad_total, kept_grads)

    start_backward = (
        empty_field,
        jnp.zeros(weight.shape, jnp.float32),
        jnp.zeros_like(local_grads),
    )
    _, grad_total, kept_grads = lax.fori_loop(0, step_count, backward_step, start_backward)
    grad_share = scatter_rows(grad_total.reshape(lax.axis_size("dp"), -1, grad_total.shape[-1]))
    return (produced[None, :, None], grad_share[None])


def solution(mesh):
    placed = (
        P(None, "dp", None, None, None, None),
        P(None, "dp", None, None, None, None),
        P("section", "dp", None),
    )
    return jax.shard_map(
        per_device,
        mesh=mesh,
        in_specs=placed,
        out_specs=(P("section", None, "dp", None, None, None, None), P("section", "dp", None)),
        check_vma=False,
    )
```

```python
import jax
import jax.numpy as jnp
from jax import lax
from jax.sharding import PartitionSpec as P

from jax.experimental import pallas as pl
from jax.experimental.pallas import tpu as pltpu

MESH_ID = pl.DeviceIdType.MESH


def greet_peers(peers, here, row):
    barrier = pltpu.get_barrier_semaphore()

    def signal(i, carry):
        peer = lax.rem(here + i, peers)
        pl.semaphore_signal(barrier, inc=1, device_id=(row, peer), device_id_type=MESH_ID)
        return carry

    lax.fori_loop(1, peers, signal, 0)
    pl.semaphore_wait(barrier, peers - 1)


def gather_kernel(shard_ref, out_ref, send_sem, recv_sem):
    peers = lax.axis_size("dp")
    here = lax.axis_index("dp")
    row = lax.axis_index("section")
    greet_peers(peers, here, row)

    def outgoing(peer):
        return pltpu.make_async_remote_copy(
            src_ref=shard_ref,
            dst_ref=out_ref.at[here],
            send_sem=send_sem.at[peer],
            recv_sem=recv_sem.at[here],
            device_id=(row, peer),
            device_id_type=MESH_ID,
        )

    def incoming(peer):
        return pltpu.make_async_remote_copy(
            src_ref=shard_ref,
            dst_ref=out_ref.at[peer],
            send_sem=send_sem.at[peer],
            recv_sem=recv_sem.at[peer],
            device_id=(row, peer),
            device_id_type=MESH_ID,
        )

    def start(i, carry):
        outgoing(lax.rem(here + i, peers)).start()
        return carry

    lax.fori_loop(1, peers, start, 0)
    out_ref[here] = shard_ref[...]

    def finish(i, carry):
        peer = lax.rem(here + i, peers)
        outgoing(peer).wait_send()
        incoming(peer).wait_recv()
        return carry

    lax.fori_loop(1, peers, finish, 0)


def gather_rows(shard):
    peers = lax.axis_size("dp")
    rows, cols = shard.shape
    return pl.pallas_call(
        gather_kernel,
        out_shape=jax.ShapeDtypeStruct((peers, rows, cols), shard.dtype),
        in_specs=[pl.BlockSpec(memory_space=pltpu.VMEM)],
        out_specs=pl.BlockSpec(memory_space=pltpu.VMEM),
        scratch_shapes=[pltpu.SemaphoreType.DMA((peers,)), pltpu.SemaphoreType.DMA((peers,))],
        compiler_params=pltpu.CompilerParams(collective_id=0, has_side_effects=True),
    )(shard)


def scatter_kernel(parts_ref, out_ref, held, send_sem, recv_sem):
    peers = lax.axis_size("dp")
    here = lax.axis_index("dp")
    row = lax.axis_index("section")
    greet_peers(peers, here, row)

    def outgoing(peer):
        return pltpu.make_async_remote_copy(
            src_ref=parts_ref.at[peer],
            dst_ref=held.at[here],
            send_sem=send_sem.at[peer],
            recv_sem=recv_sem.at[here],
            device_id=(row, peer),
            device_id_type=MESH_ID,
        )

    def incoming(peer):
        return pltpu.make_async_remote_copy(
            src_ref=parts_ref.at[peer],
            dst_ref=held.at[peer],
            send_sem=send_sem.at[peer],
            recv_sem=recv_sem.at[peer],
            device_id=(row, peer),
            device_id_type=MESH_ID,
        )

    def start(i, carry):
        outgoing(lax.rem(here + i, peers)).start()
        return carry

    lax.fori_loop(1, peers, start, 0)

    def finish(i, total):
        peer = lax.rem(here + i, peers)
        outgoing(peer).wait_send()
        incoming(peer).wait_recv()
        return total + held[peer]

    out_ref[...] = lax.fori_loop(1, peers, finish, parts_ref[here])


def scatter_rows(parts):
    peers, rows, cols = parts.shape
    return pl.pallas_call(
        scatter_kernel,
        out_shape=jax.ShapeDtypeStruct((rows, cols), parts.dtype),
        in_specs=[pl.BlockSpec(memory_space=pltpu.VMEM)],
        out_specs=pl.BlockSpec(memory_space=pltpu.VMEM),
        scratch_shapes=[
            pltpu.VMEM((peers, rows, cols), parts.dtype),
            pltpu.SemaphoreType.DMA((peers,)),
            pltpu.SemaphoreType.DMA((peers,)),
        ],
        compiler_params=pltpu.CompilerParams(collective_id=1, has_side_effects=True),
    )(parts)


def squash_into(pad_ref, activation):
    squashed = (activation / (1.0 + jnp.exp(-activation))).astype(jnp.bfloat16).astype(jnp.float32)
    field = squashed.reshape(pad_ref.shape[0] - 2, 8, 8, pad_ref.shape[-1])
    pad_ref[2:, 1:9, 1:9, :] = field
    pad_ref[0:2, 1:9, 1:9, :] = jnp.broadcast_to(field[0:1], (2,) + field.shape[1:])


def tap_window(pad_ref, tap, frames, base):
    offset_time, offset_row, offset_col = tap // 9, (tap // 3) % 3, tap % 3
    if base:
        t0, r0, c0 = 2 - offset_time, 2 - offset_row, 2 - offset_col
    else:
        t0, r0, c0 = offset_time, offset_row, offset_col
    window = pad_ref[t0 : t0 + frames, r0 : r0 + 8, c0 : c0 + 8, :]
    return window.reshape(frames * 64, window.shape[-1]).astype(jnp.bfloat16)


def greet_line(here, count, col):
    barrier = pltpu.get_barrier_semaphore()

    @pl.when(here > 0)
    def _():
        pl.semaphore_signal(barrier, inc=1, device_id=(here - 1, col), device_id_type=MESH_ID)

    @pl.when(here < count - 1)
    def _():
        pl.semaphore_signal(barrier, inc=1, device_id=(here + 1, col), device_id_type=MESH_ID)

    neighbours = (here + count - 1) // count + (2 * count - 2 - here) // count
    pl.semaphore_wait(barrier, neighbours)


def line_copy(src, dst, send_sem, recv_sem, target, col):
    return pltpu.make_async_remote_copy(
        src_ref=src,
        dst_ref=dst,
        send_sem=send_sem,
        recv_sem=recv_sem,
        device_id=(target, col),
        device_id_type=MESH_ID,
    )


def forward_kernel(clips_ref, w_ref, seen_ref, out_ref, recv, pad, send_sem, recv_sem):
    count = lax.axis_size("section")
    here = lax.axis_index("section")
    col = lax.axis_index("dp")
    micro_count = clips_ref.shape[0]
    greet_line(here, count, col)
    pad[...] = jnp.zeros_like(pad)

    def step(m, carry):
        @pl.when(here == 0)
        def _():
            seen_ref[m] = clips_ref[m]

        @pl.when(here > 0)
        def _():
            line_copy(out_ref.at[m], recv.at[m], send_sem.at[m], recv_sem.at[m], here - 1, col).wait_recv()
            seen_ref[m] = recv[m]

        base = seen_ref[m].astype(jnp.float32)
        squash_into(pad, base)
        total = base
        for tap in range(27):
            total = total + jnp.dot(tap_window(pad, tap, 4, False), w_ref[tap], preferred_element_type=jnp.float32)
        out_ref[m] = total.astype(out_ref.dtype)

        @pl.when(here < count - 1)
        def _():
            line_copy(out_ref.at[m], recv.at[m], send_sem.at[m], recv_sem.at[m], here + 1, col).start()

        return carry

    lax.fori_loop(0, micro_count, step, 0)

    @pl.when(here < count - 1)
    def _():
        for m in range(micro_count):
            line_copy(out_ref.at[m], recv.at[m], send_sem.at[m], recv_sem.at[m], here + 1, col).wait_send()


def forward_line(clips_local, weight):
    shape = jax.ShapeDtypeStruct(clips_local.shape, clips_local.dtype)
    micro_count, cells, channels = clips_local.shape
    return pl.pallas_call(
        forward_kernel,
        out_shape=(shape, shape),
        in_specs=[pl.BlockSpec(memory_space=pltpu.VMEM)] * 2,
        out_specs=(pl.BlockSpec(memory_space=pltpu.VMEM),) * 2,
        scratch_shapes=[
            pltpu.VMEM(clips_local.shape, clips_local.dtype),
            pltpu.VMEM((cells // 64 + 2, 10, 10, channels), jnp.float32),
            pltpu.SemaphoreType.DMA((micro_count,)),
            pltpu.SemaphoreType.DMA((micro_count,)),
        ],
        compiler_params=pltpu.CompilerParams(collective_id=2, has_side_effects=True),
    )(clips_local, weight)


def backward_kernel(cot_ref, seen_ref, w_ref, wg_ref, recv, sendbuf, pad, gpad, send_sem, recv_sem):
    count = lax.axis_size("section")
    here = lax.axis_index("section")
    col = lax.axis_index("dp")
    micro_count = cot_ref.shape[0]
    greet_line(here, count, col)
    pad[...] = jnp.zeros_like(pad)
    gpad[...] = jnp.zeros_like(gpad)
    wg_ref[...] = jnp.zeros_like(wg_ref)

    def step(m, carry):
        @pl.when(here == count - 1)
        def _():
            recv[m] = cot_ref[m]

        @pl.when(here < count - 1)
        def _():
            line_copy(sendbuf.at[m], recv.at[m], send_sem.at[m], recv_sem.at[m], here + 1, col).wait_recv()

        upstream = recv[m]
        base = seen_ref[m].astype(jnp.float32)
        squash_into(pad, base)
        for tap in range(27):
            wg_ref[tap] += lax.dot_general(
                tap_window(pad, tap, 4, False), upstream, (((0,), (0,)), ((), ())),
                preferred_element_type=jnp.float32,
            )

        @pl.when(here > 0)
        def _():
            up = upstream.astype(jnp.float32)
            gpad[2:6, 1:9, 1:9, :] = up.reshape(4, 8, 8, up.shape[-1])
            spread = jnp.zeros((384, up.shape[-1]), jnp.float32)
            for tap in range(27):
                spread = spread + lax.dot_general(
                    tap_window(gpad, tap, 6, True), w_ref[tap], (((1,), (1,)), ((), ())),
                    preferred_element_type=jnp.float32,
                )
            field = jnp.concatenate([spread[0:64] + spread[64:128] + spread[128:192], spread[192:384]], axis=0)
            sig = 1.0 / (1.0 + jnp.exp(-base))
            slope = sig * (1.0 + base * (1.0 - sig))
            sendbuf[m] = (up + field * slope).astype(sendbuf.dtype)
            line_copy(sendbuf.at[m], recv.at[m], send_sem.at[m], recv_sem.at[m], here - 1, col).start()

        return carry

    lax.fori_loop(0, micro_count, step, 0)

    @pl.when(here > 0)
    def _():
        for m in range(micro_count):
            line_copy(sendbuf.at[m], recv.at[m], send_sem.at[m], recv_sem.at[m], here - 1, col).wait_send()


def backward_line(cot_local, seen, weight):
    micro_count, cells, channels = cot_local.shape
    taps = weight.shape[0]
    return pl.pallas_call(
        backward_kernel,
        out_shape=jax.ShapeDtypeStruct((taps, channels, channels), jnp.float32),
        in_specs=[pl.BlockSpec(memory_space=pltpu.VMEM)] * 3,
        out_specs=pl.BlockSpec(memory_space=pltpu.VMEM),
        scratch_shapes=[
            pltpu.VMEM(cot_local.shape, cot_local.dtype),
            pltpu.VMEM(cot_local.shape, cot_local.dtype),
            pltpu.VMEM((cells // 64 + 2, 10, 10, channels), jnp.float32),
            pltpu.VMEM((cells // 64 + 4, 10, 10, channels), jnp.float32),
            pltpu.SemaphoreType.DMA((micro_count,)),
            pltpu.SemaphoreType.DMA((micro_count,)),
        ],
        compiler_params=pltpu.CompilerParams(collective_id=3, has_side_effects=True),
    )(cot_local, seen, weight)


def per_device(clips, cotangent, weights):
    channels = weights.shape[-1]
    weight = gather_rows(weights[0]).reshape(-1, channels, channels)
    micro_count = clips.shape[0]
    clips_local = clips[:, 0].reshape(micro_count, -1, channels)
    cot_local = cotangent[:, 0].reshape(micro_count, -1, channels)
    seen, produced = forward_line(clips_local, weight)
    grad_total = backward_line(cot_local, seen, weight)
    grad_share = scatter_rows(grad_total.reshape(lax.axis_size("dp"), -1, channels))
    return (produced.reshape(clips[:, 0].shape)[None, :, None], grad_share[None])


def solution(mesh):
    placed = (
        P(None, "dp", None, None, None, None),
        P(None, "dp", None, None, None, None),
        P("section", "dp", None),
    )
    return jax.shard_map(
        per_device,
        mesh=mesh,
        in_specs=placed,
        out_specs=(P("section", None, "dp", None, None, None, None), P("section", "dp", None)),
        check_vma=False,
    )
```

```python
import jax
import jax.numpy as jnp
from jax import lax
from jax.sharding import PartitionSpec as P

from jax.experimental import pallas as pl
from jax.experimental.pallas import tpu as pltpu

MESH_ID = pl.DeviceIdType.MESH


def greet_group(here, row):
    pair = here - here % 2
    partner = pair + 1 - here % 2
    barrier = pltpu.get_barrier_semaphore()
    pl.semaphore_signal(barrier, inc=1, device_id=(row, partner), device_id_type=MESH_ID)

    def signal(i, carry):
        peer = lax.rem(here + 2 * i, lax.axis_size("dp"))
        pl.semaphore_signal(barrier, inc=1, device_id=(row, peer), device_id_type=MESH_ID)
        return carry

    planes = lax.axis_size("dp") // 2
    lax.fori_loop(1, planes, signal, 0)
    pl.semaphore_wait(barrier, planes)
    return partner


def group_copy(src, dst, send_sem, recv_sem, row, peer):
    return pltpu.make_async_remote_copy(
        src_ref=src,
        dst_ref=dst,
        send_sem=send_sem,
        recv_sem=recv_sem,
        device_id=(row, peer),
        device_id_type=MESH_ID,
    )


def gather_kernel(shard_ref, out_ref, send_sem, recv_sem):
    peers = lax.axis_size("dp")
    here = lax.axis_index("dp")
    row = lax.axis_index("section")
    partner = greet_group(here, row)
    planes = peers // 2
    cross = group_copy(shard_ref, out_ref.at[here], send_sem.at[here], recv_sem.at[here], row, partner)
    cross.start()
    out_ref[here] = shard_ref[...]
    cross.wait_send()
    group_copy(shard_ref, out_ref.at[partner], send_sem.at[partner], recv_sem.at[partner], row, partner).wait_recv()

    def fan(i, peer):
        own = group_copy(shard_ref, out_ref.at[here], send_sem.at[peer], recv_sem.at[here], row, peer)
        relayed = group_copy(out_ref.at[partner], out_ref.at[partner], send_sem.at[peer + 1 - 2 * (peer % 2)],
                             recv_sem.at[partner], row, peer)
        return own, relayed

    def start(i, carry):
        peer = lax.rem(here + 2 * i, peers)
        own, relayed = fan(i, peer)
        own.start()
        relayed.start()
        return carry

    lax.fori_loop(1, planes, start, 0)

    def finish(i, carry):
        peer = lax.rem(here + 2 * i, peers)
        own, relayed = fan(i, peer)
        own.wait_send()
        relayed.wait_send()
        mate = peer + 1 - 2 * (peer % 2)
        group_copy(shard_ref, out_ref.at[peer], send_sem.at[peer], recv_sem.at[peer], row, peer).wait_recv()
        group_copy(shard_ref, out_ref.at[mate], send_sem.at[mate], recv_sem.at[mate], row, peer).wait_recv()
        return carry

    lax.fori_loop(1, planes, finish, 0)


def gather_rows(shard):
    peers = lax.axis_size("dp")
    rows, cols = shard.shape
    return pl.pallas_call(
        gather_kernel,
        out_shape=jax.ShapeDtypeStruct((peers, rows, cols), shard.dtype),
        in_specs=[pl.BlockSpec(memory_space=pltpu.VMEM)],
        out_specs=pl.BlockSpec(memory_space=pltpu.VMEM),
        scratch_shapes=[pltpu.SemaphoreType.DMA((peers,)), pltpu.SemaphoreType.DMA((peers,))],
        compiler_params=pltpu.CompilerParams(collective_id=0, has_side_effects=True),
    )(shard)


def scatter_kernel(parts_ref, out_ref, held, mine, theirs, send_sem, recv_sem, cross_sem):
    peers = lax.axis_size("dp")
    here = lax.axis_index("dp")
    row = lax.axis_index("section")
    partner = greet_group(here, row)
    planes = peers // 2
    slot = here // 2
    side = here % 2

    def fan(peer, block):
        return group_copy(parts_ref.at[2 * (peer // 2) + block], held.at[slot, block],
                          send_sem.at[peer // 2, block], recv_sem.at[slot, block], row, peer)

    def start(i, carry):
        peer = lax.rem(here + 2 * i, peers)
        fan(peer, 0).start()
        fan(peer, 1).start()
        return carry

    lax.fori_loop(1, planes, start, 0)

    def finish(i, totals):
        peer = lax.rem(here + 2 * i, peers)
        fan(peer, 0).wait_send()
        fan(peer, 1).wait_send()
        source = peer // 2
        for block in range(2):
            group_copy(parts_ref.at[block], held.at[source, block], send_sem.at[source, block],
                       recv_sem.at[source, block], row, peer).wait_recv()
        return (totals[0] + held[source, 0], totals[1] + held[source, 1])

    first, second = lax.fori_loop(1, planes, finish, (parts_ref[2 * slot], parts_ref[2 * slot + 1]))
    theirs[...] = jnp.where(side == 0, second, first)
    cross = group_copy(theirs, mine, cross_sem.at[0], cross_sem.at[1], row, partner)
    cross.start()
    cross.wait_send()
    cross.wait_recv()
    out_ref[...] = jnp.where(side == 0, first, second) + mine[...]


def scatter_rows(parts):
    peers, rows, cols = parts.shape
    return pl.pallas_call(
        scatter_kernel,
        out_shape=jax.ShapeDtypeStruct((rows, cols), parts.dtype),
        in_specs=[pl.BlockSpec(memory_space=pltpu.VMEM)],
        out_specs=pl.BlockSpec(memory_space=pltpu.VMEM),
        scratch_shapes=[
            pltpu.VMEM((peers // 2, 2, rows, cols), parts.dtype),
            pltpu.VMEM((rows, cols), parts.dtype),
            pltpu.VMEM((rows, cols), parts.dtype),
            pltpu.SemaphoreType.DMA((peers // 2, 2)),
            pltpu.SemaphoreType.DMA((peers // 2, 2)),
            pltpu.SemaphoreType.DMA((2,)),
        ],
        compiler_params=pltpu.CompilerParams(collective_id=1, has_side_effects=True),
    )(parts)


def squash_into(pad_ref, activation):
    squashed = (activation / (1.0 + jnp.exp(-activation))).astype(jnp.bfloat16).astype(jnp.float32)
    field = squashed.reshape(pad_ref.shape[0] - 2, 8, 8, pad_ref.shape[-1])
    pad_ref[2:, 1:9, 1:9, :] = field
    pad_ref[0:2, 1:9, 1:9, :] = jnp.broadcast_to(field[0:1], (2,) + field.shape[1:])


def tap_window(pad_ref, tap, frames, base):
    offset_time, offset_row, offset_col = tap // 9, (tap // 3) % 3, tap % 3
    if base:
        t0, r0, c0 = 2 - offset_time, 2 - offset_row, 2 - offset_col
    else:
        t0, r0, c0 = offset_time, offset_row, offset_col
    window = pad_ref[t0 : t0 + frames, r0 : r0 + 8, c0 : c0 + 8, :]
    return window.reshape(frames * 64, window.shape[-1]).astype(jnp.bfloat16)


def greet_line(here, count, col):
    barrier = pltpu.get_barrier_semaphore()

    @pl.when(here > 0)
    def _():
        pl.semaphore_signal(barrier, inc=1, device_id=(here - 1, col), device_id_type=MESH_ID)

    @pl.when(here < count - 1)
    def _():
        pl.semaphore_signal(barrier, inc=1, device_id=(here + 1, col), device_id_type=MESH_ID)

    neighbours = (here + count - 1) // count + (2 * count - 2 - here) // count
    pl.semaphore_wait(barrier, neighbours)


def line_copy(src, dst, send_sem, recv_sem, target, col):
    return pltpu.make_async_remote_copy(
        src_ref=src,
        dst_ref=dst,
        send_sem=send_sem,
        recv_sem=recv_sem,
        device_id=(target, col),
        device_id_type=MESH_ID,
    )


def forward_kernel(clips_ref, w_ref, seen_ref, out_ref, recv, pad, send_sem, recv_sem):
    count = lax.axis_size("section")
    here = lax.axis_index("section")
    col = lax.axis_index("dp")
    micro_count = clips_ref.shape[0]
    greet_line(here, count, col)
    pad[...] = jnp.zeros_like(pad)

    def step(m, carry):
        @pl.when(here == 0)
        def _():
            seen_ref[m] = clips_ref[m]

        @pl.when(here > 0)
        def _():
            line_copy(out_ref.at[m], recv.at[m], send_sem.at[m], recv_sem.at[m], here - 1, col).wait_recv()
            seen_ref[m] = recv[m]

        base = seen_ref[m].astype(jnp.float32)
        squash_into(pad, base)
        total = base
        for tap in range(27):
            total = total + jnp.dot(tap_window(pad, tap, 4, False), w_ref[tap], preferred_element_type=jnp.float32)
        out_ref[m] = total.astype(out_ref.dtype)

        @pl.when(here < count - 1)
        def _():
            line_copy(out_ref.at[m], recv.at[m], send_sem.at[m], recv_sem.at[m], here + 1, col).start()

        return carry

    lax.fori_loop(0, micro_count, step, 0)

    @pl.when(here < count - 1)
    def _():
        for m in range(micro_count):
            line_copy(out_ref.at[m], recv.at[m], send_sem.at[m], recv_sem.at[m], here + 1, col).wait_send()


def forward_line(clips_local, weight):
    shape = jax.ShapeDtypeStruct(clips_local.shape, clips_local.dtype)
    micro_count, cells, channels = clips_local.shape
    return pl.pallas_call(
        forward_kernel,
        out_shape=(shape, shape),
        in_specs=[pl.BlockSpec(memory_space=pltpu.VMEM)] * 2,
        out_specs=(pl.BlockSpec(memory_space=pltpu.VMEM),) * 2,
        scratch_shapes=[
            pltpu.VMEM(clips_local.shape, clips_local.dtype),
            pltpu.VMEM((cells // 64 + 2, 10, 10, channels), jnp.float32),
            pltpu.SemaphoreType.DMA((micro_count,)),
            pltpu.SemaphoreType.DMA((micro_count,)),
        ],
        compiler_params=pltpu.CompilerParams(collective_id=2, has_side_effects=True),
    )(clips_local, weight)


def backward_kernel(cot_ref, seen_ref, w_ref, wg_ref, recv, sendbuf, pad, gpad, send_sem, recv_sem):
    count = lax.axis_size("section")
    here = lax.axis_index("section")
    col = lax.axis_index("dp")
    micro_count = cot_ref.shape[0]
    greet_line(here, count, col)
    pad[...] = jnp.zeros_like(pad)
    gpad[...] = jnp.zeros_like(gpad)
    wg_ref[...] = jnp.zeros_like(wg_ref)

    def step(m, carry):
        @pl.when(here == count - 1)
        def _():
            recv[m] = cot_ref[m]

        @pl.when(here < count - 1)
        def _():
            line_copy(sendbuf.at[m], recv.at[m], send_sem.at[m], recv_sem.at[m], here + 1, col).wait_recv()

        upstream = recv[m]
        base = seen_ref[m].astype(jnp.float32)
        squash_into(pad, base)
        @pl.when(here > 0)
        def _():
            up = upstream.astype(jnp.float32)
            gpad[2:6, 1:9, 1:9, :] = up.reshape(4, 8, 8, up.shape[-1])
            spread = jnp.zeros((384, up.shape[-1]), jnp.float32)
            for tap in range(27):
                spread = spread + lax.dot_general(
                    tap_window(gpad, tap, 6, True), w_ref[tap], (((1,), (1,)), ((), ())),
                    preferred_element_type=jnp.float32,
                )
            field = jnp.concatenate([spread[0:64] + spread[64:128] + spread[128:192], spread[192:384]], axis=0)
            sig = 1.0 / (1.0 + jnp.exp(-base))
            slope = sig * (1.0 + base * (1.0 - sig))
            sendbuf[m] = (up + field * slope).astype(sendbuf.dtype)
            line_copy(sendbuf.at[m], recv.at[m], send_sem.at[m], recv_sem.at[m], here - 1, col).start()

        for tap in range(27):
            wg_ref[tap] += lax.dot_general(
                tap_window(pad, tap, 4, False), upstream, (((0,), (0,)), ((), ())),
                preferred_element_type=jnp.float32,
            )
        return carry

    lax.fori_loop(0, micro_count, step, 0)

    @pl.when(here > 0)
    def _():
        for m in range(micro_count):
            line_copy(sendbuf.at[m], recv.at[m], send_sem.at[m], recv_sem.at[m], here - 1, col).wait_send()


def backward_line(cot_local, seen, weight):
    micro_count, cells, channels = cot_local.shape
    taps = weight.shape[0]
    return pl.pallas_call(
        backward_kernel,
        out_shape=jax.ShapeDtypeStruct((taps, channels, channels), jnp.float32),
        in_specs=[pl.BlockSpec(memory_space=pltpu.VMEM)] * 3,
        out_specs=pl.BlockSpec(memory_space=pltpu.VMEM),
        scratch_shapes=[
            pltpu.VMEM(cot_local.shape, cot_local.dtype),
            pltpu.VMEM(cot_local.shape, cot_local.dtype),
            pltpu.VMEM((cells // 64 + 2, 10, 10, channels), jnp.float32),
            pltpu.VMEM((cells // 64 + 4, 10, 10, channels), jnp.float32),
            pltpu.SemaphoreType.DMA((micro_count,)),
            pltpu.SemaphoreType.DMA((micro_count,)),
        ],
        compiler_params=pltpu.CompilerParams(collective_id=3, has_side_effects=True),
    )(cot_local, seen, weight)


def per_device(clips, cotangent, weights):
    channels = weights.shape[-1]
    weight = gather_rows(weights[0]).reshape(-1, channels, channels)
    micro_count = clips.shape[0]
    clips_local = clips[:, 0].reshape(micro_count, -1, channels)
    cot_local = cotangent[:, 0].reshape(micro_count, -1, channels)
    seen, produced = forward_line(clips_local, weight)
    grad_total = backward_line(cot_local, seen, weight)
    grad_share = scatter_rows(grad_total.reshape(lax.axis_size("dp"), -1, channels))
    return (produced.reshape(clips[:, 0].shape)[None, :, None], grad_share[None])


def solution(mesh):
    placed = (
        P(None, "dp", None, None, None, None),
        P(None, "dp", None, None, None, None),
        P("section", "dp", None),
    )
    return jax.shard_map(
        per_device,
        mesh=mesh,
        in_specs=placed,
        out_specs=(P("section", None, "dp", None, None, None, None), P("section", "dp", None)),
        check_vma=False,
    )
```

```python
import jax
import jax.numpy as jnp
from jax import lax
from jax.sharding import PartitionSpec as P

from jax.experimental import pallas as pl
from jax.experimental.pallas import tpu as pltpu

MESH_ID = pl.DeviceIdType.MESH


def greet_group(here, row):
    pair = here - here % 2
    partner = pair + 1 - here % 2
    barrier = pltpu.get_barrier_semaphore()
    pl.semaphore_signal(barrier, inc=1, device_id=(row, partner), device_id_type=MESH_ID)

    def signal(i, carry):
        peer = lax.rem(here + 2 * i, lax.axis_size("dp"))
        pl.semaphore_signal(barrier, inc=1, device_id=(row, peer), device_id_type=MESH_ID)
        return carry

    planes = lax.axis_size("dp") // 2
    lax.fori_loop(1, planes, signal, 0)
    pl.semaphore_wait(barrier, planes)
    return partner


def group_copy(src, dst, send_sem, recv_sem, row, peer):
    return pltpu.make_async_remote_copy(
        src_ref=src,
        dst_ref=dst,
        send_sem=send_sem,
        recv_sem=recv_sem,
        device_id=(row, peer),
        device_id_type=MESH_ID,
    )


def gather_kernel(shard_ref, out_ref, send_sem, recv_sem):
    peers = lax.axis_size("dp")
    here = lax.axis_index("dp")
    row = lax.axis_index("section")
    partner = greet_group(here, row)
    planes = peers // 2
    cross = group_copy(shard_ref, out_ref.at[here], send_sem.at[here], recv_sem.at[here], row, partner)
    cross.start()

    def fan(i, peer):
        own = group_copy(shard_ref, out_ref.at[here], send_sem.at[peer], recv_sem.at[here], row, peer)
        relayed = group_copy(out_ref.at[partner], out_ref.at[partner], send_sem.at[peer + 1 - 2 * (peer % 2)],
                             recv_sem.at[partner], row, peer)
        return own, relayed

    def start_own(i, carry):
        fan(i, lax.rem(here + 2 * i, peers))[0].start()
        return carry

    def start_relay(i, carry):
        fan(i, lax.rem(here + 2 * i, peers))[1].start()
        return carry

    lax.fori_loop(1, planes, start_own, 0)
    out_ref[here] = shard_ref[...]
    cross.wait_send()
    group_copy(shard_ref, out_ref.at[partner], send_sem.at[partner], recv_sem.at[partner], row, partner).wait_recv()
    lax.fori_loop(1, planes, start_relay, 0)

    def finish(i, carry):
        peer = lax.rem(here + 2 * i, peers)
        own, relayed = fan(i, peer)
        own.wait_send()
        relayed.wait_send()
        mate = peer + 1 - 2 * (peer % 2)
        group_copy(shard_ref, out_ref.at[peer], send_sem.at[peer], recv_sem.at[peer], row, peer).wait_recv()
        group_copy(shard_ref, out_ref.at[mate], send_sem.at[mate], recv_sem.at[mate], row, peer).wait_recv()
        return carry

    lax.fori_loop(1, planes, finish, 0)


def gather_rows(shard):
    peers = lax.axis_size("dp")
    rows, cols = shard.shape
    return pl.pallas_call(
        gather_kernel,
        out_shape=jax.ShapeDtypeStruct((peers, rows, cols), shard.dtype),
        in_specs=[pl.BlockSpec(memory_space=pltpu.VMEM)],
        out_specs=pl.BlockSpec(memory_space=pltpu.VMEM),
        scratch_shapes=[pltpu.SemaphoreType.DMA((peers,)), pltpu.SemaphoreType.DMA((peers,))],
        compiler_params=pltpu.CompilerParams(collective_id=0, has_side_effects=True),
    )(shard)


def scatter_kernel(parts_ref, out_ref, held, mine, theirs, send_sem, recv_sem, cross_sem):
    peers = lax.axis_size("dp")
    here = lax.axis_index("dp")
    row = lax.axis_index("section")
    partner = greet_group(here, row)
    planes = peers // 2
    slot = here // 2
    side = here % 2

    def fan(peer, block):
        return group_copy(parts_ref.at[2 * (peer // 2) + block], held.at[slot, block],
                          send_sem.at[peer // 2, block], recv_sem.at[slot, block], row, peer)

    def start(i, carry):
        peer = lax.rem(here + 2 * i, peers)
        fan(peer, 0).start()
        fan(peer, 1).start()
        return carry

    lax.fori_loop(1, planes, start, 0)

    def finish(i, totals):
        peer = lax.rem(here + 2 * i, peers)
        fan(peer, 0).wait_send()
        fan(peer, 1).wait_send()
        source = peer // 2
        for block in range(2):
            group_copy(parts_ref.at[block], held.at[source, block], send_sem.at[source, block],
                       recv_sem.at[source, block], row, peer).wait_recv()
        return (totals[0] + held[source, 0].astype(jnp.float32), totals[1] + held[source, 1].astype(jnp.float32))

    start_totals = (parts_ref[2 * slot].astype(jnp.float32), parts_ref[2 * slot + 1].astype(jnp.float32))
    first, second = lax.fori_loop(1, planes, finish, start_totals)
    theirs[...] = jnp.where(side == 0, second, first)
    cross = group_copy(theirs, mine, cross_sem.at[0], cross_sem.at[1], row, partner)
    cross.start()
    cross.wait_send()
    cross.wait_recv()
    out_ref[...] = jnp.where(side == 0, first, second) + mine[...]


def scatter_rows(parts):
    peers, rows, cols = parts.shape
    return pl.pallas_call(
        scatter_kernel,
        out_shape=jax.ShapeDtypeStruct((rows, cols), jnp.float32),
        in_specs=[pl.BlockSpec(memory_space=pltpu.VMEM)],
        out_specs=pl.BlockSpec(memory_space=pltpu.VMEM),
        scratch_shapes=[
            pltpu.VMEM((peers // 2, 2, rows, cols), parts.dtype),
            pltpu.VMEM((rows, cols), jnp.float32),
            pltpu.VMEM((rows, cols), jnp.float32),
            pltpu.SemaphoreType.DMA((peers // 2, 2)),
            pltpu.SemaphoreType.DMA((peers // 2, 2)),
            pltpu.SemaphoreType.DMA((2,)),
        ],
        compiler_params=pltpu.CompilerParams(collective_id=1, has_side_effects=True),
    )(parts)


def squash_into(pad_ref, activation):
    squashed = (activation / (1.0 + jnp.exp(-activation))).astype(jnp.bfloat16).astype(jnp.float32)
    field = squashed.reshape(pad_ref.shape[0] - 2, 8, 8, pad_ref.shape[-1])
    pad_ref[2:, 1:9, 1:9, :] = field
    pad_ref[0:2, 1:9, 1:9, :] = jnp.broadcast_to(field[0:1], (2,) + field.shape[1:])


def tap_window(pad_ref, tap, frames, base):
    offset_time, offset_row, offset_col = tap // 9, (tap // 3) % 3, tap % 3
    if base:
        t0, r0, c0 = 2 - offset_time, 2 - offset_row, 2 - offset_col
    else:
        t0, r0, c0 = offset_time, offset_row, offset_col
    window = pad_ref[t0 : t0 + frames, r0 : r0 + 8, c0 : c0 + 8, :]
    return window.reshape(frames * 64, window.shape[-1]).astype(jnp.bfloat16)


def greet_line(here, count, col):
    barrier = pltpu.get_barrier_semaphore()

    @pl.when(here > 0)
    def _():
        pl.semaphore_signal(barrier, inc=1, device_id=(here - 1, col), device_id_type=MESH_ID)

    @pl.when(here < count - 1)
    def _():
        pl.semaphore_signal(barrier, inc=1, device_id=(here + 1, col), device_id_type=MESH_ID)

    neighbours = (here + count - 1) // count + (2 * count - 2 - here) // count
    pl.semaphore_wait(barrier, neighbours)


def line_copy(src, dst, send_sem, recv_sem, target, col):
    return pltpu.make_async_remote_copy(
        src_ref=src,
        dst_ref=dst,
        send_sem=send_sem,
        recv_sem=recv_sem,
        device_id=(target, col),
        device_id_type=MESH_ID,
    )


def forward_kernel(clips_ref, w_ref, seen_ref, out_ref, recv, pad, send_sem, recv_sem):
    count = lax.axis_size("section")
    here = lax.axis_index("section")
    col = lax.axis_index("dp")
    micro_count = clips_ref.shape[0]
    greet_line(here, count, col)
    pad[...] = jnp.zeros_like(pad)

    def step(m, carry):
        @pl.when(here == 0)
        def _():
            seen_ref[m] = clips_ref[m]

        @pl.when(here > 0)
        def _():
            line_copy(out_ref.at[m], recv.at[m], send_sem.at[m], recv_sem.at[m], here - 1, col).wait_recv()
            seen_ref[m] = recv[m]

        base = seen_ref[m].astype(jnp.float32)
        squash_into(pad, base)
        total = base
        for tap in range(27):
            total = total + jnp.dot(tap_window(pad, tap, 4, False), w_ref[tap], preferred_element_type=jnp.float32)
        out_ref[m] = total.astype(out_ref.dtype)

        @pl.when(here < count - 1)
        def _():
            line_copy(out_ref.at[m], recv.at[m], send_sem.at[m], recv_sem.at[m], here + 1, col).start()

        return carry

    lax.fori_loop(0, micro_count, step, 0)

    @pl.when(here < count - 1)
    def _():
        for m in range(micro_count):
            line_copy(out_ref.at[m], recv.at[m], send_sem.at[m], recv_sem.at[m], here + 1, col).wait_send()


def forward_line(clips_local, weight):
    shape = jax.ShapeDtypeStruct(clips_local.shape, clips_local.dtype)
    micro_count, cells, channels = clips_local.shape
    return pl.pallas_call(
        forward_kernel,
        out_shape=(shape, shape),
        in_specs=[pl.BlockSpec(memory_space=pltpu.VMEM)] * 2,
        out_specs=(pl.BlockSpec(memory_space=pltpu.VMEM),) * 2,
        scratch_shapes=[
            pltpu.VMEM(clips_local.shape, clips_local.dtype),
            pltpu.VMEM((cells // 64 + 2, 10, 10, channels), jnp.float32),
            pltpu.SemaphoreType.DMA((micro_count,)),
            pltpu.SemaphoreType.DMA((micro_count,)),
        ],
        compiler_params=pltpu.CompilerParams(collective_id=2, has_side_effects=True),
    )(clips_local, weight)


def backward_kernel(cot_ref, seen_ref, w_ref, wg_ref, recv, sendbuf, pad, gpad, send_sem, recv_sem):
    count = lax.axis_size("section")
    here = lax.axis_index("section")
    col = lax.axis_index("dp")
    micro_count = cot_ref.shape[0]
    greet_line(here, count, col)
    pad[...] = jnp.zeros_like(pad)
    gpad[...] = jnp.zeros_like(gpad)
    wg_ref[...] = jnp.zeros_like(wg_ref)

    def step(m, carry):
        @pl.when(here == count - 1)
        def _():
            recv[m] = cot_ref[m]

        @pl.when(here < count - 1)
        def _():
            line_copy(sendbuf.at[m], recv.at[m], send_sem.at[m], recv_sem.at[m], here + 1, col).wait_recv()

        upstream = recv[m]
        base = seen_ref[m].astype(jnp.float32)
        squash_into(pad, base)
        @pl.when(here > 0)
        def _():
            up = upstream.astype(jnp.float32)
            gpad[2:6, 1:9, 1:9, :] = up.reshape(4, 8, 8, up.shape[-1])
            spread = jnp.zeros((384, up.shape[-1]), jnp.float32)
            for tap in range(27):
                spread = spread + lax.dot_general(
                    tap_window(gpad, tap, 6, True), w_ref[tap], (((1,), (1,)), ((), ())),
                    preferred_element_type=jnp.float32,
                )
            field = jnp.concatenate([spread[0:64] + spread[64:128] + spread[128:192], spread[192:384]], axis=0)
            sig = 1.0 / (1.0 + jnp.exp(-base))
            slope = sig * (1.0 + base * (1.0 - sig))
            sendbuf[m] = (up + field * slope).astype(sendbuf.dtype)
            line_copy(sendbuf.at[m], recv.at[m], send_sem.at[m], recv_sem.at[m], here - 1, col).start()

        for tap in range(27):
            wg_ref[tap] += lax.dot_general(
                tap_window(pad, tap, 4, False), upstream, (((0,), (0,)), ((), ())),
                preferred_element_type=jnp.float32,
            )
        return carry

    lax.fori_loop(0, micro_count, step, 0)

    @pl.when(here > 0)
    def _():
        for m in range(micro_count):
            line_copy(sendbuf.at[m], recv.at[m], send_sem.at[m], recv_sem.at[m], here - 1, col).wait_send()


def backward_line(cot_local, seen, weight):
    micro_count, cells, channels = cot_local.shape
    taps = weight.shape[0]
    return pl.pallas_call(
        backward_kernel,
        out_shape=jax.ShapeDtypeStruct((taps, channels, channels), jnp.float32),
        in_specs=[pl.BlockSpec(memory_space=pltpu.VMEM)] * 3,
        out_specs=pl.BlockSpec(memory_space=pltpu.VMEM),
        scratch_shapes=[
            pltpu.VMEM(cot_local.shape, cot_local.dtype),
            pltpu.VMEM(cot_local.shape, cot_local.dtype),
            pltpu.VMEM((cells // 64 + 2, 10, 10, channels), jnp.float32),
            pltpu.VMEM((cells // 64 + 4, 10, 10, channels), jnp.float32),
            pltpu.SemaphoreType.DMA((micro_count,)),
            pltpu.SemaphoreType.DMA((micro_count,)),
        ],
        compiler_params=pltpu.CompilerParams(collective_id=3, has_side_effects=True),
    )(cot_local, seen, weight)


def per_device(clips, cotangent, weights):
    channels = weights.shape[-1]
    weight = gather_rows(weights[0]).reshape(-1, channels, channels)
    micro_count = clips.shape[0]
    clips_local = clips[:, 0].reshape(micro_count, -1, channels)
    cot_local = cotangent[:, 0].reshape(micro_count, -1, channels)
    seen, produced = forward_line(clips_local, weight)
    grad_total = backward_line(cot_local, seen, weight)
    grad_share = scatter_rows(grad_total.astype(jnp.bfloat16).reshape(lax.axis_size("dp"), -1, channels))
    return (produced.reshape(clips[:, 0].shape)[None, :, None], grad_share[None])


def solution(mesh):
    placed = (
        P(None, "dp", None, None, None, None),
        P(None, "dp", None, None, None, None),
        P("section", "dp", None),
    )
    return jax.shard_map(
        per_device,
        mesh=mesh,
        in_specs=placed,
        out_specs=(P("section", None, "dp", None, None, None, None), P("section", "dp", None)),
        check_vma=False,
    )
```

```python
import jax
import jax.numpy as jnp
from jax import lax
from jax.sharding import PartitionSpec as P

from jax.experimental import pallas as pl
from jax.experimental.pallas import tpu as pltpu

MESH_ID = pl.DeviceIdType.MESH


def greet_group(here, row):
    pair = here - here % 2
    partner = pair + 1 - here % 2
    barrier = pltpu.get_barrier_semaphore()
    pl.semaphore_signal(barrier, inc=1, device_id=(row, partner), device_id_type=MESH_ID)

    def signal(i, carry):
        peer = lax.rem(here + 2 * i, lax.axis_size("dp"))
        pl.semaphore_signal(barrier, inc=1, device_id=(row, peer), device_id_type=MESH_ID)
        return carry

    planes = lax.axis_size("dp") // 2
    lax.fori_loop(1, planes, signal, 0)
    pl.semaphore_wait(barrier, planes)
    return partner


def group_copy(src, dst, send_sem, recv_sem, row, peer):
    return pltpu.make_async_remote_copy(
        src_ref=src,
        dst_ref=dst,
        send_sem=send_sem,
        recv_sem=recv_sem,
        device_id=(row, peer),
        device_id_type=MESH_ID,
    )


def gather_kernel(shard_ref, out_ref, send_sem, recv_sem):
    peers = lax.axis_size("dp")
    here = lax.axis_index("dp")
    row = lax.axis_index("section")
    partner = greet_group(here, row)
    planes = peers // 2
    cross = group_copy(shard_ref, out_ref.at[here], send_sem.at[here], recv_sem.at[here], row, partner)
    cross.start()

    def fan(i, peer):
        own = group_copy(shard_ref, out_ref.at[here], send_sem.at[peer], recv_sem.at[here], row, peer)
        relayed = group_copy(out_ref.at[partner], out_ref.at[partner], send_sem.at[peer + 1 - 2 * (peer % 2)],
                             recv_sem.at[partner], row, peer)
        return own, relayed

    def start_own(i, carry):
        fan(i, lax.rem(here + 2 * i, peers))[0].start()
        return carry

    def start_relay(i, carry):
        fan(i, lax.rem(here + 2 * i, peers))[1].start()
        return carry

    lax.fori_loop(1, planes, start_own, 0)
    out_ref[here] = shard_ref[...]
    cross.wait_send()
    group_copy(shard_ref, out_ref.at[partner], send_sem.at[partner], recv_sem.at[partner], row, partner).wait_recv()
    lax.fori_loop(1, planes, start_relay, 0)

    def finish(i, carry):
        peer = lax.rem(here + 2 * i, peers)
        own, relayed = fan(i, peer)
        own.wait_send()
        relayed.wait_send()
        mate = peer + 1 - 2 * (peer % 2)
        group_copy(shard_ref, out_ref.at[peer], send_sem.at[peer], recv_sem.at[peer], row, peer).wait_recv()
        group_copy(shard_ref, out_ref.at[mate], send_sem.at[mate], recv_sem.at[mate], row, peer).wait_recv()
        return carry

    lax.fori_loop(1, planes, finish, 0)


def gather_rows(shard):
    peers = lax.axis_size("dp")
    rows, cols = shard.shape
    return pl.pallas_call(
        gather_kernel,
        out_shape=jax.ShapeDtypeStruct((peers, rows, cols), shard.dtype),
        in_specs=[pl.BlockSpec(memory_space=pltpu.VMEM)],
        out_specs=pl.BlockSpec(memory_space=pltpu.VMEM),
        scratch_shapes=[pltpu.SemaphoreType.DMA((peers,)), pltpu.SemaphoreType.DMA((peers,))],
        compiler_params=pltpu.CompilerParams(collective_id=0, has_side_effects=True),
    )(shard)


def scatter_kernel(parts_ref, out_ref, held, mine, theirs, send_sem, recv_sem, cross_sem):
    peers = lax.axis_size("dp")
    here = lax.axis_index("dp")
    row = lax.axis_index("section")
    partner = greet_group(here, row)
    planes = peers // 2
    slot = here // 2
    side = here % 2

    def fan(peer, block):
        return group_copy(parts_ref.at[2 * (peer // 2) + block], held.at[slot, block],
                          send_sem.at[peer // 2, block], recv_sem.at[slot, block], row, peer)

    def start(i, carry):
        peer = lax.rem(here + 2 * i, peers)
        fan(peer, 0).start()
        fan(peer, 1).start()
        return carry

    lax.fori_loop(1, planes, start, 0)

    def finish(i, totals):
        peer = lax.rem(here + 2 * i, peers)
        fan(peer, 0).wait_send()
        fan(peer, 1).wait_send()
        source = peer // 2
        for block in range(2):
            group_copy(parts_ref.at[block], held.at[source, block], send_sem.at[source, block],
                       recv_sem.at[source, block], row, peer).wait_recv()
        return (totals[0] + held[source, 0].astype(jnp.float32), totals[1] + held[source, 1].astype(jnp.float32))

    start_totals = (parts_ref[2 * slot].astype(jnp.float32), parts_ref[2 * slot + 1].astype(jnp.float32))
    first, second = lax.fori_loop(1, planes, finish, start_totals)
    theirs[...] = jnp.where(side == 0, second, first)
    cross = group_copy(theirs, mine, cross_sem.at[0], cross_sem.at[1], row, partner)
    cross.start()
    cross.wait_send()
    cross.wait_recv()
    out_ref[...] = jnp.where(side == 0, first, second) + mine[...]


def scatter_rows(parts):
    peers, rows, cols = parts.shape
    return pl.pallas_call(
        scatter_kernel,
        out_shape=jax.ShapeDtypeStruct((rows, cols), jnp.float32),
        in_specs=[pl.BlockSpec(memory_space=pltpu.VMEM)],
        out_specs=pl.BlockSpec(memory_space=pltpu.VMEM),
        scratch_shapes=[
            pltpu.VMEM((peers // 2, 2, rows, cols), parts.dtype),
            pltpu.VMEM((rows, cols), jnp.float32),
            pltpu.VMEM((rows, cols), jnp.float32),
            pltpu.SemaphoreType.DMA((peers // 2, 2)),
            pltpu.SemaphoreType.DMA((peers // 2, 2)),
            pltpu.SemaphoreType.DMA((2,)),
        ],
        compiler_params=pltpu.CompilerParams(collective_id=1, has_side_effects=True),
    )(parts)


def squash_into(pad_ref, activation):
    squashed = (activation / (1.0 + jnp.exp(-activation))).astype(jnp.bfloat16).astype(jnp.float32)
    field = squashed.reshape(pad_ref.shape[0] - 2, 8, 8, pad_ref.shape[-1])
    pad_ref[2:, 1:9, 1:9, :] = field
    pad_ref[0:2, 1:9, 1:9, :] = jnp.broadcast_to(field[0:1], (2,) + field.shape[1:])


def tap_window(pad_ref, tap, frames, base):
    offset_time, offset_row, offset_col = tap // 9, (tap // 3) % 3, tap % 3
    if base:
        t0, r0, c0 = 2 - offset_time, 2 - offset_row, 2 - offset_col
    else:
        t0, r0, c0 = offset_time, offset_row, offset_col
    window = pad_ref[t0 : t0 + frames, r0 : r0 + 8, c0 : c0 + 8, :]
    return window.reshape(frames * 64, window.shape[-1]).astype(jnp.bfloat16)


def greet_line(here, count, col):
    barrier = pltpu.get_barrier_semaphore()

    @pl.when(here > 0)
    def _():
        pl.semaphore_signal(barrier, inc=1, device_id=(here - 1, col), device_id_type=MESH_ID)

    @pl.when(here < count - 1)
    def _():
        pl.semaphore_signal(barrier, inc=1, device_id=(here + 1, col), device_id_type=MESH_ID)

    neighbours = (here + count - 1) // count + (2 * count - 2 - here) // count
    pl.semaphore_wait(barrier, neighbours)


def line_copy(src, dst, send_sem, recv_sem, target, col):
    return pltpu.make_async_remote_copy(
        src_ref=src,
        dst_ref=dst,
        send_sem=send_sem,
        recv_sem=recv_sem,
        device_id=(target, col),
        device_id_type=MESH_ID,
    )


def forward_kernel(clips_ref, w_ref, seen_ref, out_ref, recv, pad, send_sem, recv_sem):
    count = lax.axis_size("section")
    here = lax.axis_index("section")
    col = lax.axis_index("dp")
    micro_count = clips_ref.shape[0]
    greet_line(here, count, col)
    pad[...] = jnp.zeros_like(pad)

    def step(m, carry):
        @pl.when(here == 0)
        def _():
            seen_ref[m] = clips_ref[m]

        @pl.when(here > 0)
        def _():
            line_copy(out_ref.at[m], recv.at[m], send_sem.at[m], recv_sem.at[m], here - 1, col).wait_recv()
            seen_ref[m] = recv[m]

        base = seen_ref[m].astype(jnp.float32)
        squash_into(pad, base)
        total = base
        for tap in range(27):
            total = total + jnp.dot(tap_window(pad, tap, 4, False), w_ref[tap], preferred_element_type=jnp.float32)
        out_ref[m] = total.astype(out_ref.dtype)

        @pl.when(here < count - 1)
        def _():
            line_copy(out_ref.at[m], recv.at[m], send_sem.at[m], recv_sem.at[m], here + 1, col).start()

        return carry

    lax.fori_loop(0, micro_count, step, 0)

    @pl.when(here < count - 1)
    def _():
        for m in range(micro_count):
            line_copy(out_ref.at[m], recv.at[m], send_sem.at[m], recv_sem.at[m], here + 1, col).wait_send()


def forward_line(clips_local, weight):
    shape = jax.ShapeDtypeStruct(clips_local.shape, clips_local.dtype)
    micro_count, cells, channels = clips_local.shape
    return pl.pallas_call(
        forward_kernel,
        out_shape=(shape, shape),
        in_specs=[pl.BlockSpec(memory_space=pltpu.VMEM)] * 2,
        out_specs=(pl.BlockSpec(memory_space=pltpu.VMEM),) * 2,
        scratch_shapes=[
            pltpu.VMEM(clips_local.shape, clips_local.dtype),
            pltpu.VMEM((cells // 64 + 2, 10, 10, channels), jnp.float32),
            pltpu.SemaphoreType.DMA((micro_count,)),
            pltpu.SemaphoreType.DMA((micro_count,)),
        ],
        compiler_params=pltpu.CompilerParams(collective_id=2, has_side_effects=True),
    )(clips_local, weight)


def backward_kernel(cot_ref, seen_ref, w_ref, wg_ref, recv, sendbuf, pad, gpad, send_sem, recv_sem):
    count = lax.axis_size("section")
    here = lax.axis_index("section")
    col = lax.axis_index("dp")
    micro_count = cot_ref.shape[0]
    greet_line(here, count, col)
    pad[...] = jnp.zeros_like(pad)
    gpad[...] = jnp.zeros_like(gpad)
    wg_ref[...] = jnp.zeros_like(wg_ref)

    def step(m, carry):
        @pl.when(here == count - 1)
        def _():
            recv[m] = cot_ref[m]

        @pl.when(here < count - 1)
        def _():
            line_copy(sendbuf.at[m], recv.at[m], send_sem.at[m], recv_sem.at[m], here + 1, col).wait_recv()

        upstream = recv[m]
        base = seen_ref[m].astype(jnp.float32)
        squash_into(pad, base)
        @pl.when(here > 0)
        def _():
            up = upstream.astype(jnp.float32)
            gpad[2:6, 1:9, 1:9, :] = up.reshape(4, 8, 8, up.shape[-1])
            spread = jnp.zeros((384, up.shape[-1]), jnp.float32)
            for tap in range(27):
                spread = spread + jnp.dot(tap_window(gpad, tap, 6, True), w_ref[tap], preferred_element_type=jnp.float32)
            field = jnp.concatenate([spread[0:64] + spread[64:128] + spread[128:192], spread[192:384]], axis=0)
            sig = 1.0 / (1.0 + jnp.exp(-base))
            slope = sig * (1.0 + base * (1.0 - sig))
            sendbuf[m] = (up + field * slope).astype(sendbuf.dtype)
            line_copy(sendbuf.at[m], recv.at[m], send_sem.at[m], recv_sem.at[m], here - 1, col).start()

        upstream_t = upstream.T
        for tap in range(27):
            wg_ref[tap] += jnp.dot(upstream_t, tap_window(pad, tap, 4, False), preferred_element_type=jnp.float32)
        return carry

    lax.fori_loop(0, micro_count, step, 0)

    @pl.when(here > 0)
    def _():
        for m in range(micro_count):
            line_copy(sendbuf.at[m], recv.at[m], send_sem.at[m], recv_sem.at[m], here - 1, col).wait_send()


def backward_line(cot_local, seen, weight):
    micro_count, cells, channels = cot_local.shape
    taps = weight.shape[0]
    return pl.pallas_call(
        backward_kernel,
        out_shape=jax.ShapeDtypeStruct((taps, channels, channels), jnp.float32),
        in_specs=[pl.BlockSpec(memory_space=pltpu.VMEM)] * 3,
        out_specs=pl.BlockSpec(memory_space=pltpu.VMEM),
        scratch_shapes=[
            pltpu.VMEM(cot_local.shape, cot_local.dtype),
            pltpu.VMEM(cot_local.shape, cot_local.dtype),
            pltpu.VMEM((cells // 64 + 2, 10, 10, channels), jnp.float32),
            pltpu.VMEM((cells // 64 + 4, 10, 10, channels), jnp.float32),
            pltpu.SemaphoreType.DMA((micro_count,)),
            pltpu.SemaphoreType.DMA((micro_count,)),
        ],
        compiler_params=pltpu.CompilerParams(collective_id=3, has_side_effects=True),
    )(cot_local, seen, weight)


def per_device(clips, cotangent, weights):
    channels = weights.shape[-1]
    weight = gather_rows(weights[0]).reshape(-1, channels, channels)
    micro_count = clips.shape[0]
    clips_local = clips[:, 0].reshape(micro_count, -1, channels)
    cot_local = cotangent[:, 0].reshape(micro_count, -1, channels)
    seen, produced = forward_line(clips_local, weight)
    grad_t = backward_line(cot_local, seen, jnp.swapaxes(weight, 1, 2))
    grad_total = jnp.swapaxes(grad_t, 1, 2).astype(jnp.bfloat16)
    grad_share = scatter_rows(grad_total.reshape(lax.axis_size("dp"), -1, channels))
    return (produced.reshape(clips[:, 0].shape)[None, :, None], grad_share[None])


def solution(mesh):
    placed = (
        P(None, "dp", None, None, None, None),
        P(None, "dp", None, None, None, None),
        P("section", "dp", None),
    )
    return jax.shard_map(
        per_device,
        mesh=mesh,
        in_specs=placed,
        out_specs=(P("section", None, "dp", None, None, None, None), P("section", "dp", None)),
        check_vma=False,
    )
```

```python
import jax
import jax.numpy as jnp
from jax import lax
from jax.sharding import PartitionSpec as P

from jax.experimental import pallas as pl
from jax.experimental.pallas import tpu as pltpu

MESH_ID = pl.DeviceIdType.MESH


def greet_group(here, row):
    pair = here - here % 2
    partner = pair + 1 - here % 2
    barrier = pltpu.get_barrier_semaphore()
    pl.semaphore_signal(barrier, inc=1, device_id=(row, partner), device_id_type=MESH_ID)

    def signal(i, carry):
        peer = lax.rem(here + 2 * i, lax.axis_size("dp"))
        pl.semaphore_signal(barrier, inc=1, device_id=(row, peer), device_id_type=MESH_ID)
        return carry

    planes = lax.axis_size("dp") // 2
    lax.fori_loop(1, planes, signal, 0)
    pl.semaphore_wait(barrier, planes)
    return partner


def group_copy(src, dst, send_sem, recv_sem, row, peer):
    return pltpu.make_async_remote_copy(
        src_ref=src,
        dst_ref=dst,
        send_sem=send_sem,
        recv_sem=recv_sem,
        device_id=(row, peer),
        device_id_type=MESH_ID,
    )


def gather_kernel(shard_ref, out_ref, send_sem, recv_sem):
    peers = lax.axis_size("dp")
    here = lax.axis_index("dp")
    row = lax.axis_index("section")
    partner = greet_group(here, row)
    planes = peers // 2
    cross = group_copy(shard_ref, out_ref.at[here], send_sem.at[here], recv_sem.at[here], row, partner)
    cross.start()

    def fan(i, peer):
        own = group_copy(shard_ref, out_ref.at[here], send_sem.at[peer], recv_sem.at[here], row, peer)
        relayed = group_copy(out_ref.at[partner], out_ref.at[partner], send_sem.at[peer + 1 - 2 * (peer % 2)],
                             recv_sem.at[partner], row, peer)
        return own, relayed

    def start_own(i, carry):
        fan(i, lax.rem(here + 2 * i, peers))[0].start()
        return carry

    def start_relay(i, carry):
        fan(i, lax.rem(here + 2 * i, peers))[1].start()
        return carry

    lax.fori_loop(1, planes, start_own, 0)
    out_ref[here] = shard_ref[...]
    cross.wait_send()
    group_copy(shard_ref, out_ref.at[partner], send_sem.at[partner], recv_sem.at[partner], row, partner).wait_recv()
    lax.fori_loop(1, planes, start_relay, 0)

    def finish(i, carry):
        peer = lax.rem(here + 2 * i, peers)
        own, relayed = fan(i, peer)
        own.wait_send()
        relayed.wait_send()
        mate = peer + 1 - 2 * (peer % 2)
        group_copy(shard_ref, out_ref.at[peer], send_sem.at[peer], recv_sem.at[peer], row, peer).wait_recv()
        group_copy(shard_ref, out_ref.at[mate], send_sem.at[mate], recv_sem.at[mate], row, peer).wait_recv()
        return carry

    lax.fori_loop(1, planes, finish, 0)


def gather_rows(shard):
    peers = lax.axis_size("dp")
    rows, cols = shard.shape
    return pl.pallas_call(
        gather_kernel,
        out_shape=jax.ShapeDtypeStruct((peers, rows, cols), shard.dtype),
        in_specs=[pl.BlockSpec(memory_space=pltpu.VMEM)],
        out_specs=pl.BlockSpec(memory_space=pltpu.VMEM),
        scratch_shapes=[pltpu.SemaphoreType.DMA((peers,)), pltpu.SemaphoreType.DMA((peers,))],
        compiler_params=pltpu.CompilerParams(collective_id=0, has_side_effects=True),
    )(shard)


def scatter_kernel(parts_ref, out_ref, held, mine, theirs, send_sem, recv_sem, cross_sem):
    peers = lax.axis_size("dp")
    here = lax.axis_index("dp")
    row = lax.axis_index("section")
    partner = greet_group(here, row)
    planes = peers // 2
    slot = here // 2
    side = here % 2

    def fan(peer, block):
        return group_copy(parts_ref.at[2 * (peer // 2) + block], held.at[slot, block],
                          send_sem.at[peer // 2, block], recv_sem.at[slot, block], row, peer)

    def start(i, carry):
        peer = lax.rem(here + 2 * i, peers)
        fan(peer, 0).start()
        fan(peer, 1).start()
        return carry

    lax.fori_loop(1, planes, start, 0)

    def finish(i, totals):
        peer = lax.rem(here + 2 * i, peers)
        fan(peer, 0).wait_send()
        fan(peer, 1).wait_send()
        source = peer // 2
        for block in range(2):
            group_copy(parts_ref.at[block], held.at[source, block], send_sem.at[source, block],
                       recv_sem.at[source, block], row, peer).wait_recv()
        return (totals[0] + held[source, 0].astype(jnp.float32), totals[1] + held[source, 1].astype(jnp.float32))

    start_totals = (parts_ref[2 * slot].astype(jnp.float32), parts_ref[2 * slot + 1].astype(jnp.float32))
    first, second = lax.fori_loop(1, planes, finish, start_totals)
    theirs[...] = jnp.where(side == 0, second, first)
    cross = group_copy(theirs, mine, cross_sem.at[0], cross_sem.at[1], row, partner)
    cross.start()
    cross.wait_send()
    cross.wait_recv()
    out_ref[...] = jnp.where(side == 0, first, second) + mine[...]


def scatter_rows(parts):
    peers, rows, cols = parts.shape
    return pl.pallas_call(
        scatter_kernel,
        out_shape=jax.ShapeDtypeStruct((rows, cols), jnp.float32),
        in_specs=[pl.BlockSpec(memory_space=pltpu.VMEM)],
        out_specs=pl.BlockSpec(memory_space=pltpu.VMEM),
        scratch_shapes=[
            pltpu.VMEM((peers // 2, 2, rows, cols), parts.dtype),
            pltpu.VMEM((rows, cols), jnp.float32),
            pltpu.VMEM((rows, cols), jnp.float32),
            pltpu.SemaphoreType.DMA((peers // 2, 2)),
            pltpu.SemaphoreType.DMA((peers // 2, 2)),
            pltpu.SemaphoreType.DMA((2,)),
        ],
        compiler_params=pltpu.CompilerParams(collective_id=1, has_side_effects=True),
    )(parts)


def squash_into(pad_ref, activation):
    squashed = (activation / (1.0 + jnp.exp(-activation))).astype(jnp.bfloat16).astype(jnp.float32)
    field = squashed.reshape(pad_ref.shape[0] - 2, 8, 8, pad_ref.shape[-1])
    pad_ref[2:, 1:9, 1:9, :] = field
    pad_ref[0:2, 1:9, 1:9, :] = jnp.broadcast_to(field[0:1], (2,) + field.shape[1:])


def fill_columns(pad_ref, cols_ref, frames, flipped):
    channels = pad_ref.shape[-1]
    for c0 in range(3):
        shifted = pad_ref[:, :, c0 : c0 + 8, :]
        offset_col = 2 - c0 if flipped else c0
        for offset_time in range(3):
            for offset_row in range(3):
                t0 = 2 - offset_time if flipped else offset_time
                r0 = 2 - offset_row if flipped else offset_row
                tap = offset_time * 9 + offset_row * 3 + offset_col
                window = shifted[t0 : t0 + frames, r0 : r0 + 8].reshape(frames * 64, channels)
                cols_ref[:, tap * channels : (tap + 1) * channels] = window.astype(cols_ref.dtype)


def greet_line(here, count, col):
    barrier = pltpu.get_barrier_semaphore()

    @pl.when(here > 0)
    def _():
        pl.semaphore_signal(barrier, inc=1, device_id=(here - 1, col), device_id_type=MESH_ID)

    @pl.when(here < count - 1)
    def _():
        pl.semaphore_signal(barrier, inc=1, device_id=(here + 1, col), device_id_type=MESH_ID)

    neighbours = (here + count - 1) // count + (2 * count - 2 - here) // count
    pl.semaphore_wait(barrier, neighbours)


def line_copy(src, dst, send_sem, recv_sem, target, col):
    return pltpu.make_async_remote_copy(
        src_ref=src,
        dst_ref=dst,
        send_sem=send_sem,
        recv_sem=recv_sem,
        device_id=(target, col),
        device_id_type=MESH_ID,
    )


def forward_kernel(clips_ref, w_ref, seen_ref, out_ref, recv, pad, cols, send_sem, recv_sem):
    count = lax.axis_size("section")
    here = lax.axis_index("section")
    col = lax.axis_index("dp")
    micro_count = clips_ref.shape[0]
    greet_line(here, count, col)
    pad[...] = jnp.zeros_like(pad)

    def step(m, carry):
        @pl.when(here == 0)
        def _():
            seen_ref[m] = clips_ref[m]

        @pl.when(here > 0)
        def _():
            line_copy(out_ref.at[m], recv.at[m], send_sem.at[m], recv_sem.at[m], here - 1, col).wait_recv()
            seen_ref[m] = recv[m]

        base = seen_ref[m].astype(jnp.float32)
        squash_into(pad, base)
        fill_columns(pad, cols, 4, False)
        total = base + jnp.dot(cols[...], w_ref[...], preferred_element_type=jnp.float32)
        out_ref[m] = total.astype(out_ref.dtype)

        @pl.when(here < count - 1)
        def _():
            line_copy(out_ref.at[m], recv.at[m], send_sem.at[m], recv_sem.at[m], here + 1, col).start()

        return carry

    lax.fori_loop(0, micro_count, step, 0)

    @pl.when(here < count - 1)
    def _():
        for m in range(micro_count):
            line_copy(out_ref.at[m], recv.at[m], send_sem.at[m], recv_sem.at[m], here + 1, col).wait_send()


def forward_line(clips_local, weight):
    shape = jax.ShapeDtypeStruct(clips_local.shape, clips_local.dtype)
    micro_count, cells, channels = clips_local.shape
    return pl.pallas_call(
        forward_kernel,
        out_shape=(shape, shape),
        in_specs=[pl.BlockSpec(memory_space=pltpu.VMEM)] * 2,
        out_specs=(pl.BlockSpec(memory_space=pltpu.VMEM),) * 2,
        scratch_shapes=[
            pltpu.VMEM(clips_local.shape, clips_local.dtype),
            pltpu.VMEM((cells // 64 + 2, 10, 10, channels), jnp.float32),
            pltpu.VMEM((cells, weight.shape[0]), jnp.bfloat16),
            pltpu.SemaphoreType.DMA((micro_count,)),
            pltpu.SemaphoreType.DMA((micro_count,)),
        ],
        compiler_params=pltpu.CompilerParams(collective_id=2, has_side_effects=True),
    )(clips_local, weight)


def backward_kernel(cot_ref, seen_ref, w_ref, wg_ref, recv, sendbuf, pad, gpad, cols, gcols, send_sem, recv_sem):
    count = lax.axis_size("section")
    here = lax.axis_index("section")
    col = lax.axis_index("dp")
    micro_count = cot_ref.shape[0]
    greet_line(here, count, col)
    pad[...] = jnp.zeros_like(pad)
    gpad[...] = jnp.zeros_like(gpad)
    wg_ref[...] = jnp.zeros_like(wg_ref)

    def step(m, carry):
        @pl.when(here == count - 1)
        def _():
            recv[m] = cot_ref[m]

        @pl.when(here < count - 1)
        def _():
            line_copy(sendbuf.at[m], recv.at[m], send_sem.at[m], recv_sem.at[m], here + 1, col).wait_recv()

        upstream = recv[m]
        base = seen_ref[m].astype(jnp.float32)
        squash_into(pad, base)
        @pl.when(here > 0)
        def _():
            up = upstream.astype(jnp.float32)
            gpad[2:6, 1:9, 1:9, :] = up.reshape(4, 8, 8, up.shape[-1])
            fill_columns(gpad, gcols, 6, True)
            spread = jnp.dot(gcols[...], w_ref[...], preferred_element_type=jnp.float32)
            field = jnp.concatenate([spread[0:64] + spread[64:128] + spread[128:192], spread[192:384]], axis=0)
            sig = 1.0 / (1.0 + jnp.exp(-base))
            slope = sig * (1.0 + base * (1.0 - sig))
            sendbuf[m] = (up + field * slope).astype(sendbuf.dtype)
            line_copy(sendbuf.at[m], recv.at[m], send_sem.at[m], recv_sem.at[m], here - 1, col).start()

        fill_columns(pad, cols, 4, False)
        wg_ref[...] += jnp.dot(upstream.T, cols[...], preferred_element_type=jnp.float32)
        return carry

    lax.fori_loop(0, micro_count, step, 0)

    @pl.when(here > 0)
    def _():
        for m in range(micro_count):
            line_copy(sendbuf.at[m], recv.at[m], send_sem.at[m], recv_sem.at[m], here - 1, col).wait_send()


def backward_line(cot_local, seen, weight):
    micro_count, cells, channels = cot_local.shape
    rows = weight.shape[0]
    return pl.pallas_call(
        backward_kernel,
        out_shape=jax.ShapeDtypeStruct((channels, rows), jnp.float32),
        in_specs=[pl.BlockSpec(memory_space=pltpu.VMEM)] * 3,
        out_specs=pl.BlockSpec(memory_space=pltpu.VMEM),
        scratch_shapes=[
            pltpu.VMEM(cot_local.shape, cot_local.dtype),
            pltpu.VMEM(cot_local.shape, cot_local.dtype),
            pltpu.VMEM((cells // 64 + 2, 10, 10, channels), jnp.float32),
            pltpu.VMEM((cells // 64 + 4, 10, 10, channels), jnp.float32),
            pltpu.VMEM((cells, rows), jnp.bfloat16),
            pltpu.VMEM((cells * 3 // 2, rows), jnp.bfloat16),
            pltpu.SemaphoreType.DMA((micro_count,)),
            pltpu.SemaphoreType.DMA((micro_count,)),
        ],
        compiler_params=pltpu.CompilerParams(collective_id=3, has_side_effects=True),
    )(cot_local, seen, weight)


def per_device(clips, cotangent, weights):
    channels = weights.shape[-1]
    weight = gather_rows(weights[0]).reshape(-1, channels)
    taps = weight.shape[0] // channels
    micro_count = clips.shape[0]
    clips_local = clips[:, 0].reshape(micro_count, -1, channels)
    cot_local = cotangent[:, 0].reshape(micro_count, -1, channels)
    seen, produced = forward_line(clips_local, weight)
    weight_t = jnp.swapaxes(weight.reshape(taps, channels, channels), 1, 2).reshape(-1, channels)
    grad_t = backward_line(cot_local, seen, weight_t)
    grad_total = grad_t.T.astype(jnp.bfloat16)
    grad_share = scatter_rows(grad_total.reshape(lax.axis_size("dp"), -1, channels))
    return (produced.reshape(clips[:, 0].shape)[None, :, None], grad_share[None])


def solution(mesh):
    placed = (
        P(None, "dp", None, None, None, None),
        P(None, "dp", None, None, None, None),
        P("section", "dp", None),
    )
    return jax.shard_map(
        per_device,
        mesh=mesh,
        in_specs=placed,
        out_specs=(P("section", None, "dp", None, None, None, None), P("section", "dp", None)),
        check_vma=False,
    )
```

```python
import jax
import jax.numpy as jnp
from jax import lax
from jax.sharding import PartitionSpec as P

from jax.experimental import pallas as pl
from jax.experimental.pallas import tpu as pltpu

MESH_ID = pl.DeviceIdType.MESH


def greet_group(here, row):
    pair = here - here % 2
    partner = pair + 1 - here % 2
    barrier = pltpu.get_barrier_semaphore()
    pl.semaphore_signal(barrier, inc=1, device_id=(row, partner), device_id_type=MESH_ID)

    def signal(i, carry):
        peer = lax.rem(here + 2 * i, lax.axis_size("dp"))
        pl.semaphore_signal(barrier, inc=1, device_id=(row, peer), device_id_type=MESH_ID)
        return carry

    planes = lax.axis_size("dp") // 2
    lax.fori_loop(1, planes, signal, 0)
    pl.semaphore_wait(barrier, planes)
    return partner


def group_copy(src, dst, send_sem, recv_sem, row, peer):
    return pltpu.make_async_remote_copy(
        src_ref=src,
        dst_ref=dst,
        send_sem=send_sem,
        recv_sem=recv_sem,
        device_id=(row, peer),
        device_id_type=MESH_ID,
    )


def gather_kernel(shard_ref, out_ref, send_sem, recv_sem):
    peers = lax.axis_size("dp")
    here = lax.axis_index("dp")
    row = lax.axis_index("section")
    partner = greet_group(here, row)
    planes = peers // 2
    cross = group_copy(shard_ref, out_ref.at[here], send_sem.at[here], recv_sem.at[here], row, partner)
    cross.start()

    def fan(i, peer):
        own = group_copy(shard_ref, out_ref.at[here], send_sem.at[peer], recv_sem.at[here], row, peer)
        relayed = group_copy(out_ref.at[partner], out_ref.at[partner], send_sem.at[peer + 1 - 2 * (peer % 2)],
                             recv_sem.at[partner], row, peer)
        return own, relayed

    def start_own(i, carry):
        fan(i, lax.rem(here + 2 * i, peers))[0].start()
        return carry

    def start_relay(i, carry):
        fan(i, lax.rem(here + 2 * i, peers))[1].start()
        return carry

    lax.fori_loop(1, planes, start_own, 0)
    out_ref[here] = shard_ref[...]
    cross.wait_send()
    group_copy(shard_ref, out_ref.at[partner], send_sem.at[partner], recv_sem.at[partner], row, partner).wait_recv()
    lax.fori_loop(1, planes, start_relay, 0)

    def finish(i, carry):
        peer = lax.rem(here + 2 * i, peers)
        own, relayed = fan(i, peer)
        own.wait_send()
        relayed.wait_send()
        mate = peer + 1 - 2 * (peer % 2)
        group_copy(shard_ref, out_ref.at[peer], send_sem.at[peer], recv_sem.at[peer], row, peer).wait_recv()
        group_copy(shard_ref, out_ref.at[mate], send_sem.at[mate], recv_sem.at[mate], row, peer).wait_recv()
        return carry

    lax.fori_loop(1, planes, finish, 0)


def gather_rows(shard):
    peers = lax.axis_size("dp")
    rows, cols = shard.shape
    return pl.pallas_call(
        gather_kernel,
        out_shape=jax.ShapeDtypeStruct((peers, rows, cols), shard.dtype),
        in_specs=[pl.BlockSpec(memory_space=pltpu.VMEM)],
        out_specs=pl.BlockSpec(memory_space=pltpu.VMEM),
        scratch_shapes=[pltpu.SemaphoreType.DMA((peers,)), pltpu.SemaphoreType.DMA((peers,))],
        compiler_params=pltpu.CompilerParams(collective_id=0, has_side_effects=True),
    )(shard)


def scatter_kernel(parts_ref, out_ref, held, mine, theirs, send_sem, recv_sem, cross_sem):
    peers = lax.axis_size("dp")
    here = lax.axis_index("dp")
    row = lax.axis_index("section")
    partner = greet_group(here, row)
    planes = peers // 2
    slot = here // 2
    side = here % 2

    def fan(peer, block):
        return group_copy(parts_ref.at[2 * (peer // 2) + block], held.at[slot, block],
                          send_sem.at[peer // 2, block], recv_sem.at[slot, block], row, peer)

    def start(i, carry):
        peer = lax.rem(here + 2 * i, peers)
        fan(peer, 0).start()
        fan(peer, 1).start()
        return carry

    lax.fori_loop(1, planes, start, 0)

    def finish(i, totals):
        peer = lax.rem(here + 2 * i, peers)
        fan(peer, 0).wait_send()
        fan(peer, 1).wait_send()
        source = peer // 2
        for block in range(2):
            group_copy(parts_ref.at[block], held.at[source, block], send_sem.at[source, block],
                       recv_sem.at[source, block], row, peer).wait_recv()
        return (totals[0] + held[source, 0].astype(jnp.float32), totals[1] + held[source, 1].astype(jnp.float32))

    start_totals = (parts_ref[2 * slot].astype(jnp.float32), parts_ref[2 * slot + 1].astype(jnp.float32))
    first, second = lax.fori_loop(1, planes, finish, start_totals)
    theirs[...] = jnp.where(side == 0, second, first)
    cross = group_copy(theirs, mine, cross_sem.at[0], cross_sem.at[1], row, partner)
    cross.start()
    cross.wait_send()
    cross.wait_recv()
    out_ref[...] = jnp.where(side == 0, first, second) + mine[...]


def scatter_rows(parts):
    peers, rows, cols = parts.shape
    return pl.pallas_call(
        scatter_kernel,
        out_shape=jax.ShapeDtypeStruct((rows, cols), jnp.float32),
        in_specs=[pl.BlockSpec(memory_space=pltpu.VMEM)],
        out_specs=pl.BlockSpec(memory_space=pltpu.VMEM),
        scratch_shapes=[
            pltpu.VMEM((peers // 2, 2, rows, cols), parts.dtype),
            pltpu.VMEM((rows, cols), jnp.float32),
            pltpu.VMEM((rows, cols), jnp.float32),
            pltpu.SemaphoreType.DMA((peers // 2, 2)),
            pltpu.SemaphoreType.DMA((peers // 2, 2)),
            pltpu.SemaphoreType.DMA((2,)),
        ],
        compiler_params=pltpu.CompilerParams(collective_id=1, has_side_effects=True),
    )(parts)


def squash_into(pad_ref, activation):
    squashed = (activation / (1.0 + jnp.exp(-activation))).astype(jnp.bfloat16).astype(jnp.float32)
    field = squashed.reshape(pad_ref.shape[0] - 2, 8, 8, pad_ref.shape[-1])
    pad_ref[2:, 1:9, 1:9, :] = field
    pad_ref[0:2, 1:9, 1:9, :] = jnp.broadcast_to(field[0:1], (2,) + field.shape[1:])


def tap_windows(pad_ref, frames, flipped):
    channels = pad_ref.shape[-1]
    for c0 in range(3):
        shifted = pad_ref[:, :, c0 : c0 + 8, :]
        offset_col = 2 - c0 if flipped else c0
        for offset_time in range(3):
            for offset_row in range(3):
                t0 = 2 - offset_time if flipped else offset_time
                r0 = 2 - offset_row if flipped else offset_row
                window = shifted[t0 : t0 + frames, r0 : r0 + 8].reshape(frames * 64, channels)
                yield offset_time * 9 + offset_row * 3 + offset_col, window.astype(jnp.bfloat16)


def greet_line(here, count, col):
    barrier = pltpu.get_barrier_semaphore()

    @pl.when(here > 0)
    def _():
        pl.semaphore_signal(barrier, inc=1, device_id=(here - 1, col), device_id_type=MESH_ID)

    @pl.when(here < count - 1)
    def _():
        pl.semaphore_signal(barrier, inc=1, device_id=(here + 1, col), device_id_type=MESH_ID)

    neighbours = (here + count - 1) // count + (2 * count - 2 - here) // count
    pl.semaphore_wait(barrier, neighbours)


def line_copy(src, dst, send_sem, recv_sem, target, col):
    return pltpu.make_async_remote_copy(
        src_ref=src,
        dst_ref=dst,
        send_sem=send_sem,
        recv_sem=recv_sem,
        device_id=(target, col),
        device_id_type=MESH_ID,
    )


def forward_kernel(clips_ref, w_ref, seen_ref, out_ref, recv, pad, send_sem, recv_sem):
    count = lax.axis_size("section")
    here = lax.axis_index("section")
    col = lax.axis_index("dp")
    micro_count = clips_ref.shape[0]
    greet_line(here, count, col)
    pad[...] = jnp.zeros_like(pad)

    def step(m, carry):
        @pl.when(here == 0)
        def _():
            seen_ref[m] = clips_ref[m]

        @pl.when(here > 0)
        def _():
            line_copy(out_ref.at[m], recv.at[m], send_sem.at[m], recv_sem.at[m], here - 1, col).wait_recv()
            seen_ref[m] = recv[m]

        base = seen_ref[m].astype(jnp.float32)
        squash_into(pad, base)
        total = base
        for tap, window in tap_windows(pad, 4, False):
            total = total + jnp.dot(window, w_ref[tap], preferred_element_type=jnp.float32)
        out_ref[m] = total.astype(out_ref.dtype)

        @pl.when(here < count - 1)
        def _():
            line_copy(out_ref.at[m], recv.at[m], send_sem.at[m], recv_sem.at[m], here + 1, col).start()

        return carry

    lax.fori_loop(0, micro_count, step, 0)

    @pl.when(here < count - 1)
    def _():
        for m in range(micro_count):
            line_copy(out_ref.at[m], recv.at[m], send_sem.at[m], recv_sem.at[m], here + 1, col).wait_send()


def forward_line(clips_local, weight):
    shape = jax.ShapeDtypeStruct(clips_local.shape, clips_local.dtype)
    micro_count, cells, channels = clips_local.shape
    return pl.pallas_call(
        forward_kernel,
        out_shape=(shape, shape),
        in_specs=[pl.BlockSpec(memory_space=pltpu.VMEM)] * 2,
        out_specs=(pl.BlockSpec(memory_space=pltpu.VMEM),) * 2,
        scratch_shapes=[
            pltpu.VMEM(clips_local.shape, clips_local.dtype),
            pltpu.VMEM((cells // 64 + 2, 10, 10, channels), jnp.float32),
            pltpu.SemaphoreType.DMA((micro_count,)),
            pltpu.SemaphoreType.DMA((micro_count,)),
        ],
        compiler_params=pltpu.CompilerParams(collective_id=2, has_side_effects=True),
    )(clips_local, weight)


def backward_kernel(cot_ref, seen_ref, w_ref, wg_ref, recv, sendbuf, pad, gpad, send_sem, recv_sem):
    count = lax.axis_size("section")
    here = lax.axis_index("section")
    col = lax.axis_index("dp")
    micro_count = cot_ref.shape[0]
    greet_line(here, count, col)
    pad[...] = jnp.zeros_like(pad)
    gpad[...] = jnp.zeros_like(gpad)
    wg_ref[...] = jnp.zeros_like(wg_ref)

    def step(m, carry):
        @pl.when(here == count - 1)
        def _():
            recv[m] = cot_ref[m]

        @pl.when(here < count - 1)
        def _():
            line_copy(sendbuf.at[m], recv.at[m], send_sem.at[m], recv_sem.at[m], here + 1, col).wait_recv()

        upstream = recv[m]
        base = seen_ref[m].astype(jnp.float32)
        squash_into(pad, base)
        @pl.when(here > 0)
        def _():
            up = upstream.astype(jnp.float32)
            gpad[2:6, 1:9, 1:9, :] = up.reshape(4, 8, 8, up.shape[-1])
            spread = jnp.zeros((384, up.shape[-1]), jnp.float32)
            for tap, window in tap_windows(gpad, 6, True):
                spread = spread + lax.dot_general(
                    window, w_ref[tap], (((1,), (1,)), ((), ())),
                    preferred_element_type=jnp.float32,
                )
            field = jnp.concatenate([spread[0:64] + spread[64:128] + spread[128:192], spread[192:384]], axis=0)
            sig = 1.0 / (1.0 + jnp.exp(-base))
            slope = sig * (1.0 + base * (1.0 - sig))
            sendbuf[m] = (up + field * slope).astype(sendbuf.dtype)
            line_copy(sendbuf.at[m], recv.at[m], send_sem.at[m], recv_sem.at[m], here - 1, col).start()

        for tap, window in tap_windows(pad, 4, False):
            wg_ref[tap] += lax.dot_general(
                window, upstream, (((0,), (0,)), ((), ())),
                preferred_element_type=jnp.float32,
            )
        return carry

    lax.fori_loop(0, micro_count, step, 0)

    @pl.when(here > 0)
    def _():
        for m in range(micro_count):
            line_copy(sendbuf.at[m], recv.at[m], send_sem.at[m], recv_sem.at[m], here - 1, col).wait_send()


def backward_line(cot_local, seen, weight):
    micro_count, cells, channels = cot_local.shape
    taps = weight.shape[0]
    return pl.pallas_call(
        backward_kernel,
        out_shape=jax.ShapeDtypeStruct((taps, channels, channels), jnp.float32),
        in_specs=[pl.BlockSpec(memory_space=pltpu.VMEM)] * 3,
        out_specs=pl.BlockSpec(memory_space=pltpu.VMEM),
        scratch_shapes=[
            pltpu.VMEM(cot_local.shape, cot_local.dtype),
            pltpu.VMEM(cot_local.shape, cot_local.dtype),
            pltpu.VMEM((cells // 64 + 2, 10, 10, channels), jnp.float32),
            pltpu.VMEM((cells // 64 + 4, 10, 10, channels), jnp.float32),
            pltpu.SemaphoreType.DMA((micro_count,)),
            pltpu.SemaphoreType.DMA((micro_count,)),
        ],
        compiler_params=pltpu.CompilerParams(collective_id=3, has_side_effects=True),
    )(cot_local, seen, weight)


def per_device(clips, cotangent, weights):
    channels = weights.shape[-1]
    weight = gather_rows(weights[0]).reshape(-1, channels, channels)
    micro_count = clips.shape[0]
    clips_local = clips[:, 0].reshape(micro_count, -1, channels)
    cot_local = cotangent[:, 0].reshape(micro_count, -1, channels)
    seen, produced = forward_line(clips_local, weight)
    grad_total = backward_line(cot_local, seen, weight)
    grad_share = scatter_rows(grad_total.astype(jnp.bfloat16).reshape(lax.axis_size("dp"), -1, channels))
    return (produced.reshape(clips[:, 0].shape)[None, :, None], grad_share[None])


def solution(mesh):
    placed = (
        P(None, "dp", None, None, None, None),
        P(None, "dp", None, None, None, None),
        P("section", "dp", None),
    )
    return jax.shard_map(
        per_device,
        mesh=mesh,
        in_specs=placed,
        out_specs=(P("section", None, "dp", None, None, None, None), P("section", "dp", None)),
        check_vma=False,
    )
```

```python
import jax
import jax.numpy as jnp
from jax import lax
from jax.sharding import PartitionSpec as P

from jax.experimental import pallas as pl
from jax.experimental.pallas import tpu as pltpu

MESH_ID = pl.DeviceIdType.MESH


def greet_group(here, row):
    pair = here - here % 2
    partner = pair + 1 - here % 2
    barrier = pltpu.get_barrier_semaphore()
    pl.semaphore_signal(barrier, inc=1, device_id=(row, partner), device_id_type=MESH_ID)

    def signal(i, carry):
        peer = lax.rem(here + 2 * i, lax.axis_size("dp"))
        pl.semaphore_signal(barrier, inc=1, device_id=(row, peer), device_id_type=MESH_ID)
        return carry

    planes = lax.axis_size("dp") // 2
    lax.fori_loop(1, planes, signal, 0)
    pl.semaphore_wait(barrier, planes)
    return partner


def group_copy(src, dst, send_sem, recv_sem, row, peer):
    return pltpu.make_async_remote_copy(
        src_ref=src,
        dst_ref=dst,
        send_sem=send_sem,
        recv_sem=recv_sem,
        device_id=(row, peer),
        device_id_type=MESH_ID,
    )


def gather_kernel(shard_ref, out_ref, send_sem, recv_sem):
    peers = lax.axis_size("dp")
    here = lax.axis_index("dp")
    row = lax.axis_index("section")
    partner = greet_group(here, row)
    planes = peers // 2
    cross = group_copy(shard_ref, out_ref.at[here], send_sem.at[here], recv_sem.at[here], row, partner)
    cross.start()

    def fan(i, peer):
        own = group_copy(shard_ref, out_ref.at[here], send_sem.at[peer], recv_sem.at[here], row, peer)
        relayed = group_copy(out_ref.at[partner], out_ref.at[partner], send_sem.at[peer + 1 - 2 * (peer % 2)],
                             recv_sem.at[partner], row, peer)
        return own, relayed

    def start_own(i, carry):
        fan(i, lax.rem(here + 2 * i, peers))[0].start()
        return carry

    def start_relay(i, carry):
        fan(i, lax.rem(here + 2 * i, peers))[1].start()
        return carry

    lax.fori_loop(1, planes, start_own, 0)
    out_ref[here] = shard_ref[...]
    cross.wait_send()
    group_copy(shard_ref, out_ref.at[partner], send_sem.at[partner], recv_sem.at[partner], row, partner).wait_recv()
    lax.fori_loop(1, planes, start_relay, 0)

    def finish(i, carry):
        peer = lax.rem(here + 2 * i, peers)
        own, relayed = fan(i, peer)
        own.wait_send()
        relayed.wait_send()
        mate = peer + 1 - 2 * (peer % 2)
        group_copy(shard_ref, out_ref.at[peer], send_sem.at[peer], recv_sem.at[peer], row, peer).wait_recv()
        group_copy(shard_ref, out_ref.at[mate], send_sem.at[mate], recv_sem.at[mate], row, peer).wait_recv()
        return carry

    lax.fori_loop(1, planes, finish, 0)


def gather_rows(shard):
    peers = lax.axis_size("dp")
    rows, cols = shard.shape
    return pl.pallas_call(
        gather_kernel,
        out_shape=jax.ShapeDtypeStruct((peers, rows, cols), shard.dtype),
        in_specs=[pl.BlockSpec(memory_space=pltpu.VMEM)],
        out_specs=pl.BlockSpec(memory_space=pltpu.VMEM),
        scratch_shapes=[pltpu.SemaphoreType.DMA((peers,)), pltpu.SemaphoreType.DMA((peers,))],
        compiler_params=pltpu.CompilerParams(collective_id=0, has_side_effects=True),
    )(shard)


def scatter_kernel(parts_ref, out_ref, held, mine, theirs, send_sem, recv_sem, cross_sem):
    peers = lax.axis_size("dp")
    here = lax.axis_index("dp")
    row = lax.axis_index("section")
    partner = greet_group(here, row)
    planes = peers // 2
    slot = here // 2
    side = here % 2

    def fan(peer, block):
        return group_copy(parts_ref.at[2 * (peer // 2) + block], held.at[slot, block],
                          send_sem.at[peer // 2, block], recv_sem.at[slot, block], row, peer)

    def start(i, carry):
        peer = lax.rem(here + 2 * i, peers)
        fan(peer, 0).start()
        fan(peer, 1).start()
        return carry

    lax.fori_loop(1, planes, start, 0)

    def finish(i, totals):
        peer = lax.rem(here + 2 * i, peers)
        fan(peer, 0).wait_send()
        fan(peer, 1).wait_send()
        source = peer // 2
        for block in range(2):
            group_copy(parts_ref.at[block], held.at[source, block], send_sem.at[source, block],
                       recv_sem.at[source, block], row, peer).wait_recv()
        return (totals[0] + held[source, 0].astype(jnp.float32), totals[1] + held[source, 1].astype(jnp.float32))

    start_totals = (parts_ref[2 * slot].astype(jnp.float32), parts_ref[2 * slot + 1].astype(jnp.float32))
    first, second = lax.fori_loop(1, planes, finish, start_totals)
    theirs[...] = jnp.where(side == 0, second, first)
    cross = group_copy(theirs, mine, cross_sem.at[0], cross_sem.at[1], row, partner)
    cross.start()
    cross.wait_send()
    cross.wait_recv()
    out_ref[...] = jnp.where(side == 0, first, second) + mine[...]


def scatter_rows(parts):
    peers, rows, cols = parts.shape
    return pl.pallas_call(
        scatter_kernel,
        out_shape=jax.ShapeDtypeStruct((rows, cols), jnp.float32),
        in_specs=[pl.BlockSpec(memory_space=pltpu.VMEM)],
        out_specs=pl.BlockSpec(memory_space=pltpu.VMEM),
        scratch_shapes=[
            pltpu.VMEM((peers // 2, 2, rows, cols), parts.dtype),
            pltpu.VMEM((rows, cols), jnp.float32),
            pltpu.VMEM((rows, cols), jnp.float32),
            pltpu.SemaphoreType.DMA((peers // 2, 2)),
            pltpu.SemaphoreType.DMA((peers // 2, 2)),
            pltpu.SemaphoreType.DMA((2,)),
        ],
        compiler_params=pltpu.CompilerParams(collective_id=1, has_side_effects=True),
    )(parts)


def squash_into(pad_ref, activation):
    squashed = (activation / (1.0 + jnp.exp(-activation))).astype(jnp.bfloat16).astype(jnp.float32)
    field = squashed.reshape(pad_ref.shape[0] - 2, 8, 8, pad_ref.shape[-1])
    pad_ref[2:, 1:9, 1:9, :] = field
    pad_ref[0:2, 1:9, 1:9, :] = jnp.broadcast_to(field[0:1], (2,) + field.shape[1:])


def tap_windows(pad_ref, frames, flipped, start=0):
    channels = pad_ref.shape[-1]
    for c0 in range(3):
        shifted = pad_ref[:, :, c0 : c0 + 8, :]
        offset_col = 2 - c0 if flipped else c0
        for offset_time in range(3):
            for offset_row in range(3):
                t0 = 2 - offset_time if flipped else offset_time
                r0 = 2 - offset_row if flipped else offset_row
                window = shifted[start + t0 : start + t0 + frames, r0 : r0 + 8].reshape(frames * 64, channels)
                yield offset_time * 9 + offset_row * 3 + offset_col, window.astype(jnp.bfloat16)


def greet_line(here, count, col):
    barrier = pltpu.get_barrier_semaphore()

    @pl.when(here > 0)
    def _():
        pl.semaphore_signal(barrier, inc=1, device_id=(here - 1, col), device_id_type=MESH_ID)

    @pl.when(here < count - 1)
    def _():
        pl.semaphore_signal(barrier, inc=1, device_id=(here + 1, col), device_id_type=MESH_ID)

    neighbours = (here + count - 1) // count + (2 * count - 2 - here) // count
    pl.semaphore_wait(barrier, neighbours)


def line_copy(src, dst, send_sem, recv_sem, target, col):
    return pltpu.make_async_remote_copy(
        src_ref=src,
        dst_ref=dst,
        send_sem=send_sem,
        recv_sem=recv_sem,
        device_id=(target, col),
        device_id_type=MESH_ID,
    )


def forward_kernel(clips_ref, w_ref, seen_ref, out_ref, recv, pad, send_sem, recv_sem):
    count = lax.axis_size("section")
    here = lax.axis_index("section")
    col = lax.axis_index("dp")
    micro_count, cells, channels = clips_ref.shape
    half = cells // 2
    greet_line(here, count, col)
    pad[...] = jnp.zeros_like(pad)

    def hop(m, part, target):
        rows = pl.ds(part * half, half)
        return line_copy(out_ref.at[m, rows], recv.at[m, rows], send_sem.at[m, part], recv_sem.at[m, part], target, col)

    def step(m, carry):
        for part in range(2):
            rows = pl.ds(part * half, half)

            @pl.when(here == 0)
            def _():
                seen_ref[m, rows] = clips_ref[m, rows]

            @pl.when(here > 0)
            def _():
                hop(m, part, here - 1).wait_recv()
                seen_ref[m, rows] = recv[m, rows]

            base = seen_ref[m, rows].astype(jnp.float32)
            squashed = (base / (1.0 + jnp.exp(-base))).astype(jnp.bfloat16).astype(jnp.float32)
            field = squashed.reshape(2, 8, 8, channels)
            pad[2 + 2 * part : 4 + 2 * part, 1:9, 1:9, :] = field
            if part == 0:
                pad[0:2, 1:9, 1:9, :] = jnp.broadcast_to(field[0:1], field.shape)
            total = base
            for tap, window in tap_windows(pad, 2, False, 2 * part):
                total = total + jnp.dot(window, w_ref[tap], preferred_element_type=jnp.float32)
            out_ref[m, rows] = total.astype(out_ref.dtype)

            @pl.when(here < count - 1)
            def _():
                hop(m, part, here + 1).start()

        return carry

    lax.fori_loop(0, micro_count, step, 0)

    @pl.when(here < count - 1)
    def _():
        for m in range(micro_count):
            for part in range(2):
                hop(m, part, here + 1).wait_send()


def forward_line(clips_local, weight):
    shape = jax.ShapeDtypeStruct(clips_local.shape, clips_local.dtype)
    micro_count, cells, channels = clips_local.shape
    return pl.pallas_call(
        forward_kernel,
        out_shape=(shape, shape),
        in_specs=[pl.BlockSpec(memory_space=pltpu.VMEM)] * 2,
        out_specs=(pl.BlockSpec(memory_space=pltpu.VMEM),) * 2,
        scratch_shapes=[
            pltpu.VMEM(clips_local.shape, clips_local.dtype),
            pltpu.VMEM((cells // 64 + 2, 10, 10, channels), jnp.float32),
            pltpu.SemaphoreType.DMA((micro_count, 2)),
            pltpu.SemaphoreType.DMA((micro_count, 2)),
        ],
        compiler_params=pltpu.CompilerParams(collective_id=2, has_side_effects=True),
    )(clips_local, weight)


def backward_kernel(cot_ref, seen_ref, w_ref, wg_ref, recv, sendbuf, pad, gpad, send_sem, recv_sem):
    count = lax.axis_size("section")
    here = lax.axis_index("section")
    col = lax.axis_index("dp")
    micro_count, cells, channels = cot_ref.shape
    half = cells // 2
    greet_line(here, count, col)
    pad[...] = jnp.zeros_like(pad)
    gpad[...] = jnp.zeros_like(gpad)
    wg_ref[...] = jnp.zeros_like(wg_ref)

    def hop(m, part, target):
        rows = pl.ds(part * half, half)
        return line_copy(sendbuf.at[m, rows], recv.at[m, rows], send_sem.at[m, part], recv_sem.at[m, part], target, col)

    def step(m, carry):
        for part in (1, 0):
            rows = pl.ds(part * half, half)

            @pl.when(here == count - 1)
            def _():
                recv[m, rows] = cot_ref[m, rows]

            @pl.when(here < count - 1)
            def _():
                hop(m, part, here + 1).wait_recv()

            @pl.when(here > 0)
            def _():
                up = recv[m, rows].astype(jnp.float32)
                gpad[2 + 2 * part : 4 + 2 * part, 1:9, 1:9, :] = up.reshape(2, 8, 8, channels)
                frames = 2 if part else 4
                spread = jnp.zeros((frames * 64, channels), jnp.float32)
                for tap, window in tap_windows(gpad, frames, True, 4 if part else 0):
                    spread = spread + lax.dot_general(
                        window, w_ref[tap], (((1,), (1,)), ((), ())),
                        preferred_element_type=jnp.float32,
                    )
                if part:
                    field = spread
                else:
                    field = jnp.concatenate([spread[0:64] + spread[64:128] + spread[128:192], spread[192:256]], axis=0)
                base = seen_ref[m, rows].astype(jnp.float32)
                sig = 1.0 / (1.0 + jnp.exp(-base))
                slope = sig * (1.0 + base * (1.0 - sig))
                sendbuf[m, rows] = (up + field * slope).astype(sendbuf.dtype)
                hop(m, part, here - 1).start()

        upstream = recv[m]
        squash_into(pad, seen_ref[m].astype(jnp.float32))
        for tap, window in tap_windows(pad, 4, False):
            wg_ref[tap] += lax.dot_general(
                window, upstream, (((0,), (0,)), ((), ())),
                preferred_element_type=jnp.float32,
            )
        return carry

    lax.fori_loop(0, micro_count, step, 0)

    @pl.when(here > 0)
    def _():
        for m in range(micro_count):
            for part in range(2):
                hop(m, part, here - 1).wait_send()


def backward_line(cot_local, seen, weight):
    micro_count, cells, channels = cot_local.shape
    taps = weight.shape[0]
    return pl.pallas_call(
        backward_kernel,
        out_shape=jax.ShapeDtypeStruct((taps, channels, channels), jnp.float32),
        in_specs=[pl.BlockSpec(memory_space=pltpu.VMEM)] * 3,
        out_specs=pl.BlockSpec(memory_space=pltpu.VMEM),
        scratch_shapes=[
            pltpu.VMEM(cot_local.shape, cot_local.dtype),
            pltpu.VMEM(cot_local.shape, cot_local.dtype),
            pltpu.VMEM((cells // 64 + 2, 10, 10, channels), jnp.float32),
            pltpu.VMEM((cells // 64 + 4, 10, 10, channels), jnp.float32),
            pltpu.SemaphoreType.DMA((micro_count, 2)),
            pltpu.SemaphoreType.DMA((micro_count, 2)),
        ],
        compiler_params=pltpu.CompilerParams(collective_id=3, has_side_effects=True),
    )(cot_local, seen, weight)


def per_device(clips, cotangent, weights):
    channels = weights.shape[-1]
    weight = gather_rows(weights[0]).reshape(-1, channels, channels)
    micro_count = clips.shape[0]
    clips_local = clips[:, 0].reshape(micro_count, -1, channels)
    cot_local = cotangent[:, 0].reshape(micro_count, -1, channels)
    seen, produced = forward_line(clips_local, weight)
    grad_total = backward_line(cot_local, seen, weight)
    grad_share = scatter_rows(grad_total.astype(jnp.bfloat16).reshape(lax.axis_size("dp"), -1, channels))
    return (produced.reshape(clips[:, 0].shape)[None, :, None], grad_share[None])


def solution(mesh):
    placed = (
        P(None, "dp", None, None, None, None),
        P(None, "dp", None, None, None, None),
        P("section", "dp", None),
    )
    return jax.shard_map(
        per_device,
        mesh=mesh,
        in_specs=placed,
        out_specs=(P("section", None, "dp", None, None, None, None), P("section", "dp", None)),
        check_vma=False,
    )
```

```python
import jax
import jax.numpy as jnp
from jax import lax
from jax.sharding import PartitionSpec as P

from jax.experimental import pallas as pl
from jax.experimental.pallas import tpu as pltpu

MESH_ID = pl.DeviceIdType.MESH


def greet_group(here, row):
    pair = here - here % 2
    partner = pair + 1 - here % 2
    barrier = pltpu.get_barrier_semaphore()
    pl.semaphore_signal(barrier, inc=1, device_id=(row, partner), device_id_type=MESH_ID)

    def signal(i, carry):
        peer = lax.rem(here + 2 * i, lax.axis_size("dp"))
        pl.semaphore_signal(barrier, inc=1, device_id=(row, peer), device_id_type=MESH_ID)
        return carry

    planes = lax.axis_size("dp") // 2
    lax.fori_loop(1, planes, signal, 0)
    pl.semaphore_wait(barrier, planes)
    return partner


def group_copy(src, dst, send_sem, recv_sem, row, peer):
    return pltpu.make_async_remote_copy(
        src_ref=src,
        dst_ref=dst,
        send_sem=send_sem,
        recv_sem=recv_sem,
        device_id=(row, peer),
        device_id_type=MESH_ID,
    )


def gather_kernel(shard_ref, out_ref, send_sem, recv_sem):
    peers = lax.axis_size("dp")
    here = lax.axis_index("dp")
    row = lax.axis_index("section")
    partner = greet_group(here, row)
    planes = peers // 2
    cross = group_copy(shard_ref, out_ref.at[here], send_sem.at[here], recv_sem.at[here], row, partner)
    cross.start()

    def fan(i, peer):
        own = group_copy(shard_ref, out_ref.at[here], send_sem.at[peer], recv_sem.at[here], row, peer)
        relayed = group_copy(out_ref.at[partner], out_ref.at[partner], send_sem.at[peer + 1 - 2 * (peer % 2)],
                             recv_sem.at[partner], row, peer)
        return own, relayed

    def start_own(i, carry):
        fan(i, lax.rem(here + 2 * i, peers))[0].start()
        return carry

    def start_relay(i, carry):
        fan(i, lax.rem(here + 2 * i, peers))[1].start()
        return carry

    lax.fori_loop(1, planes, start_own, 0)
    out_ref[here] = shard_ref[...]
    cross.wait_send()
    group_copy(shard_ref, out_ref.at[partner], send_sem.at[partner], recv_sem.at[partner], row, partner).wait_recv()
    lax.fori_loop(1, planes, start_relay, 0)

    def finish(i, carry):
        peer = lax.rem(here + 2 * i, peers)
        own, relayed = fan(i, peer)
        own.wait_send()
        relayed.wait_send()
        mate = peer + 1 - 2 * (peer % 2)
        group_copy(shard_ref, out_ref.at[peer], send_sem.at[peer], recv_sem.at[peer], row, peer).wait_recv()
        group_copy(shard_ref, out_ref.at[mate], send_sem.at[mate], recv_sem.at[mate], row, peer).wait_recv()
        return carry

    lax.fori_loop(1, planes, finish, 0)


def gather_rows(shard):
    peers = lax.axis_size("dp")
    rows, cols = shard.shape
    return pl.pallas_call(
        gather_kernel,
        out_shape=jax.ShapeDtypeStruct((peers, rows, cols), shard.dtype),
        in_specs=[pl.BlockSpec(memory_space=pltpu.VMEM)],
        out_specs=pl.BlockSpec(memory_space=pltpu.VMEM),
        scratch_shapes=[pltpu.SemaphoreType.DMA((peers,)), pltpu.SemaphoreType.DMA((peers,))],
        compiler_params=pltpu.CompilerParams(collective_id=0, has_side_effects=True),
    )(shard)


def scatter_kernel(parts_ref, out_ref, held, mine, theirs, send_sem, recv_sem, cross_sem):
    peers = lax.axis_size("dp")
    here = lax.axis_index("dp")
    row = lax.axis_index("section")
    partner = greet_group(here, row)
    planes = peers // 2
    slot = here // 2
    side = here % 2

    def fan(peer, block):
        return group_copy(parts_ref.at[2 * (peer // 2) + block], held.at[slot, block],
                          send_sem.at[peer // 2, block], recv_sem.at[slot, block], row, peer)

    def start(i, carry):
        peer = lax.rem(here + 2 * i, peers)
        fan(peer, 0).start()
        fan(peer, 1).start()
        return carry

    lax.fori_loop(1, planes, start, 0)

    def finish(i, totals):
        peer = lax.rem(here + 2 * i, peers)
        fan(peer, 0).wait_send()
        fan(peer, 1).wait_send()
        source = peer // 2
        for block in range(2):
            group_copy(parts_ref.at[block], held.at[source, block], send_sem.at[source, block],
                       recv_sem.at[source, block], row, peer).wait_recv()
        return (totals[0] + held[source, 0].astype(jnp.float32), totals[1] + held[source, 1].astype(jnp.float32))

    start_totals = (parts_ref[2 * slot].astype(jnp.float32), parts_ref[2 * slot + 1].astype(jnp.float32))
    first, second = lax.fori_loop(1, planes, finish, start_totals)
    theirs[...] = jnp.where(side == 0, second, first)
    cross = group_copy(theirs, mine, cross_sem.at[0], cross_sem.at[1], row, partner)
    cross.start()
    cross.wait_send()
    cross.wait_recv()
    out_ref[...] = jnp.where(side == 0, first, second) + mine[...]


def scatter_rows(parts):
    peers, rows, cols = parts.shape
    return pl.pallas_call(
        scatter_kernel,
        out_shape=jax.ShapeDtypeStruct((rows, cols), jnp.float32),
        in_specs=[pl.BlockSpec(memory_space=pltpu.VMEM)],
        out_specs=pl.BlockSpec(memory_space=pltpu.VMEM),
        scratch_shapes=[
            pltpu.VMEM((peers // 2, 2, rows, cols), parts.dtype),
            pltpu.VMEM((rows, cols), jnp.float32),
            pltpu.VMEM((rows, cols), jnp.float32),
            pltpu.SemaphoreType.DMA((peers // 2, 2)),
            pltpu.SemaphoreType.DMA((peers // 2, 2)),
            pltpu.SemaphoreType.DMA((2,)),
        ],
        compiler_params=pltpu.CompilerParams(collective_id=1, has_side_effects=True),
    )(parts)


def squash_into(pad_ref, activation):
    squashed = (activation / (1.0 + jnp.exp(-activation))).astype(jnp.bfloat16).astype(jnp.float32)
    field = squashed.reshape(pad_ref.shape[0] - 2, 8, 8, pad_ref.shape[-1])
    pad_ref[2:, 1:9, 1:9, :] = field
    pad_ref[0:2, 1:9, 1:9, :] = jnp.broadcast_to(field[0:1], (2,) + field.shape[1:])


def tap_windows(pad_ref, frames, flipped):
    channels = pad_ref.shape[-1]
    windows = {}
    for c0 in range(3):
        shifted = pad_ref[:, :, c0 : c0 + 8, :]
        offset_col = 2 - c0 if flipped else c0
        for offset_time in range(3):
            for offset_row in range(3):
                t0 = 2 - offset_time if flipped else offset_time
                r0 = 2 - offset_row if flipped else offset_row
                window = shifted[t0 : t0 + frames, r0 : r0 + 8].reshape(frames * 64, channels)
                windows[offset_time * 9 + offset_row * 3 + offset_col] = window.astype(jnp.bfloat16)
    taps = len(windows)
    for first in range(0, taps, 2):
        group = [windows[tap] for tap in range(first, min(first + 2, taps))]
        yield first, len(group), jnp.concatenate(group, axis=1) if len(group) > 1 else group[0]


def greet_line(here, count, col):
    barrier = pltpu.get_barrier_semaphore()

    @pl.when(here > 0)
    def _():
        pl.semaphore_signal(barrier, inc=1, device_id=(here - 1, col), device_id_type=MESH_ID)

    @pl.when(here < count - 1)
    def _():
        pl.semaphore_signal(barrier, inc=1, device_id=(here + 1, col), device_id_type=MESH_ID)

    neighbours = (here + count - 1) // count + (2 * count - 2 - here) // count
    pl.semaphore_wait(barrier, neighbours)


def line_copy(src, dst, send_sem, recv_sem, target, col):
    return pltpu.make_async_remote_copy(
        src_ref=src,
        dst_ref=dst,
        send_sem=send_sem,
        recv_sem=recv_sem,
        device_id=(target, col),
        device_id_type=MESH_ID,
    )


def forward_kernel(clips_ref, w_ref, seen_ref, out_ref, recv, pad, send_sem, recv_sem):
    count = lax.axis_size("section")
    here = lax.axis_index("section")
    col = lax.axis_index("dp")
    micro_count, _, channels = clips_ref.shape
    greet_line(here, count, col)
    pad[...] = jnp.zeros_like(pad)

    def step(m, carry):
        @pl.when(here == 0)
        def _():
            seen_ref[m] = clips_ref[m]

        @pl.when(here > 0)
        def _():
            line_copy(out_ref.at[m], recv.at[m], send_sem.at[m], recv_sem.at[m], here - 1, col).wait_recv()
            seen_ref[m] = recv[m]

        base = seen_ref[m].astype(jnp.float32)
        squash_into(pad, base)
        total = base
        for tap, width, window in tap_windows(pad, 4, False):
            rows = pl.ds(tap * channels, width * channels)
            total = total + jnp.dot(window, w_ref[rows, :], preferred_element_type=jnp.float32)
        out_ref[m] = total.astype(out_ref.dtype)

        @pl.when(here < count - 1)
        def _():
            line_copy(out_ref.at[m], recv.at[m], send_sem.at[m], recv_sem.at[m], here + 1, col).start()

        return carry

    lax.fori_loop(0, micro_count, step, 0)

    @pl.when(here < count - 1)
    def _():
        for m in range(micro_count):
            line_copy(out_ref.at[m], recv.at[m], send_sem.at[m], recv_sem.at[m], here + 1, col).wait_send()


def forward_line(clips_local, weight):
    shape = jax.ShapeDtypeStruct(clips_local.shape, clips_local.dtype)
    micro_count, cells, channels = clips_local.shape
    return pl.pallas_call(
        forward_kernel,
        out_shape=(shape, shape),
        in_specs=[pl.BlockSpec(memory_space=pltpu.VMEM)] * 2,
        out_specs=(pl.BlockSpec(memory_space=pltpu.VMEM),) * 2,
        scratch_shapes=[
            pltpu.VMEM(clips_local.shape, clips_local.dtype),
            pltpu.VMEM((cells // 64 + 2, 10, 10, channels), jnp.float32),
            pltpu.SemaphoreType.DMA((micro_count,)),
            pltpu.SemaphoreType.DMA((micro_count,)),
        ],
        compiler_params=pltpu.CompilerParams(collective_id=2, has_side_effects=True),
    )(clips_local, weight)


def backward_kernel(cot_ref, seen_ref, w_ref, wg_ref, recv, sendbuf, pad, gpad, send_sem, recv_sem):
    count = lax.axis_size("section")
    here = lax.axis_index("section")
    col = lax.axis_index("dp")
    micro_count, _, channels = cot_ref.shape
    greet_line(here, count, col)
    pad[...] = jnp.zeros_like(pad)
    gpad[...] = jnp.zeros_like(gpad)
    wg_ref[...] = jnp.zeros_like(wg_ref)

    def step(m, carry):
        @pl.when(here == count - 1)
        def _():
            recv[m] = cot_ref[m]

        @pl.when(here < count - 1)
        def _():
            line_copy(sendbuf.at[m], recv.at[m], send_sem.at[m], recv_sem.at[m], here + 1, col).wait_recv()

        upstream = recv[m]
        base = seen_ref[m].astype(jnp.float32)
        squash_into(pad, base)
        @pl.when(here > 0)
        def _():
            up = upstream.astype(jnp.float32)
            gpad[2:6, 1:9, 1:9, :] = up.reshape(4, 8, 8, up.shape[-1])
            spread = jnp.zeros((384, up.shape[-1]), jnp.float32)
            for tap, width, window in tap_windows(gpad, 6, True):
                paired = jnp.concatenate([w_ref[pl.ds((tap + k) * channels, channels), :] for k in range(width)], axis=1)
                spread = spread + lax.dot_general(
                    window, paired, (((1,), (1,)), ((), ())),
                    preferred_element_type=jnp.float32,
                )
            field = jnp.concatenate([spread[0:64] + spread[64:128] + spread[128:192], spread[192:384]], axis=0)
            sig = 1.0 / (1.0 + jnp.exp(-base))
            slope = sig * (1.0 + base * (1.0 - sig))
            sendbuf[m] = (up + field * slope).astype(sendbuf.dtype)
            line_copy(sendbuf.at[m], recv.at[m], send_sem.at[m], recv_sem.at[m], here - 1, col).start()

        for tap, width, window in tap_windows(pad, 4, False):
            wg_ref[pl.ds(tap * channels, width * channels), :] += lax.dot_general(
                window, upstream, (((0,), (0,)), ((), ())),
                preferred_element_type=jnp.float32,
            )
        return carry

    lax.fori_loop(0, micro_count, step, 0)

    @pl.when(here > 0)
    def _():
        for m in range(micro_count):
            line_copy(sendbuf.at[m], recv.at[m], send_sem.at[m], recv_sem.at[m], here - 1, col).wait_send()


def backward_line(cot_local, seen, weight):
    micro_count, cells, channels = cot_local.shape
    return pl.pallas_call(
        backward_kernel,
        out_shape=jax.ShapeDtypeStruct(weight.shape, jnp.float32),
        in_specs=[pl.BlockSpec(memory_space=pltpu.VMEM)] * 3,
        out_specs=pl.BlockSpec(memory_space=pltpu.VMEM),
        scratch_shapes=[
            pltpu.VMEM(cot_local.shape, cot_local.dtype),
            pltpu.VMEM(cot_local.shape, cot_local.dtype),
            pltpu.VMEM((cells // 64 + 2, 10, 10, channels), jnp.float32),
            pltpu.VMEM((cells // 64 + 4, 10, 10, channels), jnp.float32),
            pltpu.SemaphoreType.DMA((micro_count,)),
            pltpu.SemaphoreType.DMA((micro_count,)),
        ],
        compiler_params=pltpu.CompilerParams(collective_id=3, has_side_effects=True),
    )(cot_local, seen, weight)


def per_device(clips, cotangent, weights):
    channels = weights.shape[-1]
    weight = gather_rows(weights[0]).reshape(-1, channels)
    micro_count = clips.shape[0]
    clips_local = clips[:, 0].reshape(micro_count, -1, channels)
    cot_local = cotangent[:, 0].reshape(micro_count, -1, channels)
    seen, produced = forward_line(clips_local, weight)
    grad_total = backward_line(cot_local, seen, weight)
    grad_share = scatter_rows(grad_total.astype(jnp.bfloat16).reshape(lax.axis_size("dp"), -1, channels))
    return (produced.reshape(clips[:, 0].shape)[None, :, None], grad_share[None])


def solution(mesh):
    placed = (
        P(None, "dp", None, None, None, None),
        P(None, "dp", None, None, None, None),
        P("section", "dp", None),
    )
    return jax.shard_map(
        per_device,
        mesh=mesh,
        in_specs=placed,
        out_specs=(P("section", None, "dp", None, None, None, None), P("section", "dp", None)),
        check_vma=False,
    )
```

```python
import jax
import jax.numpy as jnp
from jax import lax
from jax.sharding import PartitionSpec as P

from jax.experimental import pallas as pl
from jax.experimental.pallas import tpu as pltpu

MESH_ID = pl.DeviceIdType.MESH


def greet_group(here, row):
    pair = here - here % 2
    partner = pair + 1 - here % 2
    barrier = pltpu.get_barrier_semaphore()
    pl.semaphore_signal(barrier, inc=1, device_id=(row, partner), device_id_type=MESH_ID)

    def signal(i, carry):
        peer = lax.rem(here + 2 * i, lax.axis_size("dp"))
        pl.semaphore_signal(barrier, inc=1, device_id=(row, peer), device_id_type=MESH_ID)
        return carry

    planes = lax.axis_size("dp") // 2
    lax.fori_loop(1, planes, signal, 0)
    pl.semaphore_wait(barrier, planes)
    return partner


def group_copy(src, dst, send_sem, recv_sem, row, peer):
    return pltpu.make_async_remote_copy(
        src_ref=src,
        dst_ref=dst,
        send_sem=send_sem,
        recv_sem=recv_sem,
        device_id=(row, peer),
        device_id_type=MESH_ID,
    )


def gather_kernel(shard_ref, flat_ref, out_ref, send_sem, recv_sem):
    peers = lax.axis_size("dp")
    here = lax.axis_index("dp")
    row = lax.axis_index("section")
    partner = greet_group(here, row)
    planes = peers // 2
    cross = group_copy(shard_ref, out_ref.at[here], send_sem.at[here], recv_sem.at[here], row, partner)
    cross.start()

    def fan(i, peer):
        own = group_copy(shard_ref, out_ref.at[here], send_sem.at[peer], recv_sem.at[here], row, peer)
        relayed = group_copy(out_ref.at[partner], out_ref.at[partner], send_sem.at[peer + 1 - 2 * (peer % 2)],
                             recv_sem.at[partner], row, peer)
        return own, relayed

    def start_own(i, carry):
        fan(i, lax.rem(here + 2 * i, peers))[0].start()
        return carry

    def start_relay(i, carry):
        fan(i, lax.rem(here + 2 * i, peers))[1].start()
        return carry

    lax.fori_loop(1, planes, start_own, 0)
    out_ref[here] = shard_ref[...]
    cross.wait_send()
    group_copy(shard_ref, out_ref.at[partner], send_sem.at[partner], recv_sem.at[partner], row, partner).wait_recv()
    lax.fori_loop(1, planes, start_relay, 0)

    def finish(i, carry):
        peer = lax.rem(here + 2 * i, peers)
        own, relayed = fan(i, peer)
        own.wait_send()
        relayed.wait_send()
        mate = peer + 1 - 2 * (peer % 2)
        group_copy(shard_ref, out_ref.at[peer], send_sem.at[peer], recv_sem.at[peer], row, peer).wait_recv()
        group_copy(shard_ref, out_ref.at[mate], send_sem.at[mate], recv_sem.at[mate], row, peer).wait_recv()
        return carry

    lax.fori_loop(1, planes, finish, 0)
    rows = shard_ref.shape[0]
    for block in range(peers):
        flat_ref[block * rows : (block + 1) * rows, :] = out_ref[block]


def gather_rows(shard):
    peers = lax.axis_size("dp")
    rows, cols = shard.shape
    return pl.pallas_call(
        gather_kernel,
        out_shape=jax.ShapeDtypeStruct((peers * rows, cols), shard.dtype),
        in_specs=[pl.BlockSpec(memory_space=pltpu.VMEM)],
        out_specs=pl.BlockSpec(memory_space=pltpu.VMEM),
        scratch_shapes=[
            pltpu.VMEM((peers, rows, cols), shard.dtype),
            pltpu.SemaphoreType.DMA((peers,)),
            pltpu.SemaphoreType.DMA((peers,)),
        ],
        compiler_params=pltpu.CompilerParams(collective_id=0, has_side_effects=True),
    )(shard)


def scatter_kernel(parts_ref, out_ref, held, mine, theirs, send_sem, recv_sem, cross_sem):
    peers = lax.axis_size("dp")
    here = lax.axis_index("dp")
    row = lax.axis_index("section")
    partner = greet_group(here, row)
    planes = peers // 2
    slot = here // 2
    side = here % 2

    def fan(peer, block):
        return group_copy(parts_ref.at[2 * (peer // 2) + block], held.at[slot, block],
                          send_sem.at[peer // 2, block], recv_sem.at[slot, block], row, peer)

    def start(i, carry):
        peer = lax.rem(here + 2 * i, peers)
        fan(peer, 0).start()
        fan(peer, 1).start()
        return carry

    lax.fori_loop(1, planes, start, 0)

    def finish(i, totals):
        peer = lax.rem(here + 2 * i, peers)
        fan(peer, 0).wait_send()
        fan(peer, 1).wait_send()
        source = peer // 2
        for block in range(2):
            group_copy(parts_ref.at[block], held.at[source, block], send_sem.at[source, block],
                       recv_sem.at[source, block], row, peer).wait_recv()
        return (totals[0] + held[source, 0].astype(jnp.float32), totals[1] + held[source, 1].astype(jnp.float32))

    start_totals = (parts_ref[2 * slot].astype(jnp.float32), parts_ref[2 * slot + 1].astype(jnp.float32))
    first, second = lax.fori_loop(1, planes, finish, start_totals)
    theirs[...] = jnp.where(side == 0, second, first)
    cross = group_copy(theirs, mine, cross_sem.at[0], cross_sem.at[1], row, partner)
    cross.start()
    cross.wait_send()
    cross.wait_recv()
    out_ref[...] = jnp.where(side == 0, first, second) + mine[...]


def scatter_rows(parts):
    peers, rows, cols = parts.shape
    return pl.pallas_call(
        scatter_kernel,
        out_shape=jax.ShapeDtypeStruct((rows, cols), jnp.float32),
        in_specs=[pl.BlockSpec(memory_space=pltpu.VMEM)],
        out_specs=pl.BlockSpec(memory_space=pltpu.VMEM),
        scratch_shapes=[
            pltpu.VMEM((peers // 2, 2, rows, cols), parts.dtype),
            pltpu.VMEM((rows, cols), jnp.float32),
            pltpu.VMEM((rows, cols), jnp.float32),
            pltpu.SemaphoreType.DMA((peers // 2, 2)),
            pltpu.SemaphoreType.DMA((peers // 2, 2)),
            pltpu.SemaphoreType.DMA((2,)),
        ],
        compiler_params=pltpu.CompilerParams(collective_id=1, has_side_effects=True),
    )(parts)


def squash_into(pad_ref, activation):
    squashed = (activation / (1.0 + jnp.exp(-activation))).astype(jnp.bfloat16).astype(jnp.float32)
    field = squashed.reshape(pad_ref.shape[0] - 2, 8, 8, pad_ref.shape[-1])
    pad_ref[2:, 1:9, 1:9, :] = field
    pad_ref[0:2, 1:9, 1:9, :] = jnp.broadcast_to(field[0:1], (2,) + field.shape[1:])


def tap_windows(pad_ref, frames, flipped):
    channels = pad_ref.shape[-1]
    for c0 in range(3):
        shifted = pad_ref[:, :, c0 : c0 + 8, :]
        offset_col = 2 - c0 if flipped else c0
        for offset_time in range(3):
            for offset_row in range(3):
                t0 = 2 - offset_time if flipped else offset_time
                r0 = 2 - offset_row if flipped else offset_row
                window = shifted[t0 : t0 + frames, r0 : r0 + 8].reshape(frames * 64, channels)
                yield offset_time * 9 + offset_row * 3 + offset_col, window.astype(jnp.bfloat16)


def greet_line(here, count, col):
    barrier = pltpu.get_barrier_semaphore()

    @pl.when(here > 0)
    def _():
        pl.semaphore_signal(barrier, inc=1, device_id=(here - 1, col), device_id_type=MESH_ID)

    @pl.when(here < count - 1)
    def _():
        pl.semaphore_signal(barrier, inc=1, device_id=(here + 1, col), device_id_type=MESH_ID)

    neighbours = (here + count - 1) // count + (2 * count - 2 - here) // count
    pl.semaphore_wait(barrier, neighbours)


def line_copy(src, dst, send_sem, recv_sem, target, col):
    return pltpu.make_async_remote_copy(
        src_ref=src,
        dst_ref=dst,
        send_sem=send_sem,
        recv_sem=recv_sem,
        device_id=(target, col),
        device_id_type=MESH_ID,
    )


def forward_kernel(clips_ref, w_ref, seen_ref, out_ref, recv, pad, send_sem, recv_sem):
    count = lax.axis_size("section")
    here = lax.axis_index("section")
    col = lax.axis_index("dp")
    micro_count = clips_ref.shape[0]
    greet_line(here, count, col)
    pad[...] = jnp.zeros_like(pad)

    def step(m, carry):
        @pl.when(here == 0)
        def _():
            seen_ref[m] = clips_ref[m]

        @pl.when(here > 0)
        def _():
            line_copy(out_ref.at[m], recv.at[m], send_sem.at[m], recv_sem.at[m], here - 1, col).wait_recv()
            seen_ref[m] = recv[m]

        base = seen_ref[m].astype(jnp.float32)
        squash_into(pad, base)
        total = base
        for tap, window in tap_windows(pad, 4, False):
            total = total + jnp.dot(window, w_ref[tap], preferred_element_type=jnp.float32)
        out_ref[m] = total.astype(out_ref.dtype)

        @pl.when(here < count - 1)
        def _():
            line_copy(out_ref.at[m], recv.at[m], send_sem.at[m], recv_sem.at[m], here + 1, col).start()

        return carry

    lax.fori_loop(0, micro_count, step, 0)

    @pl.when(here < count - 1)
    def _():
        for m in range(micro_count):
            line_copy(out_ref.at[m], recv.at[m], send_sem.at[m], recv_sem.at[m], here + 1, col).wait_send()


def forward_line(clips_local, weight):
    shape = jax.ShapeDtypeStruct(clips_local.shape, clips_local.dtype)
    micro_count, cells, channels = clips_local.shape
    return pl.pallas_call(
        forward_kernel,
        out_shape=(shape, shape),
        in_specs=[pl.BlockSpec(memory_space=pltpu.VMEM)] * 2,
        out_specs=(pl.BlockSpec(memory_space=pltpu.VMEM),) * 2,
        scratch_shapes=[
            pltpu.VMEM(clips_local.shape, clips_local.dtype),
            pltpu.VMEM((cells // 64 + 2, 10, 10, channels), jnp.float32),
            pltpu.SemaphoreType.DMA((micro_count,)),
            pltpu.SemaphoreType.DMA((micro_count,)),
        ],
        compiler_params=pltpu.CompilerParams(collective_id=2, has_side_effects=True),
    )(clips_local, weight)


def backward_kernel(cot_ref, seen_ref, w_ref, parts_ref, recv, sendbuf, pad, gpad, wg_ref, send_sem, recv_sem):
    count = lax.axis_size("section")
    here = lax.axis_index("section")
    col = lax.axis_index("dp")
    micro_count = cot_ref.shape[0]
    greet_line(here, count, col)
    pad[...] = jnp.zeros_like(pad)
    gpad[...] = jnp.zeros_like(gpad)
    wg_ref[...] = jnp.zeros_like(wg_ref)

    def step(m, carry):
        @pl.when(here == count - 1)
        def _():
            recv[m] = cot_ref[m]

        @pl.when(here < count - 1)
        def _():
            line_copy(sendbuf.at[m], recv.at[m], send_sem.at[m], recv_sem.at[m], here + 1, col).wait_recv()

        upstream = recv[m]
        base = seen_ref[m].astype(jnp.float32)
        squash_into(pad, base)
        @pl.when(here > 0)
        def _():
            up = upstream.astype(jnp.float32)
            gpad[2:6, 1:9, 1:9, :] = up.reshape(4, 8, 8, up.shape[-1])
            spread = jnp.zeros((384, up.shape[-1]), jnp.float32)
            for tap, window in tap_windows(gpad, 6, True):
                spread = spread + lax.dot_general(
                    window, w_ref[tap], (((1,), (1,)), ((), ())),
                    preferred_element_type=jnp.float32,
                )
            field = jnp.concatenate([spread[0:64] + spread[64:128] + spread[128:192], spread[192:384]], axis=0)
            sig = 1.0 / (1.0 + jnp.exp(-base))
            slope = sig * (1.0 + base * (1.0 - sig))
            sendbuf[m] = (up + field * slope).astype(sendbuf.dtype)
            line_copy(sendbuf.at[m], recv.at[m], send_sem.at[m], recv_sem.at[m], here - 1, col).start()

        for tap, window in tap_windows(pad, 4, False):
            wg_ref[tap * 128 : (tap + 1) * 128, :] += lax.dot_general(
                window, upstream, (((0,), (0,)), ((), ())),
                preferred_element_type=jnp.float32,
            )
        return carry

    lax.fori_loop(0, micro_count, step, 0)

    block_rows = parts_ref.shape[1]
    for block in range(parts_ref.shape[0]):
        parts_ref[block] = wg_ref[block * block_rows : (block + 1) * block_rows, :].astype(parts_ref.dtype)

    @pl.when(here > 0)
    def _():
        for m in range(micro_count):
            line_copy(sendbuf.at[m], recv.at[m], send_sem.at[m], recv_sem.at[m], here - 1, col).wait_send()


def backward_line(cot_local, seen, weight, blocks):
    micro_count, cells, channels = cot_local.shape
    taps = weight.shape[0]
    return pl.pallas_call(
        backward_kernel,
        out_shape=jax.ShapeDtypeStruct((blocks, taps * channels // blocks, channels), jnp.bfloat16),
        in_specs=[pl.BlockSpec(memory_space=pltpu.VMEM)] * 3,
        out_specs=pl.BlockSpec(memory_space=pltpu.VMEM),
        scratch_shapes=[
            pltpu.VMEM(cot_local.shape, cot_local.dtype),
            pltpu.VMEM(cot_local.shape, cot_local.dtype),
            pltpu.VMEM((cells // 64 + 2, 10, 10, channels), jnp.float32),
            pltpu.VMEM((cells // 64 + 4, 10, 10, channels), jnp.float32),
            pltpu.VMEM((taps * channels, channels), jnp.float32),
            pltpu.SemaphoreType.DMA((micro_count,)),
            pltpu.SemaphoreType.DMA((micro_count,)),
        ],
        compiler_params=pltpu.CompilerParams(collective_id=3, has_side_effects=True),
    )(cot_local, seen, weight)


def per_device(clips, cotangent, weights):
    channels = weights.shape[-1]
    weight = gather_rows(weights[0]).reshape(-1, channels, channels)
    blocks = lax.axis_size("dp")
    micro_count = clips.shape[0]
    clips_local = clips[:, 0].reshape(micro_count, -1, channels)
    cot_local = cotangent[:, 0].reshape(micro_count, -1, channels)
    seen, produced = forward_line(clips_local, weight)
    grad_share = scatter_rows(backward_line(cot_local, seen, weight, blocks))
    return (produced.reshape(clips[:, 0].shape)[None, :, None], grad_share[None])


def solution(mesh):
    placed = (
        P(None, "dp", None, None, None, None),
        P(None, "dp", None, None, None, None),
        P("section", "dp", None),
    )
    return jax.shard_map(
        per_device,
        mesh=mesh,
        in_specs=placed,
        out_specs=(P("section", None, "dp", None, None, None, None), P("section", "dp", None)),
        check_vma=False,
    )
```

```python
import jax
import jax.numpy as jnp
from jax import lax
from jax.sharding import PartitionSpec as P

from jax.experimental import pallas as pl
from jax.experimental.pallas import tpu as pltpu

MESH_ID = pl.DeviceIdType.MESH


def greet_group(here, row):
    pair = here - here % 2
    partner = pair + 1 - here % 2
    barrier = pltpu.get_barrier_semaphore()
    pl.semaphore_signal(barrier, inc=1, device_id=(row, partner), device_id_type=MESH_ID)

    def signal(i, carry):
        peer = lax.rem(here + 2 * i, lax.axis_size("dp"))
        pl.semaphore_signal(barrier, inc=1, device_id=(row, peer), device_id_type=MESH_ID)
        return carry

    planes = lax.axis_size("dp") // 2
    lax.fori_loop(1, planes, signal, 0)
    pl.semaphore_wait(barrier, planes)
    return partner


def group_copy(src, dst, send_sem, recv_sem, row, peer):
    return pltpu.make_async_remote_copy(
        src_ref=src,
        dst_ref=dst,
        send_sem=send_sem,
        recv_sem=recv_sem,
        device_id=(row, peer),
        device_id_type=MESH_ID,
    )


def gather_kernel(shard_ref, flat_ref, out_ref, send_sem, recv_sem):
    peers = lax.axis_size("dp")
    here = lax.axis_index("dp")
    row = lax.axis_index("section")
    partner = greet_group(here, row)
    planes = peers // 2
    cross = group_copy(shard_ref, out_ref.at[here], send_sem.at[here], recv_sem.at[here], row, partner)
    cross.start()

    def fan(i, peer):
        own = group_copy(shard_ref, out_ref.at[here], send_sem.at[peer], recv_sem.at[here], row, peer)
        relayed = group_copy(out_ref.at[partner], out_ref.at[partner], send_sem.at[peer + 1 - 2 * (peer % 2)],
                             recv_sem.at[partner], row, peer)
        return own, relayed

    def start_own(i, carry):
        fan(i, lax.rem(here + 2 * i, peers))[0].start()
        return carry

    def start_relay(i, carry):
        fan(i, lax.rem(here + 2 * i, peers))[1].start()
        return carry

    lax.fori_loop(1, planes, start_own, 0)
    out_ref[here] = shard_ref[...]
    cross.wait_send()
    group_copy(shard_ref, out_ref.at[partner], send_sem.at[partner], recv_sem.at[partner], row, partner).wait_recv()
    lax.fori_loop(1, planes, start_relay, 0)

    def finish(i, carry):
        peer = lax.rem(here + 2 * i, peers)
        own, relayed = fan(i, peer)
        own.wait_send()
        relayed.wait_send()
        mate = peer + 1 - 2 * (peer % 2)
        group_copy(shard_ref, out_ref.at[peer], send_sem.at[peer], recv_sem.at[peer], row, peer).wait_recv()
        group_copy(shard_ref, out_ref.at[mate], send_sem.at[mate], recv_sem.at[mate], row, peer).wait_recv()
        return carry

    lax.fori_loop(1, planes, finish, 0)
    rows = shard_ref.shape[0]
    for block in range(peers):
        flat_ref[block * rows : (block + 1) * rows, :] = out_ref[block]


def gather_rows(shard):
    peers = lax.axis_size("dp")
    rows, cols = shard.shape
    return pl.pallas_call(
        gather_kernel,
        out_shape=jax.ShapeDtypeStruct((peers * rows, cols), shard.dtype),
        in_specs=[pl.BlockSpec(memory_space=pltpu.VMEM)],
        out_specs=pl.BlockSpec(memory_space=pltpu.VMEM),
        scratch_shapes=[
            pltpu.VMEM((peers, rows, cols), shard.dtype),
            pltpu.SemaphoreType.DMA((peers,)),
            pltpu.SemaphoreType.DMA((peers,)),
        ],
        compiler_params=pltpu.CompilerParams(collective_id=0, has_side_effects=True),
    )(shard)


def scatter_kernel(parts_ref, out_ref, held, mine, theirs, send_sem, recv_sem, cross_sem):
    peers = lax.axis_size("dp")
    here = lax.axis_index("dp")
    row = lax.axis_index("section")
    partner = greet_group(here, row)
    planes = peers // 2
    slot = here // 2
    side = here % 2

    def fan(peer, block):
        return group_copy(parts_ref.at[2 * (peer // 2) + block], held.at[slot, block],
                          send_sem.at[peer // 2, block], recv_sem.at[slot, block], row, peer)

    far = 1 - side

    def start_far(i, carry):
        fan(lax.rem(here + 2 * i, peers), far).start()
        return carry

    def start_near(i, carry):
        fan(lax.rem(here + 2 * i, peers), side).start()
        return carry

    lax.fori_loop(1, planes, start_far, 0)
    lax.fori_loop(1, planes, start_near, 0)

    def gather_block(block):
        def finish(i, total):
            peer = lax.rem(here + 2 * i, peers)
            fan(peer, block).wait_send()
            source = peer // 2
            group_copy(parts_ref.at[block], held.at[source, block], send_sem.at[source, block],
                       recv_sem.at[source, block], row, peer).wait_recv()
            return total + held[source, block].astype(jnp.float32)

        return lax.fori_loop(1, planes, finish, parts_ref[2 * slot + block].astype(jnp.float32))

    theirs[...] = gather_block(far)
    cross = group_copy(theirs, mine, cross_sem.at[0], cross_sem.at[1], row, partner)
    cross.start()
    own = gather_block(side)
    cross.wait_send()
    cross.wait_recv()
    out_ref[...] = own + mine[...]


def scatter_rows(parts):
    peers, rows, cols = parts.shape
    return pl.pallas_call(
        scatter_kernel,
        out_shape=jax.ShapeDtypeStruct((rows, cols), jnp.float32),
        in_specs=[pl.BlockSpec(memory_space=pltpu.VMEM)],
        out_specs=pl.BlockSpec(memory_space=pltpu.VMEM),
        scratch_shapes=[
            pltpu.VMEM((peers // 2, 2, rows, cols), parts.dtype),
            pltpu.VMEM((rows, cols), jnp.float32),
            pltpu.VMEM((rows, cols), jnp.float32),
            pltpu.SemaphoreType.DMA((peers // 2, 2)),
            pltpu.SemaphoreType.DMA((peers // 2, 2)),
            pltpu.SemaphoreType.DMA((2,)),
        ],
        compiler_params=pltpu.CompilerParams(collective_id=1, has_side_effects=True),
    )(parts)


def squash_into(pad_ref, activation):
    squashed = (activation / (1.0 + jnp.exp(-activation))).astype(jnp.bfloat16).astype(jnp.float32)
    field = squashed.reshape(pad_ref.shape[0] - 2, 8, 8, pad_ref.shape[-1])
    pad_ref[2:, 1:9, 1:9, :] = field
    pad_ref[0:2, 1:9, 1:9, :] = jnp.broadcast_to(field[0:1], (2,) + field.shape[1:])


def tap_windows(pad_ref, frames, flipped):
    channels = pad_ref.shape[-1]
    for c0 in range(3):
        shifted = pad_ref[:, :, c0 : c0 + 8, :]
        offset_col = 2 - c0 if flipped else c0
        for offset_time in range(3):
            for offset_row in range(3):
                t0 = 2 - offset_time if flipped else offset_time
                r0 = 2 - offset_row if flipped else offset_row
                window = shifted[t0 : t0 + frames, r0 : r0 + 8].reshape(frames * 64, channels)
                yield offset_time * 9 + offset_row * 3 + offset_col, window.astype(jnp.bfloat16)


def greet_line(here, count, col):
    barrier = pltpu.get_barrier_semaphore()

    @pl.when(here > 0)
    def _():
        pl.semaphore_signal(barrier, inc=1, device_id=(here - 1, col), device_id_type=MESH_ID)

    @pl.when(here < count - 1)
    def _():
        pl.semaphore_signal(barrier, inc=1, device_id=(here + 1, col), device_id_type=MESH_ID)

    neighbours = (here + count - 1) // count + (2 * count - 2 - here) // count
    pl.semaphore_wait(barrier, neighbours)


def line_copy(src, dst, send_sem, recv_sem, target, col):
    return pltpu.make_async_remote_copy(
        src_ref=src,
        dst_ref=dst,
        send_sem=send_sem,
        recv_sem=recv_sem,
        device_id=(target, col),
        device_id_type=MESH_ID,
    )


def forward_kernel(clips_ref, w_ref, seen_ref, out_ref, recv, pad, send_sem, recv_sem):
    count = lax.axis_size("section")
    here = lax.axis_index("section")
    col = lax.axis_index("dp")
    micro_count = clips_ref.shape[0]
    greet_line(here, count, col)
    pad[...] = jnp.zeros_like(pad)

    def step(m, carry):
        @pl.when(here == 0)
        def _():
            seen_ref[m] = clips_ref[m]

        @pl.when(here > 0)
        def _():
            line_copy(out_ref.at[m], recv.at[m], send_sem.at[m], recv_sem.at[m], here - 1, col).wait_recv()
            seen_ref[m] = recv[m]

        base = seen_ref[m].astype(jnp.float32)
        squash_into(pad, base)
        total = base
        for tap, window in tap_windows(pad, 4, False):
            total = total + jnp.dot(window, w_ref[tap], preferred_element_type=jnp.float32)
        out_ref[m] = total.astype(out_ref.dtype)

        @pl.when(here < count - 1)
        def _():
            line_copy(out_ref.at[m], recv.at[m], send_sem.at[m], recv_sem.at[m], here + 1, col).start()

        return carry

    lax.fori_loop(0, micro_count, step, 0)

    @pl.when(here < count - 1)
    def _():
        for m in range(micro_count):
            line_copy(out_ref.at[m], recv.at[m], send_sem.at[m], recv_sem.at[m], here + 1, col).wait_send()


def forward_line(clips_local, weight):
    shape = jax.ShapeDtypeStruct(clips_local.shape, clips_local.dtype)
    micro_count, cells, channels = clips_local.shape
    return pl.pallas_call(
        forward_kernel,
        out_shape=(shape, shape),
        in_specs=[pl.BlockSpec(memory_space=pltpu.VMEM)] * 2,
        out_specs=(pl.BlockSpec(memory_space=pltpu.VMEM),) * 2,
        scratch_shapes=[
            pltpu.VMEM(clips_local.shape, clips_local.dtype),
            pltpu.VMEM((cells // 64 + 2, 10, 10, channels), jnp.float32),
            pltpu.SemaphoreType.DMA((micro_count,)),
            pltpu.SemaphoreType.DMA((micro_count,)),
        ],
        compiler_params=pltpu.CompilerParams(collective_id=2, has_side_effects=True),
    )(clips_local, weight)


def backward_kernel(cot_ref, seen_ref, w_ref, parts_ref, recv, sendbuf, pad, gpad, wg_ref, send_sem, recv_sem):
    count = lax.axis_size("section")
    here = lax.axis_index("section")
    col = lax.axis_index("dp")
    micro_count = cot_ref.shape[0]
    greet_line(here, count, col)
    pad[...] = jnp.zeros_like(pad)
    gpad[...] = jnp.zeros_like(gpad)
    wg_ref[...] = jnp.zeros_like(wg_ref)

    def step(m, carry):
        @pl.when(here == count - 1)
        def _():
            recv[m] = cot_ref[m]

        @pl.when(here < count - 1)
        def _():
            line_copy(sendbuf.at[m], recv.at[m], send_sem.at[m], recv_sem.at[m], here + 1, col).wait_recv()

        upstream = recv[m]
        base = seen_ref[m].astype(jnp.float32)
        squash_into(pad, base)
        @pl.when(here > 0)
        def _():
            up = upstream.astype(jnp.float32)
            gpad[2:6, 1:9, 1:9, :] = up.reshape(4, 8, 8, up.shape[-1])
            spread = jnp.zeros((384, up.shape[-1]), jnp.float32)
            for tap, window in tap_windows(gpad, 6, True):
                spread = spread + lax.dot_general(
                    window, w_ref[tap], (((1,), (1,)), ((), ())),
                    preferred_element_type=jnp.float32,
                )
            field = jnp.concatenate([spread[0:64] + spread[64:128] + spread[128:192], spread[192:384]], axis=0)
            sig = 1.0 / (1.0 + jnp.exp(-base))
            slope = sig * (1.0 + base * (1.0 - sig))
            sendbuf[m] = (up + field * slope).astype(sendbuf.dtype)
            line_copy(sendbuf.at[m], recv.at[m], send_sem.at[m], recv_sem.at[m], here - 1, col).start()

        for tap, window in tap_windows(pad, 4, False):
            wg_ref[tap * 128 : (tap + 1) * 128, :] += lax.dot_general(
                window, upstream, (((0,), (0,)), ((), ())),
                preferred_element_type=jnp.float32,
            )
        return carry

    lax.fori_loop(0, micro_count, step, 0)

    block_rows = parts_ref.shape[1]
    for block in range(parts_ref.shape[0]):
        parts_ref[block] = wg_ref[block * block_rows : (block + 1) * block_rows, :].astype(parts_ref.dtype)

    @pl.when(here > 0)
    def _():
        for m in range(micro_count):
            line_copy(sendbuf.at[m], recv.at[m], send_sem.at[m], recv_sem.at[m], here - 1, col).wait_send()


def backward_line(cot_local, seen, weight, blocks):
    micro_count, cells, channels = cot_local.shape
    taps = weight.shape[0]
    return pl.pallas_call(
        backward_kernel,
        out_shape=jax.ShapeDtypeStruct((blocks, taps * channels // blocks, channels), jnp.bfloat16),
        in_specs=[pl.BlockSpec(memory_space=pltpu.VMEM)] * 3,
        out_specs=pl.BlockSpec(memory_space=pltpu.VMEM),
        scratch_shapes=[
            pltpu.VMEM(cot_local.shape, cot_local.dtype),
            pltpu.VMEM(cot_local.shape, cot_local.dtype),
            pltpu.VMEM((cells // 64 + 2, 10, 10, channels), jnp.float32),
            pltpu.VMEM((cells // 64 + 4, 10, 10, channels), jnp.float32),
            pltpu.VMEM((taps * channels, channels), jnp.float32),
            pltpu.SemaphoreType.DMA((micro_count,)),
            pltpu.SemaphoreType.DMA((micro_count,)),
        ],
        compiler_params=pltpu.CompilerParams(collective_id=3, has_side_effects=True),
    )(cot_local, seen, weight)


def per_device(clips, cotangent, weights):
    channels = weights.shape[-1]
    weight = gather_rows(weights[0]).reshape(-1, channels, channels)
    blocks = lax.axis_size("dp")
    micro_count = clips.shape[0]
    clips_local = clips[:, 0].reshape(micro_count, -1, channels)
    cot_local = cotangent[:, 0].reshape(micro_count, -1, channels)
    seen, produced = forward_line(clips_local, weight)
    grad_share = scatter_rows(backward_line(cot_local, seen, weight, blocks))
    return (produced.reshape(clips[:, 0].shape)[None, :, None], grad_share[None])


def solution(mesh):
    placed = (
        P(None, "dp", None, None, None, None),
        P(None, "dp", None, None, None, None),
        P("section", "dp", None),
    )
    return jax.shard_map(
        per_device,
        mesh=mesh,
        in_specs=placed,
        out_specs=(P("section", None, "dp", None, None, None, None), P("section", "dp", None)),
        check_vma=False,
    )
```

```python
import jax
import jax.numpy as jnp
from jax import lax
from jax.sharding import PartitionSpec as P

from jax.experimental import pallas as pl
from jax.experimental.pallas import tpu as pltpu

MESH_ID = pl.DeviceIdType.MESH


def greet_group(here, row, extra=0):
    pair = here - here % 2
    partner = pair + 1 - here % 2
    barrier = pltpu.get_barrier_semaphore()
    pl.semaphore_signal(barrier, inc=1, device_id=(row, partner), device_id_type=MESH_ID)

    def signal(i, carry):
        peer = lax.rem(here + 2 * i, lax.axis_size("dp"))
        pl.semaphore_signal(barrier, inc=1, device_id=(row, peer), device_id_type=MESH_ID)
        return carry

    planes = lax.axis_size("dp") // 2
    lax.fori_loop(1, planes, signal, 0)
    pl.semaphore_wait(barrier, planes + extra)
    return partner


def group_copy(src, dst, send_sem, recv_sem, row, peer):
    return pltpu.make_async_remote_copy(
        src_ref=src,
        dst_ref=dst,
        send_sem=send_sem,
        recv_sem=recv_sem,
        device_id=(row, peer),
        device_id_type=MESH_ID,
    )


def gather_kernel(shard_ref, flat_ref, out_ref, send_sem, recv_sem):
    peers = lax.axis_size("dp")
    here = lax.axis_index("dp")
    row = lax.axis_index("section")
    partner = greet_group(here, row)
    planes = peers // 2
    cross = group_copy(shard_ref, out_ref.at[here], send_sem.at[here], recv_sem.at[here], row, partner)
    cross.start()

    def fan(i, peer):
        own = group_copy(shard_ref, out_ref.at[here], send_sem.at[peer], recv_sem.at[here], row, peer)
        relayed = group_copy(out_ref.at[partner], out_ref.at[partner], send_sem.at[peer + 1 - 2 * (peer % 2)],
                             recv_sem.at[partner], row, peer)
        return own, relayed

    def start_own(i, carry):
        fan(i, lax.rem(here + 2 * i, peers))[0].start()
        return carry

    def start_relay(i, carry):
        fan(i, lax.rem(here + 2 * i, peers))[1].start()
        return carry

    lax.fori_loop(1, planes, start_own, 0)
    out_ref[here] = shard_ref[...]
    cross.wait_send()
    group_copy(shard_ref, out_ref.at[partner], send_sem.at[partner], recv_sem.at[partner], row, partner).wait_recv()
    lax.fori_loop(1, planes, start_relay, 0)

    def finish(i, carry):
        peer = lax.rem(here + 2 * i, peers)
        own, relayed = fan(i, peer)
        own.wait_send()
        relayed.wait_send()
        mate = peer + 1 - 2 * (peer % 2)
        group_copy(shard_ref, out_ref.at[peer], send_sem.at[peer], recv_sem.at[peer], row, peer).wait_recv()
        group_copy(shard_ref, out_ref.at[mate], send_sem.at[mate], recv_sem.at[mate], row, peer).wait_recv()
        return carry

    lax.fori_loop(1, planes, finish, 0)
    rows = shard_ref.shape[0]
    for block in range(peers):
        flat_ref[block * rows : (block + 1) * rows, :] = out_ref[block]


def gather_rows(shard):
    peers = lax.axis_size("dp")
    rows, cols = shard.shape
    return pl.pallas_call(
        gather_kernel,
        out_shape=jax.ShapeDtypeStruct((peers * rows, cols), shard.dtype),
        in_specs=[pl.BlockSpec(memory_space=pltpu.VMEM)],
        out_specs=pl.BlockSpec(memory_space=pltpu.VMEM),
        scratch_shapes=[
            pltpu.VMEM((peers, rows, cols), shard.dtype),
            pltpu.SemaphoreType.DMA((peers,)),
            pltpu.SemaphoreType.DMA((peers,)),
        ],
        compiler_params=pltpu.CompilerParams(collective_id=0, has_side_effects=True),
    )(shard)


def scatter_kernel(parts_ref, out_ref, held, mine, theirs, send_sem, recv_sem, cross_sem):
    greet_group(lax.axis_index("dp"), lax.axis_index("section"))
    scatter_blocks(parts_ref, out_ref, held, mine, theirs, send_sem, recv_sem, cross_sem)


def scatter_blocks(parts_ref, out_ref, held, mine, theirs, send_sem, recv_sem, cross_sem):
    peers = lax.axis_size("dp")
    here = lax.axis_index("dp")
    row = lax.axis_index("section")
    partner = here - here % 2 + 1 - here % 2
    planes = peers // 2
    slot = here // 2
    side = here % 2

    def fan(peer, block):
        return group_copy(parts_ref.at[2 * (peer // 2) + block], held.at[slot, block],
                          send_sem.at[peer // 2, block], recv_sem.at[slot, block], row, peer)

    far = 1 - side

    def start_far(i, carry):
        fan(lax.rem(here + 2 * i, peers), far).start()
        return carry

    def start_near(i, carry):
        fan(lax.rem(here + 2 * i, peers), side).start()
        return carry

    lax.fori_loop(1, planes, start_far, 0)
    lax.fori_loop(1, planes, start_near, 0)

    def gather_block(block):
        def finish(i, total):
            peer = lax.rem(here + 2 * i, peers)
            fan(peer, block).wait_send()
            source = peer // 2
            group_copy(parts_ref.at[block], held.at[source, block], send_sem.at[source, block],
                       recv_sem.at[source, block], row, peer).wait_recv()
            return total + held[source, block].astype(jnp.float32)

        return lax.fori_loop(1, planes, finish, parts_ref[2 * slot + block].astype(jnp.float32))

    theirs[...] = gather_block(far)
    cross = group_copy(theirs, mine, cross_sem.at[0], cross_sem.at[1], row, partner)
    cross.start()
    own = gather_block(side)
    cross.wait_send()
    cross.wait_recv()
    out_ref[...] = own + mine[...]


def scatter_rows(parts):
    peers, rows, cols = parts.shape
    return pl.pallas_call(
        scatter_kernel,
        out_shape=jax.ShapeDtypeStruct((rows, cols), jnp.float32),
        in_specs=[pl.BlockSpec(memory_space=pltpu.VMEM)],
        out_specs=pl.BlockSpec(memory_space=pltpu.VMEM),
        scratch_shapes=[
            pltpu.VMEM((peers // 2, 2, rows, cols), parts.dtype),
            pltpu.VMEM((rows, cols), jnp.float32),
            pltpu.VMEM((rows, cols), jnp.float32),
            pltpu.SemaphoreType.DMA((peers // 2, 2)),
            pltpu.SemaphoreType.DMA((peers // 2, 2)),
            pltpu.SemaphoreType.DMA((2,)),
        ],
        compiler_params=pltpu.CompilerParams(collective_id=1, has_side_effects=True),
    )(parts)


def squash_into(pad_ref, activation):
    squashed = (activation / (1.0 + jnp.exp(-activation))).astype(jnp.bfloat16).astype(jnp.float32)
    field = squashed.reshape(pad_ref.shape[0] - 2, 8, 8, pad_ref.shape[-1])
    pad_ref[2:, 1:9, 1:9, :] = field
    pad_ref[0:2, 1:9, 1:9, :] = jnp.broadcast_to(field[0:1], (2,) + field.shape[1:])


def tap_windows(pad_ref, frames, flipped):
    channels = pad_ref.shape[-1]
    for c0 in range(3):
        shifted = pad_ref[:, :, c0 : c0 + 8, :]
        offset_col = 2 - c0 if flipped else c0
        for offset_time in range(3):
            for offset_row in range(3):
                t0 = 2 - offset_time if flipped else offset_time
                r0 = 2 - offset_row if flipped else offset_row
                window = shifted[t0 : t0 + frames, r0 : r0 + 8].reshape(frames * 64, channels)
                yield offset_time * 9 + offset_row * 3 + offset_col, window.astype(jnp.bfloat16)


def greet_line(here, count, col, settle=True):
    barrier = pltpu.get_barrier_semaphore()

    @pl.when(here > 0)
    def _():
        pl.semaphore_signal(barrier, inc=1, device_id=(here - 1, col), device_id_type=MESH_ID)

    @pl.when(here < count - 1)
    def _():
        pl.semaphore_signal(barrier, inc=1, device_id=(here + 1, col), device_id_type=MESH_ID)

    neighbours = (here + count - 1) // count + (2 * count - 2 - here) // count
    if settle:
        pl.semaphore_wait(barrier, neighbours)
    return neighbours


def line_copy(src, dst, send_sem, recv_sem, target, col):
    return pltpu.make_async_remote_copy(
        src_ref=src,
        dst_ref=dst,
        send_sem=send_sem,
        recv_sem=recv_sem,
        device_id=(target, col),
        device_id_type=MESH_ID,
    )


def forward_kernel(clips_ref, w_ref, seen_ref, out_ref, recv, pad, send_sem, recv_sem):
    count = lax.axis_size("section")
    here = lax.axis_index("section")
    col = lax.axis_index("dp")
    micro_count = clips_ref.shape[0]
    greet_line(here, count, col)
    pad[...] = jnp.zeros_like(pad)

    def step(m, carry):
        @pl.when(here == 0)
        def _():
            seen_ref[m] = clips_ref[m]

        @pl.when(here > 0)
        def _():
            line_copy(out_ref.at[m], recv.at[m], send_sem.at[m], recv_sem.at[m], here - 1, col).wait_recv()
            seen_ref[m] = recv[m]

        base = seen_ref[m].astype(jnp.float32)
        squash_into(pad, base)
        total = base
        for tap, window in tap_windows(pad, 4, False):
            total = total + jnp.dot(window, w_ref[tap], preferred_element_type=jnp.float32)
        out_ref[m] = total.astype(out_ref.dtype)

        @pl.when(here < count - 1)
        def _():
            line_copy(out_ref.at[m], recv.at[m], send_sem.at[m], recv_sem.at[m], here + 1, col).start()

        return carry

    lax.fori_loop(0, micro_count, step, 0)

    @pl.when(here < count - 1)
    def _():
        for m in range(micro_count):
            line_copy(out_ref.at[m], recv.at[m], send_sem.at[m], recv_sem.at[m], here + 1, col).wait_send()


def forward_line(clips_local, weight):
    shape = jax.ShapeDtypeStruct(clips_local.shape, clips_local.dtype)
    micro_count, cells, channels = clips_local.shape
    return pl.pallas_call(
        forward_kernel,
        out_shape=(shape, shape),
        in_specs=[pl.BlockSpec(memory_space=pltpu.VMEM)] * 2,
        out_specs=(pl.BlockSpec(memory_space=pltpu.VMEM),) * 2,
        scratch_shapes=[
            pltpu.VMEM(clips_local.shape, clips_local.dtype),
            pltpu.VMEM((cells // 64 + 2, 10, 10, channels), jnp.float32),
            pltpu.SemaphoreType.DMA((micro_count,)),
            pltpu.SemaphoreType.DMA((micro_count,)),
        ],
        compiler_params=pltpu.CompilerParams(collective_id=2, has_side_effects=True),
    )(clips_local, weight)


def backward_kernel(cot_ref, seen_ref, w_ref, share_ref, recv, sendbuf, pad, gpad, wg_ref, parts_ref, held, mine,
                    theirs, send_sem, recv_sem, share_send, share_recv, cross_sem):
    count = lax.axis_size("section")
    here = lax.axis_index("section")
    col = lax.axis_index("dp")
    micro_count = cot_ref.shape[0]
    greet_group(col, here, greet_line(here, count, col, settle=False))
    pad[...] = jnp.zeros_like(pad)
    gpad[...] = jnp.zeros_like(gpad)
    wg_ref[...] = jnp.zeros_like(wg_ref)

    def step(m, carry):
        @pl.when(here == count - 1)
        def _():
            recv[m] = cot_ref[m]

        @pl.when(here < count - 1)
        def _():
            line_copy(sendbuf.at[m], recv.at[m], send_sem.at[m], recv_sem.at[m], here + 1, col).wait_recv()

        upstream = recv[m]
        base = seen_ref[m].astype(jnp.float32)
        squash_into(pad, base)
        @pl.when(here > 0)
        def _():
            up = upstream.astype(jnp.float32)
            gpad[2:6, 1:9, 1:9, :] = up.reshape(4, 8, 8, up.shape[-1])
            spread = jnp.zeros((384, up.shape[-1]), jnp.float32)
            for tap, window in tap_windows(gpad, 6, True):
                spread = spread + lax.dot_general(
                    window, w_ref[tap], (((1,), (1,)), ((), ())),
                    preferred_element_type=jnp.float32,
                )
            field = jnp.concatenate([spread[0:64] + spread[64:128] + spread[128:192], spread[192:384]], axis=0)
            sig = 1.0 / (1.0 + jnp.exp(-base))
            slope = sig * (1.0 + base * (1.0 - sig))
            sendbuf[m] = (up + field * slope).astype(sendbuf.dtype)
            line_copy(sendbuf.at[m], recv.at[m], send_sem.at[m], recv_sem.at[m], here - 1, col).start()

        for tap, window in tap_windows(pad, 4, False):
            wg_ref[tap * 128 : (tap + 1) * 128, :] += lax.dot_general(
                window, upstream, (((0,), (0,)), ((), ())),
                preferred_element_type=jnp.float32,
            )
        return carry

    lax.fori_loop(0, micro_count, step, 0)

    block_rows = parts_ref.shape[1]
    for block in range(parts_ref.shape[0]):
        parts_ref[block] = wg_ref[block * block_rows : (block + 1) * block_rows, :].astype(parts_ref.dtype)

    @pl.when(here > 0)
    def _():
        for m in range(micro_count):
            line_copy(sendbuf.at[m], recv.at[m], send_sem.at[m], recv_sem.at[m], here - 1, col).wait_send()

    scatter_blocks(parts_ref, share_ref, held, mine, theirs, share_send, share_recv, cross_sem)


def backward_line(cot_local, seen, weight, blocks):
    micro_count, cells, channels = cot_local.shape
    taps = weight.shape[0]
    block_rows = taps * channels // blocks
    return pl.pallas_call(
        backward_kernel,
        out_shape=jax.ShapeDtypeStruct((block_rows, channels), jnp.float32),
        in_specs=[pl.BlockSpec(memory_space=pltpu.VMEM)] * 3,
        out_specs=pl.BlockSpec(memory_space=pltpu.VMEM),
        scratch_shapes=[
            pltpu.VMEM(cot_local.shape, cot_local.dtype),
            pltpu.VMEM(cot_local.shape, cot_local.dtype),
            pltpu.VMEM((cells // 64 + 2, 10, 10, channels), jnp.float32),
            pltpu.VMEM((cells // 64 + 4, 10, 10, channels), jnp.float32),
            pltpu.VMEM((taps * channels, channels), jnp.float32),
            pltpu.VMEM((blocks, block_rows, channels), jnp.bfloat16),
            pltpu.VMEM((blocks // 2, 2, block_rows, channels), jnp.bfloat16),
            pltpu.VMEM((block_rows, channels), jnp.float32),
            pltpu.VMEM((block_rows, channels), jnp.float32),
            pltpu.SemaphoreType.DMA((micro_count,)),
            pltpu.SemaphoreType.DMA((micro_count,)),
            pltpu.SemaphoreType.DMA((blocks // 2, 2)),
            pltpu.SemaphoreType.DMA((blocks // 2, 2)),
            pltpu.SemaphoreType.DMA((2,)),
        ],
        compiler_params=pltpu.CompilerParams(collective_id=3, has_side_effects=True),
    )(cot_local, seen, weight)


def per_device(clips, cotangent, weights):
    channels = weights.shape[-1]
    weight = gather_rows(weights[0]).reshape(-1, channels, channels)
    blocks = lax.axis_size("dp")
    micro_count = clips.shape[0]
    clips_local = clips[:, 0].reshape(micro_count, -1, channels)
    cot_local = cotangent[:, 0].reshape(micro_count, -1, channels)
    seen, produced = forward_line(clips_local, weight)
    grad_share = backward_line(cot_local, seen, weight, blocks)
    return (produced.reshape(clips[:, 0].shape)[None, :, None], grad_share[None])


def solution(mesh):
    placed = (
        P(None, "dp", None, None, None, None),
        P(None, "dp", None, None, None, None),
        P("section", "dp", None),
    )
    return jax.shard_map(
        per_device,
        mesh=mesh,
        in_specs=placed,
        out_specs=(P("section", None, "dp", None, None, None, None), P("section", "dp", None)),
        check_vma=False,
    )
```

```python
import jax
import jax.numpy as jnp
from jax import lax
from jax.sharding import PartitionSpec as P

from jax.experimental import pallas as pl
from jax.experimental.pallas import tpu as pltpu

MESH_ID = pl.DeviceIdType.MESH


def greet_group(here, row, extra=0):
    pair = here - here % 2
    partner = pair + 1 - here % 2
    barrier = pltpu.get_barrier_semaphore()
    pl.semaphore_signal(barrier, inc=1, device_id=(row, partner), device_id_type=MESH_ID)

    def signal(i, carry):
        peer = lax.rem(here + 2 * i, lax.axis_size("dp"))
        pl.semaphore_signal(barrier, inc=1, device_id=(row, peer), device_id_type=MESH_ID)
        return carry

    planes = lax.axis_size("dp") // 2
    lax.fori_loop(1, planes, signal, 0)
    pl.semaphore_wait(barrier, planes + extra)
    return partner


def group_copy(src, dst, send_sem, recv_sem, row, peer):
    return pltpu.make_async_remote_copy(
        src_ref=src,
        dst_ref=dst,
        send_sem=send_sem,
        recv_sem=recv_sem,
        device_id=(row, peer),
        device_id_type=MESH_ID,
    )


def gather_kernel(shard_ref, flat_ref, out_ref, send_sem, recv_sem):
    greet_group(lax.axis_index("dp"), lax.axis_index("section"))
    gather_blocks(shard_ref, flat_ref, out_ref, send_sem, recv_sem)


def gather_blocks(shard_ref, flat_ref, out_ref, send_sem, recv_sem):
    peers = lax.axis_size("dp")
    here = lax.axis_index("dp")
    row = lax.axis_index("section")
    partner = here - here % 2 + 1 - here % 2
    planes = peers // 2
    cross = group_copy(shard_ref, out_ref.at[here], send_sem.at[here], recv_sem.at[here], row, partner)
    cross.start()

    def fan(i, peer):
        own = group_copy(shard_ref, out_ref.at[here], send_sem.at[peer], recv_sem.at[here], row, peer)
        relayed = group_copy(out_ref.at[partner], out_ref.at[partner], send_sem.at[peer + 1 - 2 * (peer % 2)],
                             recv_sem.at[partner], row, peer)
        return own, relayed

    def start_own(i, carry):
        fan(i, lax.rem(here + 2 * i, peers))[0].start()
        return carry

    def start_relay(i, carry):
        fan(i, lax.rem(here + 2 * i, peers))[1].start()
        return carry

    lax.fori_loop(1, planes, start_own, 0)
    out_ref[here] = shard_ref[...]
    cross.wait_send()
    group_copy(shard_ref, out_ref.at[partner], send_sem.at[partner], recv_sem.at[partner], row, partner).wait_recv()
    lax.fori_loop(1, planes, start_relay, 0)

    def finish(i, carry):
        peer = lax.rem(here + 2 * i, peers)
        own, relayed = fan(i, peer)
        own.wait_send()
        relayed.wait_send()
        mate = peer + 1 - 2 * (peer % 2)
        group_copy(shard_ref, out_ref.at[peer], send_sem.at[peer], recv_sem.at[peer], row, peer).wait_recv()
        group_copy(shard_ref, out_ref.at[mate], send_sem.at[mate], recv_sem.at[mate], row, peer).wait_recv()
        return carry

    lax.fori_loop(1, planes, finish, 0)
    rows = shard_ref.shape[0]
    for block in range(peers):
        flat_ref[block * rows : (block + 1) * rows, :] = out_ref[block]


def gather_rows(shard):
    peers = lax.axis_size("dp")
    rows, cols = shard.shape
    return pl.pallas_call(
        gather_kernel,
        out_shape=jax.ShapeDtypeStruct((peers * rows, cols), shard.dtype),
        in_specs=[pl.BlockSpec(memory_space=pltpu.VMEM)],
        out_specs=pl.BlockSpec(memory_space=pltpu.VMEM),
        scratch_shapes=[
            pltpu.VMEM((peers, rows, cols), shard.dtype),
            pltpu.SemaphoreType.DMA((peers,)),
            pltpu.SemaphoreType.DMA((peers,)),
        ],
        compiler_params=pltpu.CompilerParams(collective_id=0, has_side_effects=True),
    )(shard)


def scatter_kernel(parts_ref, out_ref, held, mine, theirs, send_sem, recv_sem, cross_sem):
    greet_group(lax.axis_index("dp"), lax.axis_index("section"))
    scatter_blocks(parts_ref, out_ref, held, mine, theirs, send_sem, recv_sem, cross_sem)


def scatter_blocks(parts_ref, out_ref, held, mine, theirs, send_sem, recv_sem, cross_sem):
    peers = lax.axis_size("dp")
    here = lax.axis_index("dp")
    row = lax.axis_index("section")
    partner = here - here % 2 + 1 - here % 2
    planes = peers // 2
    slot = here // 2
    side = here % 2

    def fan(peer, block):
        return group_copy(parts_ref.at[2 * (peer // 2) + block], held.at[slot, block],
                          send_sem.at[peer // 2, block], recv_sem.at[slot, block], row, peer)

    far = 1 - side

    def start_far(i, carry):
        fan(lax.rem(here + 2 * i, peers), far).start()
        return carry

    def start_near(i, carry):
        fan(lax.rem(here + 2 * i, peers), side).start()
        return carry

    lax.fori_loop(1, planes, start_far, 0)
    lax.fori_loop(1, planes, start_near, 0)

    def gather_block(block):
        def finish(i, total):
            peer = lax.rem(here + 2 * i, peers)
            fan(peer, block).wait_send()
            source = peer // 2
            group_copy(parts_ref.at[block], held.at[source, block], send_sem.at[source, block],
                       recv_sem.at[source, block], row, peer).wait_recv()
            return total + held[source, block].astype(jnp.float32)

        return lax.fori_loop(1, planes, finish, parts_ref[2 * slot + block].astype(jnp.float32))

    theirs[...] = gather_block(far)
    cross = group_copy(theirs, mine, cross_sem.at[0], cross_sem.at[1], row, partner)
    cross.start()
    own = gather_block(side)
    cross.wait_send()
    cross.wait_recv()
    out_ref[...] = own + mine[...]


def scatter_rows(parts):
    peers, rows, cols = parts.shape
    return pl.pallas_call(
        scatter_kernel,
        out_shape=jax.ShapeDtypeStruct((rows, cols), jnp.float32),
        in_specs=[pl.BlockSpec(memory_space=pltpu.VMEM)],
        out_specs=pl.BlockSpec(memory_space=pltpu.VMEM),
        scratch_shapes=[
            pltpu.VMEM((peers // 2, 2, rows, cols), parts.dtype),
            pltpu.VMEM((rows, cols), jnp.float32),
            pltpu.VMEM((rows, cols), jnp.float32),
            pltpu.SemaphoreType.DMA((peers // 2, 2)),
            pltpu.SemaphoreType.DMA((peers // 2, 2)),
            pltpu.SemaphoreType.DMA((2,)),
        ],
        compiler_params=pltpu.CompilerParams(collective_id=1, has_side_effects=True),
    )(parts)


def squash_into(pad_ref, activation):
    squashed = (activation / (1.0 + jnp.exp(-activation))).astype(jnp.bfloat16).astype(jnp.float32)
    field = squashed.reshape(pad_ref.shape[0] - 2, 8, 8, pad_ref.shape[-1])
    pad_ref[2:, 1:9, 1:9, :] = field
    pad_ref[0:2, 1:9, 1:9, :] = jnp.broadcast_to(field[0:1], (2,) + field.shape[1:])


def tap_windows(pad_ref, frames, flipped):
    channels = pad_ref.shape[-1]
    for c0 in range(3):
        shifted = pad_ref[:, :, c0 : c0 + 8, :]
        offset_col = 2 - c0 if flipped else c0
        for offset_time in range(3):
            for offset_row in range(3):
                t0 = 2 - offset_time if flipped else offset_time
                r0 = 2 - offset_row if flipped else offset_row
                window = shifted[t0 : t0 + frames, r0 : r0 + 8].reshape(frames * 64, channels)
                yield offset_time * 9 + offset_row * 3 + offset_col, window.astype(jnp.bfloat16)


def greet_line(here, count, col, settle=True):
    barrier = pltpu.get_barrier_semaphore()

    @pl.when(here > 0)
    def _():
        pl.semaphore_signal(barrier, inc=1, device_id=(here - 1, col), device_id_type=MESH_ID)

    @pl.when(here < count - 1)
    def _():
        pl.semaphore_signal(barrier, inc=1, device_id=(here + 1, col), device_id_type=MESH_ID)

    neighbours = (here + count - 1) // count + (2 * count - 2 - here) // count
    if settle:
        pl.semaphore_wait(barrier, neighbours)
    return neighbours


def line_copy(src, dst, send_sem, recv_sem, target, col):
    return pltpu.make_async_remote_copy(
        src_ref=src,
        dst_ref=dst,
        send_sem=send_sem,
        recv_sem=recv_sem,
        device_id=(target, col),
        device_id_type=MESH_ID,
    )


def forward_kernel(clips_ref, shard_ref, seen_ref, out_ref, flat_ref, recv, pad, blocks, gather_send, gather_recv,
                   send_sem, recv_sem):
    count = lax.axis_size("section")
    here = lax.axis_index("section")
    col = lax.axis_index("dp")
    micro_count = clips_ref.shape[0]
    greet_group(col, here, greet_line(here, count, col, settle=False))
    pad[...] = jnp.zeros_like(pad)
    gather_blocks(shard_ref, flat_ref, blocks, gather_send, gather_recv)
    channels = flat_ref.shape[-1]

    def step(m, carry):
        @pl.when(here == 0)
        def _():
            seen_ref[m] = clips_ref[m]

        @pl.when(here > 0)
        def _():
            line_copy(out_ref.at[m], recv.at[m], send_sem.at[m], recv_sem.at[m], here - 1, col).wait_recv()
            seen_ref[m] = recv[m]

        base = seen_ref[m].astype(jnp.float32)
        squash_into(pad, base)
        total = base
        for tap, window in tap_windows(pad, 4, False):
            total = total + jnp.dot(
                window, flat_ref[tap * channels : (tap + 1) * channels, :], preferred_element_type=jnp.float32
            )
        out_ref[m] = total.astype(out_ref.dtype)

        @pl.when(here < count - 1)
        def _():
            line_copy(out_ref.at[m], recv.at[m], send_sem.at[m], recv_sem.at[m], here + 1, col).start()

        return carry

    lax.fori_loop(0, micro_count, step, 0)

    @pl.when(here < count - 1)
    def _():
        for m in range(micro_count):
            line_copy(out_ref.at[m], recv.at[m], send_sem.at[m], recv_sem.at[m], here + 1, col).wait_send()


def forward_line(clips_local, shard):
    shape = jax.ShapeDtypeStruct(clips_local.shape, clips_local.dtype)
    micro_count, cells, channels = clips_local.shape
    peers = lax.axis_size("dp")
    rows = shard.shape[0]
    return pl.pallas_call(
        forward_kernel,
        out_shape=(shape, shape, jax.ShapeDtypeStruct((peers * rows, channels), shard.dtype)),
        in_specs=[pl.BlockSpec(memory_space=pltpu.VMEM)] * 2,
        out_specs=(pl.BlockSpec(memory_space=pltpu.VMEM),) * 3,
        scratch_shapes=[
            pltpu.VMEM(clips_local.shape, clips_local.dtype),
            pltpu.VMEM((cells // 64 + 2, 10, 10, channels), jnp.float32),
            pltpu.VMEM((peers, rows, channels), shard.dtype),
            pltpu.SemaphoreType.DMA((peers,)),
            pltpu.SemaphoreType.DMA((peers,)),
            pltpu.SemaphoreType.DMA((micro_count,)),
            pltpu.SemaphoreType.DMA((micro_count,)),
        ],
        compiler_params=pltpu.CompilerParams(collective_id=2, has_side_effects=True),
    )(clips_local, shard)


def backward_kernel(cot_ref, seen_ref, w_ref, share_ref, recv, sendbuf, pad, gpad, wg_ref, parts_ref, held, mine,
                    theirs, send_sem, recv_sem, share_send, share_recv, cross_sem):
    count = lax.axis_size("section")
    here = lax.axis_index("section")
    col = lax.axis_index("dp")
    micro_count = cot_ref.shape[0]
    greet_group(col, here, greet_line(here, count, col, settle=False))
    pad[...] = jnp.zeros_like(pad)
    gpad[...] = jnp.zeros_like(gpad)
    wg_ref[...] = jnp.zeros_like(wg_ref)

    def step(m, carry):
        @pl.when(here == count - 1)
        def _():
            recv[m] = cot_ref[m]

        @pl.when(here < count - 1)
        def _():
            line_copy(sendbuf.at[m], recv.at[m], send_sem.at[m], recv_sem.at[m], here + 1, col).wait_recv()

        upstream = recv[m]
        base = seen_ref[m].astype(jnp.float32)
        squash_into(pad, base)
        @pl.when(here > 0)
        def _():
            up = upstream.astype(jnp.float32)
            gpad[2:6, 1:9, 1:9, :] = up.reshape(4, 8, 8, up.shape[-1])
            spread = jnp.zeros((384, up.shape[-1]), jnp.float32)
            for tap, window in tap_windows(gpad, 6, True):
                spread = spread + lax.dot_general(
                    window, w_ref[tap], (((1,), (1,)), ((), ())),
                    preferred_element_type=jnp.float32,
                )
            field = jnp.concatenate([spread[0:64] + spread[64:128] + spread[128:192], spread[192:384]], axis=0)
            sig = 1.0 / (1.0 + jnp.exp(-base))
            slope = sig * (1.0 + base * (1.0 - sig))
            sendbuf[m] = (up + field * slope).astype(sendbuf.dtype)
            line_copy(sendbuf.at[m], recv.at[m], send_sem.at[m], recv_sem.at[m], here - 1, col).start()

        for tap, window in tap_windows(pad, 4, False):
            wg_ref[tap * 128 : (tap + 1) * 128, :] += lax.dot_general(
                window, upstream, (((0,), (0,)), ((), ())),
                preferred_element_type=jnp.float32,
            )
        return carry

    lax.fori_loop(0, micro_count, step, 0)

    block_rows = parts_ref.shape[1]
    for block in range(parts_ref.shape[0]):
        parts_ref[block] = wg_ref[block * block_rows : (block + 1) * block_rows, :].astype(parts_ref.dtype)

    @pl.when(here > 0)
    def _():
        for m in range(micro_count):
            line_copy(sendbuf.at[m], recv.at[m], send_sem.at[m], recv_sem.at[m], here - 1, col).wait_send()

    scatter_blocks(parts_ref, share_ref, held, mine, theirs, share_send, share_recv, cross_sem)


def backward_line(cot_local, seen, weight, blocks):
    micro_count, cells, channels = cot_local.shape
    taps = weight.shape[0]
    block_rows = taps * channels // blocks
    return pl.pallas_call(
        backward_kernel,
        out_shape=jax.ShapeDtypeStruct((block_rows, channels), jnp.float32),
        in_specs=[pl.BlockSpec(memory_space=pltpu.VMEM)] * 3,
        out_specs=pl.BlockSpec(memory_space=pltpu.VMEM),
        scratch_shapes=[
            pltpu.VMEM(cot_local.shape, cot_local.dtype),
            pltpu.VMEM(cot_local.shape, cot_local.dtype),
            pltpu.VMEM((cells // 64 + 2, 10, 10, channels), jnp.float32),
            pltpu.VMEM((cells // 64 + 4, 10, 10, channels), jnp.float32),
            pltpu.VMEM((taps * channels, channels), jnp.float32),
            pltpu.VMEM((blocks, block_rows, channels), jnp.bfloat16),
            pltpu.VMEM((blocks // 2, 2, block_rows, channels), jnp.bfloat16),
            pltpu.VMEM((block_rows, channels), jnp.float32),
            pltpu.VMEM((block_rows, channels), jnp.float32),
            pltpu.SemaphoreType.DMA((micro_count,)),
            pltpu.SemaphoreType.DMA((micro_count,)),
            pltpu.SemaphoreType.DMA((blocks // 2, 2)),
            pltpu.SemaphoreType.DMA((blocks // 2, 2)),
            pltpu.SemaphoreType.DMA((2,)),
        ],
        compiler_params=pltpu.CompilerParams(collective_id=3, has_side_effects=True),
    )(cot_local, seen, weight)


def per_device(clips, cotangent, weights):
    channels = weights.shape[-1]
    blocks = lax.axis_size("dp")
    micro_count = clips.shape[0]
    clips_local = clips[:, 0].reshape(micro_count, -1, channels)
    cot_local = cotangent[:, 0].reshape(micro_count, -1, channels)
    seen, produced, weight = forward_line(clips_local, weights[0])
    weight = weight.reshape(-1, channels, channels)
    grad_share = backward_line(cot_local, seen, weight, blocks)
    return (produced.reshape(clips[:, 0].shape)[None, :, None], grad_share[None])


def solution(mesh):
    placed = (
        P(None, "dp", None, None, None, None),
        P(None, "dp", None, None, None, None),
        P("section", "dp", None),
    )
    return jax.shard_map(
        per_device,
        mesh=mesh,
        in_specs=placed,
        out_specs=(P("section", None, "dp", None, None, None, None), P("section", "dp", None)),
        check_vma=False,
    )
```

```python
import jax
import jax.numpy as jnp
from jax import lax
from jax.sharding import PartitionSpec as P

from jax.experimental import pallas as pl
from jax.experimental.pallas import tpu as pltpu

MESH_ID = pl.DeviceIdType.MESH


def greet_group(here, row, extra=0):
    pair = here - here % 2
    partner = pair + 1 - here % 2
    barrier = pltpu.get_barrier_semaphore()
    pl.semaphore_signal(barrier, inc=1, device_id=(row, partner), device_id_type=MESH_ID)

    def signal(i, carry):
        peer = lax.rem(here + 2 * i, lax.axis_size("dp"))
        pl.semaphore_signal(barrier, inc=1, device_id=(row, peer), device_id_type=MESH_ID)
        return carry

    planes = lax.axis_size("dp") // 2
    lax.fori_loop(1, planes, signal, 0)
    pl.semaphore_wait(barrier, planes + extra)
    return partner


def group_copy(src, dst, send_sem, recv_sem, row, peer):
    return pltpu.make_async_remote_copy(
        src_ref=src,
        dst_ref=dst,
        send_sem=send_sem,
        recv_sem=recv_sem,
        device_id=(row, peer),
        device_id_type=MESH_ID,
    )


def gather_kernel(shard_ref, flat_ref, out_ref, send_sem, recv_sem):
    greet_group(lax.axis_index("dp"), lax.axis_index("section"))
    gather_blocks(shard_ref, flat_ref, out_ref, send_sem, recv_sem)


def gather_blocks(shard_ref, flat_ref, out_ref, send_sem, recv_sem):
    peers = lax.axis_size("dp")
    here = lax.axis_index("dp")
    row = lax.axis_index("section")
    partner = here - here % 2 + 1 - here % 2
    planes = peers // 2
    cross = group_copy(shard_ref, out_ref.at[here], send_sem.at[here], recv_sem.at[here], row, partner)
    cross.start()

    def fan(i, peer):
        own = group_copy(shard_ref, out_ref.at[here], send_sem.at[peer], recv_sem.at[here], row, peer)
        relayed = group_copy(out_ref.at[partner], out_ref.at[partner], send_sem.at[peer + 1 - 2 * (peer % 2)],
                             recv_sem.at[partner], row, peer)
        return own, relayed

    def start_own(i, carry):
        fan(i, lax.rem(here + 2 * i, peers))[0].start()
        return carry

    def start_relay(i, carry):
        fan(i, lax.rem(here + 2 * i, peers))[1].start()
        return carry

    lax.fori_loop(1, planes, start_own, 0)
    out_ref[here] = shard_ref[...]
    cross.wait_send()
    group_copy(shard_ref, out_ref.at[partner], send_sem.at[partner], recv_sem.at[partner], row, partner).wait_recv()
    lax.fori_loop(1, planes, start_relay, 0)

    def finish(i, carry):
        peer = lax.rem(here + 2 * i, peers)
        own, relayed = fan(i, peer)
        own.wait_send()
        relayed.wait_send()
        mate = peer + 1 - 2 * (peer % 2)
        group_copy(shard_ref, out_ref.at[peer], send_sem.at[peer], recv_sem.at[peer], row, peer).wait_recv()
        group_copy(shard_ref, out_ref.at[mate], send_sem.at[mate], recv_sem.at[mate], row, peer).wait_recv()
        return carry

    lax.fori_loop(1, planes, finish, 0)
    rows = shard_ref.shape[0]
    for block in range(peers):
        flat_ref[block * rows : (block + 1) * rows, :] = out_ref[block]


def gather_rows(shard):
    peers = lax.axis_size("dp")
    rows, cols = shard.shape
    return pl.pallas_call(
        gather_kernel,
        out_shape=jax.ShapeDtypeStruct((peers * rows, cols), shard.dtype),
        in_specs=[pl.BlockSpec(memory_space=pltpu.VMEM)],
        out_specs=pl.BlockSpec(memory_space=pltpu.VMEM),
        scratch_shapes=[
            pltpu.VMEM((peers, rows, cols), shard.dtype),
            pltpu.SemaphoreType.DMA((peers,)),
            pltpu.SemaphoreType.DMA((peers,)),
        ],
        compiler_params=pltpu.CompilerParams(collective_id=0, has_side_effects=True),
    )(shard)


def scatter_kernel(parts_ref, out_ref, held, mine, theirs, send_sem, recv_sem, cross_sem):
    greet_group(lax.axis_index("dp"), lax.axis_index("section"))
    scatter_blocks(parts_ref, out_ref, held, mine, theirs, send_sem, recv_sem, cross_sem)


def scatter_blocks(parts_ref, out_ref, held, mine, theirs, send_sem, recv_sem, cross_sem):
    peers = lax.axis_size("dp")
    here = lax.axis_index("dp")
    row = lax.axis_index("section")
    partner = here - here % 2 + 1 - here % 2
    planes = peers // 2
    slot = here // 2
    side = here % 2

    def fan(peer, block):
        return group_copy(parts_ref.at[2 * (peer // 2) + block], held.at[slot, block],
                          send_sem.at[peer // 2, block], recv_sem.at[slot, block], row, peer)

    far = 1 - side

    def start_far(i, carry):
        fan(lax.rem(here + 2 * i, peers), far).start()
        return carry

    def start_near(i, carry):
        fan(lax.rem(here + 2 * i, peers), side).start()
        return carry

    lax.fori_loop(1, planes, start_far, 0)
    lax.fori_loop(1, planes, start_near, 0)

    def gather_block(block):
        def finish(i, total):
            peer = lax.rem(here + 2 * i, peers)
            fan(peer, block).wait_send()
            source = peer // 2
            group_copy(parts_ref.at[block], held.at[source, block], send_sem.at[source, block],
                       recv_sem.at[source, block], row, peer).wait_recv()
            return total + held[source, block].astype(jnp.float32)

        return lax.fori_loop(1, planes, finish, parts_ref[2 * slot + block].astype(jnp.float32))

    theirs[...] = gather_block(far)
    cross = group_copy(theirs, mine, cross_sem.at[0], cross_sem.at[1], row, partner)
    cross.start()
    own = gather_block(side)
    cross.wait_send()
    cross.wait_recv()
    out_ref[...] = (own + mine[...]).reshape(out_ref.shape)


def scatter_rows(parts):
    peers, rows, cols = parts.shape
    return pl.pallas_call(
        scatter_kernel,
        out_shape=jax.ShapeDtypeStruct((rows, cols), jnp.float32),
        in_specs=[pl.BlockSpec(memory_space=pltpu.VMEM)],
        out_specs=pl.BlockSpec(memory_space=pltpu.VMEM),
        scratch_shapes=[
            pltpu.VMEM((peers // 2, 2, rows, cols), parts.dtype),
            pltpu.VMEM((rows, cols), jnp.float32),
            pltpu.VMEM((rows, cols), jnp.float32),
            pltpu.SemaphoreType.DMA((peers // 2, 2)),
            pltpu.SemaphoreType.DMA((peers // 2, 2)),
            pltpu.SemaphoreType.DMA((2,)),
        ],
        compiler_params=pltpu.CompilerParams(collective_id=1, has_side_effects=True),
    )(parts)


def squash_into(pad_ref, activation):
    squashed = (activation / (1.0 + jnp.exp(-activation))).astype(jnp.bfloat16).astype(jnp.float32)
    field = squashed.reshape(pad_ref.shape[0] - 2, 8, 8, pad_ref.shape[-1])
    pad_ref[2:, 1:9, 1:9, :] = field
    pad_ref[0:2, 1:9, 1:9, :] = jnp.broadcast_to(field[0:1], (2,) + field.shape[1:])


def tap_windows(pad_ref, frames, flipped):
    channels = pad_ref.shape[-1]
    for c0 in range(3):
        shifted = pad_ref[:, :, c0 : c0 + 8, :]
        offset_col = 2 - c0 if flipped else c0
        for offset_time in range(3):
            for offset_row in range(3):
                t0 = 2 - offset_time if flipped else offset_time
                r0 = 2 - offset_row if flipped else offset_row
                window = shifted[t0 : t0 + frames, r0 : r0 + 8].reshape(frames * 64, channels)
                yield offset_time * 9 + offset_row * 3 + offset_col, window.astype(jnp.bfloat16)


def greet_line(here, count, col, settle=True):
    barrier = pltpu.get_barrier_semaphore()

    @pl.when(here > 0)
    def _():
        pl.semaphore_signal(barrier, inc=1, device_id=(here - 1, col), device_id_type=MESH_ID)

    @pl.when(here < count - 1)
    def _():
        pl.semaphore_signal(barrier, inc=1, device_id=(here + 1, col), device_id_type=MESH_ID)

    neighbours = (here + count - 1) // count + (2 * count - 2 - here) // count
    if settle:
        pl.semaphore_wait(barrier, neighbours)
    return neighbours


def line_copy(src, dst, send_sem, recv_sem, target, col):
    return pltpu.make_async_remote_copy(
        src_ref=src,
        dst_ref=dst,
        send_sem=send_sem,
        recv_sem=recv_sem,
        device_id=(target, col),
        device_id_type=MESH_ID,
    )


def forward_kernel(clips_ref, shard_ref, seen_ref, out_ref, flat_ref, recv, pad, blocks, gather_send, gather_recv,
                   send_sem, recv_sem):
    count = lax.axis_size("section")
    here = lax.axis_index("section")
    col = lax.axis_index("dp")
    micro_count = clips_ref.shape[0]
    greet_group(col, here, greet_line(here, count, col, settle=False))
    pad[...] = jnp.zeros_like(pad)
    gather_blocks(shard_ref, flat_ref, blocks, gather_send, gather_recv)
    channels = flat_ref.shape[-1]

    def step(m, carry):
        @pl.when(here == 0)
        def _():
            seen_ref[m] = clips_ref[m]

        @pl.when(here > 0)
        def _():
            line_copy(out_ref.at[m], recv.at[m], send_sem.at[m], recv_sem.at[m], here - 1, col).wait_recv()
            seen_ref[m] = recv[m]

        base = seen_ref[m].astype(jnp.float32)
        squash_into(pad, base)
        total = base
        for tap, window in tap_windows(pad, 4, False):
            total = total + jnp.dot(
                window, flat_ref[tap * channels : (tap + 1) * channels, :], preferred_element_type=jnp.float32
            )
        out_ref[m] = total.astype(out_ref.dtype)

        @pl.when(here < count - 1)
        def _():
            line_copy(out_ref.at[m], recv.at[m], send_sem.at[m], recv_sem.at[m], here + 1, col).start()

        return carry

    lax.fori_loop(0, micro_count, step, 0)

    @pl.when(here < count - 1)
    def _():
        for m in range(micro_count):
            line_copy(out_ref.at[m], recv.at[m], send_sem.at[m], recv_sem.at[m], here + 1, col).wait_send()


def forward_line(clips_local, shard):
    shape = jax.ShapeDtypeStruct(clips_local.shape, clips_local.dtype)
    micro_count, cells, channels = clips_local.shape
    peers = lax.axis_size("dp")
    rows = shard.shape[0]
    return pl.pallas_call(
        forward_kernel,
        out_shape=(shape, shape, jax.ShapeDtypeStruct((peers * rows, channels), shard.dtype)),
        in_specs=[pl.BlockSpec(memory_space=pltpu.VMEM)] * 2,
        out_specs=(pl.BlockSpec(memory_space=pltpu.VMEM),) * 3,
        scratch_shapes=[
            pltpu.VMEM(clips_local.shape, clips_local.dtype),
            pltpu.VMEM((cells // 64 + 2, 10, 10, channels), jnp.float32),
            pltpu.VMEM((peers, rows, channels), shard.dtype),
            pltpu.SemaphoreType.DMA((peers,)),
            pltpu.SemaphoreType.DMA((peers,)),
            pltpu.SemaphoreType.DMA((micro_count,)),
            pltpu.SemaphoreType.DMA((micro_count,)),
        ],
        compiler_params=pltpu.CompilerParams(collective_id=2, has_side_effects=True),
    )(clips_local, shard)


def backward_kernel(cot_ref, seen_ref, w_ref, share_ref, recv, sendbuf, pad, gpad, wg_ref, parts_ref, held, mine,
                    theirs, send_sem, recv_sem, share_send, share_recv, cross_sem):
    count = lax.axis_size("section")
    here = lax.axis_index("section")
    col = lax.axis_index("dp")
    micro_count = cot_ref.shape[0]
    greet_group(col, here, greet_line(here, count, col, settle=False))
    pad[...] = jnp.zeros_like(pad)
    gpad[...] = jnp.zeros_like(gpad)
    wg_ref[...] = jnp.zeros_like(wg_ref)

    def step(m, carry):
        @pl.when(here == count - 1)
        def _():
            recv[m] = cot_ref[m]

        @pl.when(here < count - 1)
        def _():
            line_copy(sendbuf.at[m], recv.at[m], send_sem.at[m], recv_sem.at[m], here + 1, col).wait_recv()

        upstream = recv[m]
        base = seen_ref[m].astype(jnp.float32)
        squash_into(pad, base)
        @pl.when(here > 0)
        def _():
            up = upstream.astype(jnp.float32)
            gpad[2:6, 1:9, 1:9, :] = up.reshape(4, 8, 8, up.shape[-1])
            spread = jnp.zeros((384, up.shape[-1]), jnp.float32)
            for tap, window in tap_windows(gpad, 6, True):
                spread = spread + lax.dot_general(
                    window, w_ref[tap], (((1,), (1,)), ((), ())),
                    preferred_element_type=jnp.float32,
                )
            field = jnp.concatenate([spread[0:64] + spread[64:128] + spread[128:192], spread[192:384]], axis=0)
            sig = 1.0 / (1.0 + jnp.exp(-base))
            slope = sig * (1.0 + base * (1.0 - sig))
            sendbuf[m] = (up + field * slope).astype(sendbuf.dtype)
            line_copy(sendbuf.at[m], recv.at[m], send_sem.at[m], recv_sem.at[m], here - 1, col).start()

        for tap, window in tap_windows(pad, 4, False):
            wg_ref[tap * 128 : (tap + 1) * 128, :] += lax.dot_general(
                window, upstream, (((0,), (0,)), ((), ())),
                preferred_element_type=jnp.float32,
            )
        return carry

    lax.fori_loop(0, micro_count, step, 0)

    block_rows = parts_ref.shape[1]
    for block in range(parts_ref.shape[0]):
        parts_ref[block] = wg_ref[block * block_rows : (block + 1) * block_rows, :].astype(parts_ref.dtype)

    @pl.when(here > 0)
    def _():
        for m in range(micro_count):
            line_copy(sendbuf.at[m], recv.at[m], send_sem.at[m], recv_sem.at[m], here - 1, col).wait_send()

    scatter_blocks(parts_ref, share_ref, held, mine, theirs, share_send, share_recv, cross_sem)


def backward_line(cot_local, seen, weight, blocks):
    micro_count, cells, channels = cot_local.shape
    taps = weight.shape[0]
    block_rows = taps * channels // blocks
    return pl.pallas_call(
        backward_kernel,
        out_shape=jax.ShapeDtypeStruct((block_rows, 1, channels), jnp.float32),
        in_specs=[pl.BlockSpec(memory_space=pltpu.VMEM)] * 3,
        out_specs=pl.BlockSpec(memory_space=pltpu.VMEM),
        scratch_shapes=[
            pltpu.VMEM(cot_local.shape, cot_local.dtype),
            pltpu.VMEM(cot_local.shape, cot_local.dtype),
            pltpu.VMEM((cells // 64 + 2, 10, 10, channels), jnp.float32),
            pltpu.VMEM((cells // 64 + 4, 10, 10, channels), jnp.float32),
            pltpu.VMEM((taps * channels, channels), jnp.float32),
            pltpu.VMEM((blocks, block_rows, channels), jnp.bfloat16),
            pltpu.VMEM((blocks // 2, 2, block_rows, channels), jnp.bfloat16),
            pltpu.VMEM((block_rows, channels), jnp.float32),
            pltpu.VMEM((block_rows, channels), jnp.float32),
            pltpu.SemaphoreType.DMA((micro_count,)),
            pltpu.SemaphoreType.DMA((micro_count,)),
            pltpu.SemaphoreType.DMA((blocks // 2, 2)),
            pltpu.SemaphoreType.DMA((blocks // 2, 2)),
            pltpu.SemaphoreType.DMA((2,)),
        ],
        compiler_params=pltpu.CompilerParams(collective_id=3, has_side_effects=True),
    )(cot_local, seen, weight)


def per_device(clips, cotangent, weights):
    channels = weights.shape[-1]
    blocks = lax.axis_size("dp")
    micro_count = clips.shape[0]
    clips_local = clips[:, 0].reshape(micro_count, -1, channels)
    cot_local = cotangent[:, 0].reshape(micro_count, -1, channels)
    seen, produced, weight = forward_line(clips_local, weights[0])
    weight = weight.reshape(-1, channels, channels)
    grad_share = backward_line(cot_local, seen, weight, blocks)
    return (produced.reshape(clips[:, 0].shape)[None, :, None], grad_share.reshape((1,) + grad_share.shape[::2]))


def solution(mesh):
    placed = (
        P(None, "dp", None, None, None, None),
        P(None, "dp", None, None, None, None),
        P("section", "dp", None),
    )
    return jax.shard_map(
        per_device,
        mesh=mesh,
        in_specs=placed,
        out_specs=(P("section", None, "dp", None, None, None, None), P("section", "dp", None)),
        check_vma=False,
    )
```

```python
import jax
import jax.numpy as jnp
from jax import lax
from jax.sharding import PartitionSpec as P

from jax.experimental import pallas as pl
from jax.experimental.pallas import tpu as pltpu

MESH_ID = pl.DeviceIdType.MESH


def greet_group(here, row, extra=0):
    pair = here - here % 2
    partner = pair + 1 - here % 2
    barrier = pltpu.get_barrier_semaphore()
    pl.semaphore_signal(barrier, inc=1, device_id=(row, partner), device_id_type=MESH_ID)

    def signal(i, carry):
        peer = lax.rem(here + 2 * i, lax.axis_size("dp"))
        pl.semaphore_signal(barrier, inc=1, device_id=(row, peer), device_id_type=MESH_ID)
        return carry

    planes = lax.axis_size("dp") // 2
    lax.fori_loop(1, planes, signal, 0)
    pl.semaphore_wait(barrier, planes + extra)
    return partner


def group_copy(src, dst, send_sem, recv_sem, row, peer):
    return pltpu.make_async_remote_copy(
        src_ref=src,
        dst_ref=dst,
        send_sem=send_sem,
        recv_sem=recv_sem,
        device_id=(row, peer),
        device_id_type=MESH_ID,
    )


def gather_kernel(shard_ref, flat_ref, out_ref, send_sem, recv_sem):
    greet_group(lax.axis_index("dp"), lax.axis_index("section"))
    gather_blocks(shard_ref, flat_ref, out_ref, send_sem, recv_sem)


def gather_blocks(shard_ref, flat_ref, out_ref, send_sem, recv_sem):
    peers = lax.axis_size("dp")
    here = lax.axis_index("dp")
    row = lax.axis_index("section")
    partner = here - here % 2 + 1 - here % 2
    planes = peers // 2
    cross = group_copy(shard_ref, out_ref.at[here], send_sem.at[here], recv_sem.at[here], row, partner)
    cross.start()

    def fan(i, peer):
        own = group_copy(shard_ref, out_ref.at[here], send_sem.at[peer], recv_sem.at[here], row, peer)
        relayed = group_copy(out_ref.at[partner], out_ref.at[partner], send_sem.at[peer + 1 - 2 * (peer % 2)],
                             recv_sem.at[partner], row, peer)
        return own, relayed

    def start_own(i, carry):
        fan(i, lax.rem(here + 2 * i, peers))[0].start()
        return carry

    def start_relay(i, carry):
        fan(i, lax.rem(here + 2 * i, peers))[1].start()
        return carry

    lax.fori_loop(1, planes, start_own, 0)
    out_ref[here] = shard_ref[...]
    cross.wait_send()
    group_copy(shard_ref, out_ref.at[partner], send_sem.at[partner], recv_sem.at[partner], row, partner).wait_recv()
    lax.fori_loop(1, planes, start_relay, 0)

    def finish(i, carry):
        peer = lax.rem(here + 2 * i, peers)
        own, relayed = fan(i, peer)
        own.wait_send()
        relayed.wait_send()
        mate = peer + 1 - 2 * (peer % 2)
        group_copy(shard_ref, out_ref.at[peer], send_sem.at[peer], recv_sem.at[peer], row, peer).wait_recv()
        group_copy(shard_ref, out_ref.at[mate], send_sem.at[mate], recv_sem.at[mate], row, peer).wait_recv()
        return carry

    lax.fori_loop(1, planes, finish, 0)
    rows = shard_ref.shape[0]
    for block in range(peers):
        flat_ref[block * rows : (block + 1) * rows, :] = out_ref[block]


def gather_rows(shard):
    peers = lax.axis_size("dp")
    rows, cols = shard.shape
    return pl.pallas_call(
        gather_kernel,
        out_shape=jax.ShapeDtypeStruct((peers * rows, cols), shard.dtype),
        in_specs=[pl.BlockSpec(memory_space=pltpu.VMEM)],
        out_specs=pl.BlockSpec(memory_space=pltpu.VMEM),
        scratch_shapes=[
            pltpu.VMEM((peers, rows, cols), shard.dtype),
            pltpu.SemaphoreType.DMA((peers,)),
            pltpu.SemaphoreType.DMA((peers,)),
        ],
        compiler_params=pltpu.CompilerParams(collective_id=0, has_side_effects=True),
    )(shard)


def scatter_kernel(parts_ref, out_ref, held, mine, theirs, send_sem, recv_sem, cross_sem):
    greet_group(lax.axis_index("dp"), lax.axis_index("section"))
    scatter_blocks(parts_ref, out_ref, held, mine, theirs, send_sem, recv_sem, cross_sem)


def scatter_blocks(parts_ref, out_ref, held, mine, theirs, send_sem, recv_sem, cross_sem):
    peers = lax.axis_size("dp")
    here = lax.axis_index("dp")
    row = lax.axis_index("section")
    partner = here - here % 2 + 1 - here % 2
    planes = peers // 2
    slot = here // 2
    side = here % 2

    def fan(peer, block):
        return group_copy(parts_ref.at[2 * (peer // 2) + block], held.at[slot, block],
                          send_sem.at[peer // 2, block], recv_sem.at[slot, block], row, peer)

    far = 1 - side

    def start_far(i, carry):
        fan(lax.rem(here + 2 * i, peers), far).start()
        return carry

    def start_near(i, carry):
        fan(lax.rem(here + 2 * i, peers), side).start()
        return carry

    lax.fori_loop(1, planes, start_far, 0)
    lax.fori_loop(1, planes, start_near, 0)

    def gather_block(block):
        def finish(i, total):
            peer = lax.rem(here + 2 * i, peers)
            fan(peer, block).wait_send()
            source = peer // 2
            group_copy(parts_ref.at[block], held.at[source, block], send_sem.at[source, block],
                       recv_sem.at[source, block], row, peer).wait_recv()
            return total + held[source, block].astype(jnp.float32)

        return lax.fori_loop(1, planes, finish, parts_ref[2 * slot + block].astype(jnp.float32))

    theirs[...] = gather_block(far)
    cross = group_copy(theirs, mine, cross_sem.at[0], cross_sem.at[1], row, partner)
    cross.start()
    own = gather_block(side)
    cross.wait_send()
    cross.wait_recv()
    out_ref[...] = (own + mine[...]).reshape(out_ref.shape)


def scatter_rows(parts):
    peers, rows, cols = parts.shape
    return pl.pallas_call(
        scatter_kernel,
        out_shape=jax.ShapeDtypeStruct((rows, cols), jnp.float32),
        in_specs=[pl.BlockSpec(memory_space=pltpu.VMEM)],
        out_specs=pl.BlockSpec(memory_space=pltpu.VMEM),
        scratch_shapes=[
            pltpu.VMEM((peers // 2, 2, rows, cols), parts.dtype),
            pltpu.VMEM((rows, cols), jnp.float32),
            pltpu.VMEM((rows, cols), jnp.float32),
            pltpu.SemaphoreType.DMA((peers // 2, 2)),
            pltpu.SemaphoreType.DMA((peers // 2, 2)),
            pltpu.SemaphoreType.DMA((2,)),
        ],
        compiler_params=pltpu.CompilerParams(collective_id=1, has_side_effects=True),
    )(parts)


def squash_into(pad_ref, activation):
    squashed = (activation / (1.0 + jnp.exp(-activation))).astype(jnp.bfloat16).astype(jnp.float32)
    field = squashed.reshape(pad_ref.shape[0] - 2, 8, 8, pad_ref.shape[-1])
    pad_ref[2:, 1:9, 1:9, :] = field
    pad_ref[0:2, 1:9, 1:9, :] = jnp.broadcast_to(field[0:1], (2,) + field.shape[1:])


def tap_windows(pad_ref, frames, flipped):
    channels = pad_ref.shape[-1]
    for c0 in range(3):
        shifted = pad_ref[:, :, c0 : c0 + 8, :]
        offset_col = 2 - c0 if flipped else c0
        for offset_time in range(3):
            for offset_row in range(3):
                t0 = 2 - offset_time if flipped else offset_time
                r0 = 2 - offset_row if flipped else offset_row
                window = shifted[t0 : t0 + frames, r0 : r0 + 8].reshape(frames * 64, channels)
                yield offset_time * 9 + offset_row * 3 + offset_col, window.astype(jnp.bfloat16)


def greet_line(here, count, col, settle=True):
    barrier = pltpu.get_barrier_semaphore()

    @pl.when(here > 0)
    def _():
        pl.semaphore_signal(barrier, inc=1, device_id=(here - 1, col), device_id_type=MESH_ID)

    @pl.when(here < count - 1)
    def _():
        pl.semaphore_signal(barrier, inc=1, device_id=(here + 1, col), device_id_type=MESH_ID)

    neighbours = (here + count - 1) // count + (2 * count - 2 - here) // count
    if settle:
        pl.semaphore_wait(barrier, neighbours)
    return neighbours


def line_copy(src, dst, send_sem, recv_sem, target, col):
    return pltpu.make_async_remote_copy(
        src_ref=src,
        dst_ref=dst,
        send_sem=send_sem,
        recv_sem=recv_sem,
        device_id=(target, col),
        device_id_type=MESH_ID,
    )


def forward_kernel(clips_ref, shard_ref, seen_ref, out_ref, flat_ref, recv, pad, blocks, gather_send, gather_recv,
                   send_sem, recv_sem):
    count = lax.axis_size("section")
    here = lax.axis_index("section")
    col = lax.axis_index("dp")
    micro_count = clips_ref.shape[0]
    greet_group(col, here, greet_line(here, count, col, settle=False))
    pad[...] = jnp.zeros_like(pad)
    gather_blocks(shard_ref, flat_ref, blocks, gather_send, gather_recv)
    channels = flat_ref.shape[-1]

    def step(m, carry):
        @pl.when(here == 0)
        def _():
            seen_ref[m] = clips_ref[m]

        @pl.when(here > 0)
        def _():
            line_copy(out_ref.at[m], recv.at[m], send_sem.at[m], recv_sem.at[m], here - 1, col).wait_recv()
            seen_ref[m] = recv[m]

        base = seen_ref[m].astype(jnp.float32)
        squash_into(pad, base)
        total = base
        for tap, window in tap_windows(pad, 4, False):
            total = total + jnp.dot(
                window, flat_ref[tap * channels : (tap + 1) * channels, :], preferred_element_type=jnp.float32
            )
        out_ref[m] = total.astype(out_ref.dtype)

        @pl.when(here < count - 1)
        def _():
            line_copy(out_ref.at[m], recv.at[m], send_sem.at[m], recv_sem.at[m], here + 1, col).start()

        return carry

    lax.fori_loop(0, micro_count, step, 0)

    @pl.when(here < count - 1)
    def _():
        for m in range(micro_count):
            line_copy(out_ref.at[m], recv.at[m], send_sem.at[m], recv_sem.at[m], here + 1, col).wait_send()


def forward_line(clips_local, shard):
    shape = jax.ShapeDtypeStruct(clips_local.shape, clips_local.dtype)
    micro_count, cells, channels = clips_local.shape
    peers = lax.axis_size("dp")
    rows = shard.shape[0]
    return pl.pallas_call(
        forward_kernel,
        out_shape=(shape, shape, jax.ShapeDtypeStruct((peers * rows, channels), shard.dtype)),
        in_specs=[pl.BlockSpec(memory_space=pltpu.VMEM)] * 2,
        out_specs=(pl.BlockSpec(memory_space=pltpu.VMEM),) * 3,
        scratch_shapes=[
            pltpu.VMEM(clips_local.shape, clips_local.dtype),
            pltpu.VMEM((cells // 64 + 2, 10, 10, channels), jnp.float32),
            pltpu.VMEM((peers, rows, channels), shard.dtype),
            pltpu.SemaphoreType.DMA((peers,)),
            pltpu.SemaphoreType.DMA((peers,)),
            pltpu.SemaphoreType.DMA((micro_count,)),
            pltpu.SemaphoreType.DMA((micro_count,)),
        ],
        compiler_params=pltpu.CompilerParams(collective_id=2, has_side_effects=True),
    )(clips_local, shard)


def backward_kernel(cot_ref, seen_ref, w_ref, share_ref, recv, sendbuf, pad, gpad, wg_ref, parts_ref, held, mine,
                    theirs, send_sem, recv_sem, share_send, share_recv, cross_sem):
    count = lax.axis_size("section")
    here = lax.axis_index("section")
    col = lax.axis_index("dp")
    micro_count = cot_ref.shape[0]
    greet_group(col, here, greet_line(here, count, col, settle=False))
    pad[...] = jnp.zeros_like(pad)
    gpad[...] = jnp.zeros_like(gpad)
    wg_ref[...] = jnp.zeros_like(wg_ref)

    def step(m, carry):
        @pl.when(here == count - 1)
        def _():
            recv[m] = cot_ref[m]

        @pl.when(here < count - 1)
        def _():
            line_copy(sendbuf.at[m], recv.at[m], send_sem.at[m], recv_sem.at[m], here + 1, col).wait_recv()

        upstream = recv[m]
        base = seen_ref[m].astype(jnp.float32)

        @pl.when(here > 0)
        def _():
            up = upstream.astype(jnp.float32)
            gpad[2:6, 1:9, 1:9, :] = up.reshape(4, 8, 8, up.shape[-1])
            spread = jnp.zeros((384, up.shape[-1]), jnp.float32)
            for tap, window in tap_windows(gpad, 6, True):
                spread = spread + lax.dot_general(
                    window, w_ref[tap], (((1,), (1,)), ((), ())),
                    preferred_element_type=jnp.float32,
                )
            field = jnp.concatenate([spread[0:64] + spread[64:128] + spread[128:192], spread[192:384]], axis=0)
            sig = 1.0 / (1.0 + jnp.exp(-base))
            slope = sig * (1.0 + base * (1.0 - sig))
            sendbuf[m] = (up + field * slope).astype(sendbuf.dtype)
            line_copy(sendbuf.at[m], recv.at[m], send_sem.at[m], recv_sem.at[m], here - 1, col).start()

        @pl.when(here == 0)
        def _():
            weight_term(m)

        return carry

    def weight_term(m):
        upstream = recv[m]
        squash_into(pad, seen_ref[m].astype(jnp.float32))
        for tap, window in tap_windows(pad, 4, False):
            wg_ref[tap * 128 : (tap + 1) * 128, :] += lax.dot_general(
                window, upstream, (((0,), (0,)), ((), ())),
                preferred_element_type=jnp.float32,
            )

    def late_term(m, carry):
        weight_term(m)
        return carry

    lax.fori_loop(0, micro_count, step, 0)

    @pl.when(here > 0)
    def _():
        lax.fori_loop(0, micro_count, late_term, 0)

    block_rows = parts_ref.shape[1]
    for block in range(parts_ref.shape[0]):
        parts_ref[block] = wg_ref[block * block_rows : (block + 1) * block_rows, :].astype(parts_ref.dtype)

    @pl.when(here > 0)
    def _():
        for m in range(micro_count):
            line_copy(sendbuf.at[m], recv.at[m], send_sem.at[m], recv_sem.at[m], here - 1, col).wait_send()

    scatter_blocks(parts_ref, share_ref, held, mine, theirs, share_send, share_recv, cross_sem)


def backward_line(cot_local, seen, weight, blocks):
    micro_count, cells, channels = cot_local.shape
    taps = weight.shape[0]
    block_rows = taps * channels // blocks
    return pl.pallas_call(
        backward_kernel,
        out_shape=jax.ShapeDtypeStruct((block_rows, 1, channels), jnp.float32),
        in_specs=[pl.BlockSpec(memory_space=pltpu.VMEM)] * 3,
        out_specs=pl.BlockSpec(memory_space=pltpu.VMEM),
        scratch_shapes=[
            pltpu.VMEM(cot_local.shape, cot_local.dtype),
            pltpu.VMEM(cot_local.shape, cot_local.dtype),
            pltpu.VMEM((cells // 64 + 2, 10, 10, channels), jnp.float32),
            pltpu.VMEM((cells // 64 + 4, 10, 10, channels), jnp.float32),
            pltpu.VMEM((taps * channels, channels), jnp.float32),
            pltpu.VMEM((blocks, block_rows, channels), jnp.bfloat16),
            pltpu.VMEM((blocks // 2, 2, block_rows, channels), jnp.bfloat16),
            pltpu.VMEM((block_rows, channels), jnp.float32),
            pltpu.VMEM((block_rows, channels), jnp.float32),
            pltpu.SemaphoreType.DMA((micro_count,)),
            pltpu.SemaphoreType.DMA((micro_count,)),
            pltpu.SemaphoreType.DMA((blocks // 2, 2)),
            pltpu.SemaphoreType.DMA((blocks // 2, 2)),
            pltpu.SemaphoreType.DMA((2,)),
        ],
        compiler_params=pltpu.CompilerParams(collective_id=3, has_side_effects=True),
    )(cot_local, seen, weight)


def per_device(clips, cotangent, weights):
    channels = weights.shape[-1]
    blocks = lax.axis_size("dp")
    micro_count = clips.shape[0]
    clips_local = clips[:, 0].reshape(micro_count, -1, channels)
    cot_local = cotangent[:, 0].reshape(micro_count, -1, channels)
    seen, produced, weight = forward_line(clips_local, weights[0])
    weight = weight.reshape(-1, channels, channels)
    grad_share = backward_line(cot_local, seen, weight, blocks)
    return (produced.reshape(clips[:, 0].shape)[None, :, None], grad_share.reshape((1,) + grad_share.shape[::2]))


def solution(mesh):
    placed = (
        P(None, "dp", None, None, None, None),
        P(None, "dp", None, None, None, None),
        P("section", "dp", None),
    )
    return jax.shard_map(
        per_device,
        mesh=mesh,
        in_specs=placed,
        out_specs=(P("section", None, "dp", None, None, None, None), P("section", "dp", None)),
        check_vma=False,
    )
```

```python
import jax
import jax.numpy as jnp
from jax import lax
from jax.sharding import PartitionSpec as P

from jax.experimental import pallas as pl
from jax.experimental.pallas import tpu as pltpu

MESH_ID = pl.DeviceIdType.MESH


def greet_group(here, row, extra=0):
    pair = here - here % 2
    partner = pair + 1 - here % 2
    barrier = pltpu.get_barrier_semaphore()
    pl.semaphore_signal(barrier, inc=1, device_id=(row, partner), device_id_type=MESH_ID)

    def signal(i, carry):
        peer = lax.rem(here + 2 * i, lax.axis_size("dp"))
        pl.semaphore_signal(barrier, inc=1, device_id=(row, peer), device_id_type=MESH_ID)
        return carry

    planes = lax.axis_size("dp") // 2
    lax.fori_loop(1, planes, signal, 0)
    pl.semaphore_wait(barrier, planes + extra)
    return partner


def group_copy(src, dst, send_sem, recv_sem, row, peer):
    return pltpu.make_async_remote_copy(
        src_ref=src,
        dst_ref=dst,
        send_sem=send_sem,
        recv_sem=recv_sem,
        device_id=(row, peer),
        device_id_type=MESH_ID,
    )


def gather_kernel(shard_ref, flat_ref, out_ref, send_sem, recv_sem):
    greet_group(lax.axis_index("dp"), lax.axis_index("section"))
    gather_blocks(shard_ref, flat_ref, out_ref, send_sem, recv_sem)


def gather_blocks(shard_ref, flat_ref, out_ref, send_sem, recv_sem):
    peers = lax.axis_size("dp")
    here = lax.axis_index("dp")
    row = lax.axis_index("section")
    partner = here - here % 2 + 1 - here % 2
    planes = peers // 2
    cross = group_copy(shard_ref, out_ref.at[here], send_sem.at[here], recv_sem.at[here], row, partner)
    cross.start()

    def fan(i, peer):
        own = group_copy(shard_ref, out_ref.at[here], send_sem.at[peer], recv_sem.at[here], row, peer)
        relayed = group_copy(out_ref.at[partner], out_ref.at[partner], send_sem.at[peer + 1 - 2 * (peer % 2)],
                             recv_sem.at[partner], row, peer)
        return own, relayed

    def start_own(i, carry):
        fan(i, lax.rem(here + 2 * i, peers))[0].start()
        return carry

    def start_relay(i, carry):
        fan(i, lax.rem(here + 2 * i, peers))[1].start()
        return carry

    lax.fori_loop(1, planes, start_own, 0)
    out_ref[here] = shard_ref[...]
    cross.wait_send()
    group_copy(shard_ref, out_ref.at[partner], send_sem.at[partner], recv_sem.at[partner], row, partner).wait_recv()
    lax.fori_loop(1, planes, start_relay, 0)

    def finish(i, carry):
        peer = lax.rem(here + 2 * i, peers)
        own, relayed = fan(i, peer)
        own.wait_send()
        relayed.wait_send()
        mate = peer + 1 - 2 * (peer % 2)
        group_copy(shard_ref, out_ref.at[peer], send_sem.at[peer], recv_sem.at[peer], row, peer).wait_recv()
        group_copy(shard_ref, out_ref.at[mate], send_sem.at[mate], recv_sem.at[mate], row, peer).wait_recv()
        return carry

    lax.fori_loop(1, planes, finish, 0)
    rows = shard_ref.shape[0]
    for block in range(peers):
        flat_ref[block * rows : (block + 1) * rows, :] = out_ref[block]


def gather_rows(shard):
    peers = lax.axis_size("dp")
    rows, cols = shard.shape
    return pl.pallas_call(
        gather_kernel,
        out_shape=jax.ShapeDtypeStruct((peers * rows, cols), shard.dtype),
        in_specs=[pl.BlockSpec(memory_space=pltpu.VMEM)],
        out_specs=pl.BlockSpec(memory_space=pltpu.VMEM),
        scratch_shapes=[
            pltpu.VMEM((peers, rows, cols), shard.dtype),
            pltpu.SemaphoreType.DMA((peers,)),
            pltpu.SemaphoreType.DMA((peers,)),
        ],
        compiler_params=pltpu.CompilerParams(collective_id=0, has_side_effects=True),
    )(shard)


def scatter_kernel(parts_ref, out_ref, held, mine, theirs, send_sem, recv_sem, cross_sem):
    greet_group(lax.axis_index("dp"), lax.axis_index("section"))
    scatter_blocks(parts_ref, out_ref, held, mine, theirs, send_sem, recv_sem, cross_sem)


def scatter_blocks(parts_ref, out_ref, held, mine, theirs, send_sem, recv_sem, cross_sem):
    peers = lax.axis_size("dp")
    here = lax.axis_index("dp")
    row = lax.axis_index("section")
    partner = here - here % 2 + 1 - here % 2
    planes = peers // 2
    slot = here // 2
    side = here % 2

    def fan(peer, block):
        return group_copy(parts_ref.at[2 * (peer // 2) + block], held.at[slot, block],
                          send_sem.at[peer // 2, block], recv_sem.at[slot, block], row, peer)

    far = 1 - side

    def start_far(i, carry):
        fan(lax.rem(here + 2 * i, peers), far).start()
        return carry

    def start_near(i, carry):
        fan(lax.rem(here + 2 * i, peers), side).start()
        return carry

    lax.fori_loop(1, planes, start_far, 0)
    lax.fori_loop(1, planes, start_near, 0)

    def gather_block(block):
        def finish(i, total):
            peer = lax.rem(here + 2 * i, peers)
            fan(peer, block).wait_send()
            source = peer // 2
            group_copy(parts_ref.at[block], held.at[source, block], send_sem.at[source, block],
                       recv_sem.at[source, block], row, peer).wait_recv()
            return total + held[source, block].astype(jnp.float32)

        return lax.fori_loop(1, planes, finish, parts_ref[2 * slot + block].astype(jnp.float32))

    theirs[...] = gather_block(far)
    cross = group_copy(theirs, mine, cross_sem.at[0], cross_sem.at[1], row, partner)
    cross.start()
    own = gather_block(side)
    cross.wait_send()
    cross.wait_recv()
    out_ref[...] = (own + mine[...]).reshape(out_ref.shape)


def scatter_rows(parts):
    peers, rows, cols = parts.shape
    return pl.pallas_call(
        scatter_kernel,
        out_shape=jax.ShapeDtypeStruct((rows, cols), jnp.float32),
        in_specs=[pl.BlockSpec(memory_space=pltpu.VMEM)],
        out_specs=pl.BlockSpec(memory_space=pltpu.VMEM),
        scratch_shapes=[
            pltpu.VMEM((peers // 2, 2, rows, cols), parts.dtype),
            pltpu.VMEM((rows, cols), jnp.float32),
            pltpu.VMEM((rows, cols), jnp.float32),
            pltpu.SemaphoreType.DMA((peers // 2, 2)),
            pltpu.SemaphoreType.DMA((peers // 2, 2)),
            pltpu.SemaphoreType.DMA((2,)),
        ],
        compiler_params=pltpu.CompilerParams(collective_id=1, has_side_effects=True),
    )(parts)


def squash_into(pad_ref, activation):
    squashed = (activation / (1.0 + jnp.exp(-activation))).astype(jnp.bfloat16).astype(jnp.float32)
    field = squashed.reshape(pad_ref.shape[0] - 2, 8, 8, pad_ref.shape[-1])
    pad_ref[2:, 1:9, 1:9, :] = field
    pad_ref[0:2, 1:9, 1:9, :] = jnp.broadcast_to(field[0:1], (2,) + field.shape[1:])


def tap_windows(pad_ref, frames, flipped):
    channels = pad_ref.shape[-1]
    for c0 in range(3):
        shifted = pad_ref[:, :, c0 : c0 + 8, :]
        offset_col = 2 - c0 if flipped else c0
        for offset_time in range(3):
            for offset_row in range(3):
                t0 = 2 - offset_time if flipped else offset_time
                r0 = 2 - offset_row if flipped else offset_row
                window = shifted[t0 : t0 + frames, r0 : r0 + 8].reshape(frames * 64, channels)
                yield offset_time * 9 + offset_row * 3 + offset_col, window.astype(jnp.bfloat16)


def greet_line(here, count, col, settle=True):
    barrier = pltpu.get_barrier_semaphore()

    @pl.when(here > 0)
    def _():
        pl.semaphore_signal(barrier, inc=1, device_id=(here - 1, col), device_id_type=MESH_ID)

    @pl.when(here < count - 1)
    def _():
        pl.semaphore_signal(barrier, inc=1, device_id=(here + 1, col), device_id_type=MESH_ID)

    neighbours = (here + count - 1) // count + (2 * count - 2 - here) // count
    if settle:
        pl.semaphore_wait(barrier, neighbours)
    return neighbours


def line_copy(src, dst, send_sem, recv_sem, target, col):
    return pltpu.make_async_remote_copy(
        src_ref=src,
        dst_ref=dst,
        send_sem=send_sem,
        recv_sem=recv_sem,
        device_id=(target, col),
        device_id_type=MESH_ID,
    )


def forward_kernel(clips_ref, shard_ref, seen_ref, out_ref, flat_ref, recv, pad, blocks, gather_send, gather_recv,
                   send_sem, recv_sem):
    count = lax.axis_size("section")
    here = lax.axis_index("section")
    col = lax.axis_index("dp")
    micro_count = clips_ref.shape[0]
    greet_group(col, here, greet_line(here, count, col, settle=False))
    pad[...] = jnp.zeros_like(pad)
    gather_blocks(shard_ref, flat_ref, blocks, gather_send, gather_recv)
    channels = flat_ref.shape[-1]

    def step(m, carry):
        @pl.when(here == 0)
        def _():
            seen_ref[m] = clips_ref[m]

        @pl.when(here > 0)
        def _():
            line_copy(out_ref.at[m], recv.at[m], send_sem.at[m], recv_sem.at[m], here - 1, col).wait_recv()
            seen_ref[m] = recv[m]

        base = seen_ref[m].astype(jnp.float32)
        squash_into(pad, base)
        total = base
        for tap, window in tap_windows(pad, 4, False):
            total = total + jnp.dot(
                window, flat_ref[tap * channels : (tap + 1) * channels, :], preferred_element_type=jnp.float32
            )
        out_ref[m] = total.astype(out_ref.dtype)

        @pl.when(here < count - 1)
        def _():
            line_copy(out_ref.at[m], recv.at[m], send_sem.at[m], recv_sem.at[m], here + 1, col).start()

        return carry

    lax.fori_loop(0, micro_count, step, 0)

    @pl.when(here < count - 1)
    def _():
        for m in range(micro_count):
            line_copy(out_ref.at[m], recv.at[m], send_sem.at[m], recv_sem.at[m], here + 1, col).wait_send()


def forward_line(clips_local, shard):
    shape = jax.ShapeDtypeStruct(clips_local.shape, clips_local.dtype)
    micro_count, cells, channels = clips_local.shape
    peers = lax.axis_size("dp")
    rows = shard.shape[0]
    return pl.pallas_call(
        forward_kernel,
        out_shape=(shape, shape, jax.ShapeDtypeStruct((peers * rows, channels), shard.dtype)),
        in_specs=[pl.BlockSpec(memory_space=pltpu.VMEM)] * 2,
        out_specs=(pl.BlockSpec(memory_space=pltpu.VMEM),) * 3,
        scratch_shapes=[
            pltpu.VMEM(clips_local.shape, clips_local.dtype),
            pltpu.VMEM((cells // 64 + 2, 10, 10, channels), jnp.float32),
            pltpu.VMEM((peers, rows, channels), shard.dtype),
            pltpu.SemaphoreType.DMA((peers,)),
            pltpu.SemaphoreType.DMA((peers,)),
            pltpu.SemaphoreType.DMA((micro_count,)),
            pltpu.SemaphoreType.DMA((micro_count,)),
        ],
        compiler_params=pltpu.CompilerParams(collective_id=2, has_side_effects=True),
    )(clips_local, shard)


def backward_kernel(cot_ref, seen_ref, w_ref, share_ref, recv, sendbuf, pad, gpad, wg_ref, wg_t, parts_ref, held, mine,
                    theirs, send_sem, recv_sem, share_send, share_recv, cross_sem):
    count = lax.axis_size("section")
    here = lax.axis_index("section")
    col = lax.axis_index("dp")
    micro_count = cot_ref.shape[0]
    greet_group(col, here, greet_line(here, count, col, settle=False))
    pad[...] = jnp.zeros_like(pad)
    gpad[...] = jnp.zeros_like(gpad)
    wg_t[...] = jnp.zeros_like(wg_t)

    def step(m, carry):
        @pl.when(here == count - 1)
        def _():
            recv[m] = cot_ref[m]

        @pl.when(here < count - 1)
        def _():
            line_copy(sendbuf.at[m], recv.at[m], send_sem.at[m], recv_sem.at[m], here + 1, col).wait_recv()

        upstream = recv[m]
        base = seen_ref[m].astype(jnp.float32)

        @pl.when(here > 0)
        def _():
            up = upstream.astype(jnp.float32)
            gpad[2:6, 1:9, 1:9, :] = up.reshape(4, 8, 8, up.shape[-1])
            spread = jnp.zeros((384, up.shape[-1]), jnp.float32)
            for tap, window in tap_windows(gpad, 6, True):
                spread = spread + lax.dot_general(
                    window, w_ref[tap], (((1,), (1,)), ((), ())),
                    preferred_element_type=jnp.float32,
                )
            field = jnp.concatenate([spread[0:64] + spread[64:128] + spread[128:192], spread[192:384]], axis=0)
            sig = 1.0 / (1.0 + jnp.exp(-base))
            slope = sig * (1.0 + base * (1.0 - sig))
            sendbuf[m] = (up + field * slope).astype(sendbuf.dtype)
            line_copy(sendbuf.at[m], recv.at[m], send_sem.at[m], recv_sem.at[m], here - 1, col).start()

        @pl.when(here == 0)
        def _():
            weight_term(m)

        return carry

    def weight_term(m):
        upstream_t = recv[m].T
        squash_into(pad, seen_ref[m].astype(jnp.float32))
        for tap, window in tap_windows(pad, 4, False):
            wg_t[:, tap * 128 : (tap + 1) * 128] += jnp.dot(upstream_t, window, preferred_element_type=jnp.float32)

    def late_term(m, carry):
        weight_term(m)
        return carry

    lax.fori_loop(0, micro_count, step, 0)

    @pl.when(here > 0)
    def _():
        lax.fori_loop(0, micro_count, late_term, 0)

    for tap in range(wg_ref.shape[0] // 128):
        wg_ref[tap * 128 : (tap + 1) * 128, :] = wg_t[:, tap * 128 : (tap + 1) * 128].T
    block_rows = parts_ref.shape[1]
    for block in range(parts_ref.shape[0]):
        parts_ref[block] = wg_ref[block * block_rows : (block + 1) * block_rows, :].astype(parts_ref.dtype)

    @pl.when(here > 0)
    def _():
        for m in range(micro_count):
            line_copy(sendbuf.at[m], recv.at[m], send_sem.at[m], recv_sem.at[m], here - 1, col).wait_send()

    scatter_blocks(parts_ref, share_ref, held, mine, theirs, share_send, share_recv, cross_sem)


def backward_line(cot_local, seen, weight, blocks):
    micro_count, cells, channels = cot_local.shape
    taps = weight.shape[0]
    block_rows = taps * channels // blocks
    return pl.pallas_call(
        backward_kernel,
        out_shape=jax.ShapeDtypeStruct((block_rows, 1, channels), jnp.float32),
        in_specs=[pl.BlockSpec(memory_space=pltpu.VMEM)] * 3,
        out_specs=pl.BlockSpec(memory_space=pltpu.VMEM),
        scratch_shapes=[
            pltpu.VMEM(cot_local.shape, cot_local.dtype),
            pltpu.VMEM(cot_local.shape, cot_local.dtype),
            pltpu.VMEM((cells // 64 + 2, 10, 10, channels), jnp.float32),
            pltpu.VMEM((cells // 64 + 4, 10, 10, channels), jnp.float32),
            pltpu.VMEM((taps * channels, channels), jnp.float32),
            pltpu.VMEM((channels, taps * channels), jnp.float32),
            pltpu.VMEM((blocks, block_rows, channels), jnp.bfloat16),
            pltpu.VMEM((blocks // 2, 2, block_rows, channels), jnp.bfloat16),
            pltpu.VMEM((block_rows, channels), jnp.float32),
            pltpu.VMEM((block_rows, channels), jnp.float32),
            pltpu.SemaphoreType.DMA((micro_count,)),
            pltpu.SemaphoreType.DMA((micro_count,)),
            pltpu.SemaphoreType.DMA((blocks // 2, 2)),
            pltpu.SemaphoreType.DMA((blocks // 2, 2)),
            pltpu.SemaphoreType.DMA((2,)),
        ],
        compiler_params=pltpu.CompilerParams(collective_id=3, has_side_effects=True),
    )(cot_local, seen, weight)


def per_device(clips, cotangent, weights):
    channels = weights.shape[-1]
    blocks = lax.axis_size("dp")
    micro_count = clips.shape[0]
    clips_local = clips[:, 0].reshape(micro_count, -1, channels)
    cot_local = cotangent[:, 0].reshape(micro_count, -1, channels)
    seen, produced, weight = forward_line(clips_local, weights[0])
    weight = weight.reshape(-1, channels, channels)
    grad_share = backward_line(cot_local, seen, weight, blocks)
    return (produced.reshape(clips[:, 0].shape)[None, :, None], grad_share.reshape((1,) + grad_share.shape[::2]))


def solution(mesh):
    placed = (
        P(None, "dp", None, None, None, None),
        P(None, "dp", None, None, None, None),
        P("section", "dp", None),
    )
    return jax.shard_map(
        per_device,
        mesh=mesh,
        in_specs=placed,
        out_specs=(P("section", None, "dp", None, None, None, None), P("section", "dp", None)),
        check_vma=False,
    )
```

```python
import jax
import jax.numpy as jnp
from jax import lax
from jax.sharding import PartitionSpec as P

from jax.experimental import pallas as pl
from jax.experimental.pallas import tpu as pltpu

MESH_ID = pl.DeviceIdType.MESH


def greet_group(here, row, extra=0):
    pair = here - here % 2
    partner = pair + 1 - here % 2
    barrier = pltpu.get_barrier_semaphore()
    pl.semaphore_signal(barrier, inc=1, device_id=(row, partner), device_id_type=MESH_ID)

    def signal(i, carry):
        peer = lax.rem(here + 2 * i, lax.axis_size("dp"))
        pl.semaphore_signal(barrier, inc=1, device_id=(row, peer), device_id_type=MESH_ID)
        return carry

    planes = lax.axis_size("dp") // 2
    lax.fori_loop(1, planes, signal, 0)
    pl.semaphore_wait(barrier, planes + extra)
    return partner


def group_copy(src, dst, send_sem, recv_sem, row, peer):
    return pltpu.make_async_remote_copy(
        src_ref=src,
        dst_ref=dst,
        send_sem=send_sem,
        recv_sem=recv_sem,
        device_id=(row, peer),
        device_id_type=MESH_ID,
    )


def gather_kernel(shard_ref, flat_ref, out_ref, send_sem, recv_sem):
    greet_group(lax.axis_index("dp"), lax.axis_index("section"))
    gather_blocks(shard_ref, flat_ref, out_ref, send_sem, recv_sem)


def gather_blocks(shard_ref, flat_ref, out_ref, send_sem, recv_sem):
    peers = lax.axis_size("dp")
    here = lax.axis_index("dp")
    row = lax.axis_index("section")
    partner = here - here % 2 + 1 - here % 2
    planes = peers // 2
    cross = group_copy(shard_ref, out_ref.at[here], send_sem.at[here], recv_sem.at[here], row, partner)
    cross.start()

    def fan(i, peer):
        own = group_copy(shard_ref, out_ref.at[here], send_sem.at[peer], recv_sem.at[here], row, peer)
        relayed = group_copy(out_ref.at[partner], out_ref.at[partner], send_sem.at[peer + 1 - 2 * (peer % 2)],
                             recv_sem.at[partner], row, peer)
        return own, relayed

    def start_own(i, carry):
        fan(i, lax.rem(here + 2 * i, peers))[0].start()
        return carry

    def start_relay(i, carry):
        fan(i, lax.rem(here + 2 * i, peers))[1].start()
        return carry

    lax.fori_loop(1, planes, start_own, 0)
    out_ref[here] = shard_ref[...]
    cross.wait_send()
    group_copy(shard_ref, out_ref.at[partner], send_sem.at[partner], recv_sem.at[partner], row, partner).wait_recv()
    lax.fori_loop(1, planes, start_relay, 0)

    def finish(i, carry):
        peer = lax.rem(here + 2 * i, peers)
        own, relayed = fan(i, peer)
        own.wait_send()
        relayed.wait_send()
        mate = peer + 1 - 2 * (peer % 2)
        group_copy(shard_ref, out_ref.at[peer], send_sem.at[peer], recv_sem.at[peer], row, peer).wait_recv()
        group_copy(shard_ref, out_ref.at[mate], send_sem.at[mate], recv_sem.at[mate], row, peer).wait_recv()
        return carry

    lax.fori_loop(1, planes, finish, 0)
    rows = shard_ref.shape[0]
    for block in range(peers):
        flat_ref[block * rows : (block + 1) * rows, :] = out_ref[block]


def gather_rows(shard):
    peers = lax.axis_size("dp")
    rows, cols = shard.shape
    return pl.pallas_call(
        gather_kernel,
        out_shape=jax.ShapeDtypeStruct((peers * rows, cols), shard.dtype),
        in_specs=[pl.BlockSpec(memory_space=pltpu.VMEM)],
        out_specs=pl.BlockSpec(memory_space=pltpu.VMEM),
        scratch_shapes=[
            pltpu.VMEM((peers, rows, cols), shard.dtype),
            pltpu.SemaphoreType.DMA((peers,)),
            pltpu.SemaphoreType.DMA((peers,)),
        ],
        compiler_params=pltpu.CompilerParams(collective_id=0, has_side_effects=True),
    )(shard)


def scatter_kernel(parts_ref, out_ref, held, mine, theirs, send_sem, recv_sem, cross_sem):
    greet_group(lax.axis_index("dp"), lax.axis_index("section"))
    scatter_blocks(parts_ref, out_ref, held, mine, theirs, send_sem, recv_sem, cross_sem)


def scatter_blocks(parts_ref, out_ref, held, mine, theirs, send_sem, recv_sem, cross_sem):
    peers = lax.axis_size("dp")
    here = lax.axis_index("dp")
    row = lax.axis_index("section")
    partner = here - here % 2 + 1 - here % 2
    planes = peers // 2
    slot = here // 2
    side = here % 2

    def fan(peer, block):
        return group_copy(parts_ref.at[2 * (peer // 2) + block], held.at[slot, block],
                          send_sem.at[peer // 2, block], recv_sem.at[slot, block], row, peer)

    far = 1 - side

    def start_far(i, carry):
        fan(lax.rem(here + 2 * i, peers), far).start()
        return carry

    def start_near(i, carry):
        fan(lax.rem(here + 2 * i, peers), side).start()
        return carry

    lax.fori_loop(1, planes, start_far, 0)
    lax.fori_loop(1, planes, start_near, 0)

    def gather_block(block):
        def finish(i, total):
            peer = lax.rem(here + 2 * i, peers)
            fan(peer, block).wait_send()
            source = peer // 2
            group_copy(parts_ref.at[block], held.at[source, block], send_sem.at[source, block],
                       recv_sem.at[source, block], row, peer).wait_recv()
            return total + held[source, block].astype(jnp.float32)

        return lax.fori_loop(1, planes, finish, parts_ref[2 * slot + block].astype(jnp.float32))

    theirs[...] = gather_block(far).astype(theirs.dtype)
    cross = group_copy(theirs, mine, cross_sem.at[0], cross_sem.at[1], row, partner)
    cross.start()
    own = gather_block(side)
    cross.wait_send()
    cross.wait_recv()
    out_ref[...] = (own + mine[...].astype(jnp.float32)).reshape(out_ref.shape)


def scatter_rows(parts):
    peers, rows, cols = parts.shape
    return pl.pallas_call(
        scatter_kernel,
        out_shape=jax.ShapeDtypeStruct((rows, cols), jnp.float32),
        in_specs=[pl.BlockSpec(memory_space=pltpu.VMEM)],
        out_specs=pl.BlockSpec(memory_space=pltpu.VMEM),
        scratch_shapes=[
            pltpu.VMEM((peers // 2, 2, rows, cols), parts.dtype),
            pltpu.VMEM((rows, cols), jnp.float32),
            pltpu.VMEM((rows, cols), jnp.float32),
            pltpu.SemaphoreType.DMA((peers // 2, 2)),
            pltpu.SemaphoreType.DMA((peers // 2, 2)),
            pltpu.SemaphoreType.DMA((2,)),
        ],
        compiler_params=pltpu.CompilerParams(collective_id=1, has_side_effects=True),
    )(parts)


def squash_into(pad_ref, activation):
    squashed = (activation / (1.0 + jnp.exp(-activation))).astype(jnp.bfloat16).astype(jnp.float32)
    field = squashed.reshape(pad_ref.shape[0] - 2, 8, 8, pad_ref.shape[-1])
    pad_ref[2:, 1:9, 1:9, :] = field
    pad_ref[0:2, 1:9, 1:9, :] = jnp.broadcast_to(field[0:1], (2,) + field.shape[1:])


def tap_windows(pad_ref, frames, flipped):
    channels = pad_ref.shape[-1]
    for c0 in range(3):
        shifted = pad_ref[:, :, c0 : c0 + 8, :]
        offset_col = 2 - c0 if flipped else c0
        for offset_time in range(3):
            for offset_row in range(3):
                t0 = 2 - offset_time if flipped else offset_time
                r0 = 2 - offset_row if flipped else offset_row
                window = shifted[t0 : t0 + frames, r0 : r0 + 8].reshape(frames * 64, channels)
                yield offset_time * 9 + offset_row * 3 + offset_col, window.astype(jnp.bfloat16)


def greet_line(here, count, col, settle=True):
    barrier = pltpu.get_barrier_semaphore()

    @pl.when(here > 0)
    def _():
        pl.semaphore_signal(barrier, inc=1, device_id=(here - 1, col), device_id_type=MESH_ID)

    @pl.when(here < count - 1)
    def _():
        pl.semaphore_signal(barrier, inc=1, device_id=(here + 1, col), device_id_type=MESH_ID)

    neighbours = (here + count - 1) // count + (2 * count - 2 - here) // count
    if settle:
        pl.semaphore_wait(barrier, neighbours)
    return neighbours


def line_copy(src, dst, send_sem, recv_sem, target, col):
    return pltpu.make_async_remote_copy(
        src_ref=src,
        dst_ref=dst,
        send_sem=send_sem,
        recv_sem=recv_sem,
        device_id=(target, col),
        device_id_type=MESH_ID,
    )


def forward_kernel(clips_ref, shard_ref, seen_ref, out_ref, flat_ref, recv, pad, blocks, gather_send, gather_recv,
                   send_sem, recv_sem):
    count = lax.axis_size("section")
    here = lax.axis_index("section")
    col = lax.axis_index("dp")
    micro_count = clips_ref.shape[0]
    greet_group(col, here, greet_line(here, count, col, settle=False))
    pad[...] = jnp.zeros_like(pad)
    gather_blocks(shard_ref, flat_ref, blocks, gather_send, gather_recv)
    channels = flat_ref.shape[-1]

    def step(m, carry):
        @pl.when(here == 0)
        def _():
            seen_ref[m] = clips_ref[m]

        @pl.when(here > 0)
        def _():
            line_copy(out_ref.at[m], recv.at[m], send_sem.at[m], recv_sem.at[m], here - 1, col).wait_recv()
            seen_ref[m] = recv[m]

        base = seen_ref[m].astype(jnp.float32)
        squash_into(pad, base)
        total = base
        for tap, window in tap_windows(pad, 4, False):
            total = total + jnp.dot(
                window, flat_ref[tap * channels : (tap + 1) * channels, :], preferred_element_type=jnp.float32
            )
        out_ref[m] = total.astype(out_ref.dtype)

        @pl.when(here < count - 1)
        def _():
            line_copy(out_ref.at[m], recv.at[m], send_sem.at[m], recv_sem.at[m], here + 1, col).start()

        return carry

    lax.fori_loop(0, micro_count, step, 0)

    @pl.when(here < count - 1)
    def _():
        for m in range(micro_count):
            line_copy(out_ref.at[m], recv.at[m], send_sem.at[m], recv_sem.at[m], here + 1, col).wait_send()


def forward_line(clips_local, shard):
    shape = jax.ShapeDtypeStruct(clips_local.shape, clips_local.dtype)
    micro_count, cells, channels = clips_local.shape
    peers = lax.axis_size("dp")
    rows = shard.shape[0]
    return pl.pallas_call(
        forward_kernel,
        out_shape=(shape, shape, jax.ShapeDtypeStruct((peers * rows, channels), shard.dtype)),
        in_specs=[pl.BlockSpec(memory_space=pltpu.VMEM)] * 2,
        out_specs=(pl.BlockSpec(memory_space=pltpu.VMEM),) * 3,
        scratch_shapes=[
            pltpu.VMEM(clips_local.shape, clips_local.dtype),
            pltpu.VMEM((cells // 64 + 2, 10, 10, channels), jnp.float32),
            pltpu.VMEM((peers, rows, channels), shard.dtype),
            pltpu.SemaphoreType.DMA((peers,)),
            pltpu.SemaphoreType.DMA((peers,)),
            pltpu.SemaphoreType.DMA((micro_count,)),
            pltpu.SemaphoreType.DMA((micro_count,)),
        ],
        compiler_params=pltpu.CompilerParams(collective_id=2, has_side_effects=True),
    )(clips_local, shard)


def backward_kernel(cot_ref, seen_ref, w_ref, share_ref, recv, sendbuf, pad, gpad, wg_ref, parts_ref, held, mine,
                    theirs, send_sem, recv_sem, share_send, share_recv, cross_sem):
    count = lax.axis_size("section")
    here = lax.axis_index("section")
    col = lax.axis_index("dp")
    micro_count = cot_ref.shape[0]
    greet_group(col, here, greet_line(here, count, col, settle=False))
    pad[...] = jnp.zeros_like(pad)
    gpad[...] = jnp.zeros_like(gpad)
    wg_ref[...] = jnp.zeros_like(wg_ref)

    def step(m, carry):
        @pl.when(here == count - 1)
        def _():
            recv[m] = cot_ref[m]

        @pl.when(here < count - 1)
        def _():
            line_copy(sendbuf.at[m], recv.at[m], send_sem.at[m], recv_sem.at[m], here + 1, col).wait_recv()

        upstream = recv[m]
        base = seen_ref[m].astype(jnp.float32)

        @pl.when(here > 0)
        def _():
            up = upstream.astype(jnp.float32)
            gpad[2:6, 1:9, 1:9, :] = up.reshape(4, 8, 8, up.shape[-1])
            spread = jnp.zeros((384, up.shape[-1]), jnp.float32)
            for tap, window in tap_windows(gpad, 6, True):
                spread = spread + lax.dot_general(
                    window, w_ref[tap], (((1,), (1,)), ((), ())),
                    preferred_element_type=jnp.float32,
                )
            field = jnp.concatenate([spread[0:64] + spread[64:128] + spread[128:192], spread[192:384]], axis=0)
            sig = 1.0 / (1.0 + jnp.exp(-base))
            slope = sig * (1.0 + base * (1.0 - sig))
            sendbuf[m] = (up + field * slope).astype(sendbuf.dtype)
            line_copy(sendbuf.at[m], recv.at[m], send_sem.at[m], recv_sem.at[m], here - 1, col).start()

        @pl.when(here == 0)
        def _():
            weight_term(m)

        return carry

    def weight_term(m):
        upstream = recv[m]
        squash_into(pad, seen_ref[m].astype(jnp.float32))
        for tap, window in tap_windows(pad, 4, False):
            wg_ref[tap * 128 : (tap + 1) * 128, :] += lax.dot_general(
                window, upstream, (((0,), (0,)), ((), ())),
                preferred_element_type=jnp.float32,
            )

    def late_term(m, carry):
        weight_term(m)
        return carry

    lax.fori_loop(0, micro_count, step, 0)

    @pl.when(here > 0)
    def _():
        lax.fori_loop(0, micro_count, late_term, 0)

    block_rows = parts_ref.shape[1]
    for block in range(parts_ref.shape[0]):
        parts_ref[block] = wg_ref[block * block_rows : (block + 1) * block_rows, :].astype(parts_ref.dtype)

    @pl.when(here > 0)
    def _():
        for m in range(micro_count):
            line_copy(sendbuf.at[m], recv.at[m], send_sem.at[m], recv_sem.at[m], here - 1, col).wait_send()

    scatter_blocks(parts_ref, share_ref, held, mine, theirs, share_send, share_recv, cross_sem)


def backward_line(cot_local, seen, weight, blocks):
    micro_count, cells, channels = cot_local.shape
    taps = weight.shape[0]
    block_rows = taps * channels // blocks
    return pl.pallas_call(
        backward_kernel,
        out_shape=jax.ShapeDtypeStruct((block_rows, 1, channels), jnp.float32),
        in_specs=[pl.BlockSpec(memory_space=pltpu.VMEM)] * 3,
        out_specs=pl.BlockSpec(memory_space=pltpu.VMEM),
        scratch_shapes=[
            pltpu.VMEM(cot_local.shape, cot_local.dtype),
            pltpu.VMEM(cot_local.shape, cot_local.dtype),
            pltpu.VMEM((cells // 64 + 2, 10, 10, channels), jnp.float32),
            pltpu.VMEM((cells // 64 + 4, 10, 10, channels), jnp.float32),
            pltpu.VMEM((taps * channels, channels), jnp.float32),
            pltpu.VMEM((blocks, block_rows, channels), jnp.bfloat16),
            pltpu.VMEM((blocks // 2, 2, block_rows, channels), jnp.bfloat16),
            pltpu.VMEM((block_rows, channels), jnp.bfloat16),
            pltpu.VMEM((block_rows, channels), jnp.bfloat16),
            pltpu.SemaphoreType.DMA((micro_count,)),
            pltpu.SemaphoreType.DMA((micro_count,)),
            pltpu.SemaphoreType.DMA((blocks // 2, 2)),
            pltpu.SemaphoreType.DMA((blocks // 2, 2)),
            pltpu.SemaphoreType.DMA((2,)),
        ],
        compiler_params=pltpu.CompilerParams(collective_id=3, has_side_effects=True),
    )(cot_local, seen, weight)


def per_device(clips, cotangent, weights):
    channels = weights.shape[-1]
    blocks = lax.axis_size("dp")
    micro_count = clips.shape[0]
    clips_local = clips[:, 0].reshape(micro_count, -1, channels)
    cot_local = cotangent[:, 0].reshape(micro_count, -1, channels)
    seen, produced, weight = forward_line(clips_local, weights[0])
    weight = weight.reshape(-1, channels, channels)
    grad_share = backward_line(cot_local, seen, weight, blocks)
    return (produced.reshape(clips[:, 0].shape)[None, :, None], grad_share.reshape((1,) + grad_share.shape[::2]))


def solution(mesh):
    placed = (
        P(None, "dp", None, None, None, None),
        P(None, "dp", None, None, None, None),
        P("section", "dp", None),
    )
    return jax.shard_map(
        per_device,
        mesh=mesh,
        in_specs=placed,
        out_specs=(P("section", None, "dp", None, None, None, None), P("section", "dp", None)),
        check_vma=False,
    )
```
